256 devices in a mesh: tm: 32 (over y_hi, z, core), site: 8 (over y_lo, x).
Axes of the slice: x: 4, y: 4 (y_hi: 2, y_lo: 2; y = y_hi * 2 + y_lo), z: 8, core: 2. Of those that a mesh axis runs over, the one named last changes fastest.
Arguments:
- q_time: bfloat16 [8, 4096, 768], P('site', 'tm'), may hold values from -6 to 6
- k_time: bfloat16 [8, 4096, 768], P('site', 'tm'), may hold values from -6 to 6
- v_time: bfloat16 [8, 4096, 768], P('site', 'tm'), may hold values from -6 to 6
- resid: bfloat16 [8, 4096, 1536], P('site', 'tm'), may hold values from -6 to 6
- w_out_time: bfloat16 [768, 1536], replicated, may hold values from -0.21875 to 0.21875
- norm_gain: float32 [1536], replicated, may hold values from 0.1 to 1.9
- w_qkv_site: bfloat16 [1536, 2304], replicated, may hold values from -0.15625 to 0.15625
- grad_site: bfloat16 [8, 4096, 768], P('site', 'tm'), may hold values from -16 to 16
- nbr_blocks: int32 [8, 2], P('site'), may hold values from 0 to 7, as said below
Outputs:
- site_out: bfloat16 [8, 4096, 768], P('site', 'tm')
- grad_q_time: bfloat16 [8, 4096, 768], P('site', 'tm')
- grad_k_time: bfloat16 [8, 4096, 768], P('site', 'tm')
- grad_v_time: bfloat16 [8, 4096, 768], P('site', 'tm')
- grad_resid: bfloat16 [8, 4096, 1536], P('site', 'tm')
The draws below stay inside these ranges and needn't reach their ends.
Inputs may be any that keep to these rules, and one draw needn't show every extreme that they name: `nbr_blocks`: each of a station's 2 entries names the station's own block or the block just below or just above it, station i lying in block i; in every block the first station names the block above first and the block below second, where these exist, and otherwise the one neighbouring block that exists.
All inputs are finite; a program needn't handle non-finite values.
Results may differ from the reference program's by a relative error of at most 0.017.
Values may be sent and summed in bfloat16 or wider, within the bound.
A program may use at most 64 MiB of HBM per device.

```python
import jax
import jax.numpy as jnp
from jax import lax

MODEL_DIM = 1536
HEADS = 6
HEAD_SIZE = 128
ATT = 768
ST_DEV = 1
RADIUS = 256
LISTED = 2
STATIONS = 8
HOURS = 4096


def draw_nbr_blocks(key, part):
    block_count = STATIONS // ST_DEV
    own_block = jnp.arange(STATIONS, dtype=jnp.int32) // ST_DEV
    offsets = jax.random.randint(key, (STATIONS, LISTED), -1, 2, dtype=jnp.int32)
    candidate = own_block[:, None] + offsets
    candidate_inside = (candidate >= 0) & (candidate < block_count)
    general = jnp.where(candidate_inside, candidate, own_block[:, None] + jnp.zeros_like(offsets))
    column = jnp.arange(LISTED, dtype=jnp.int32)
    forced = 1 - 2 * (column % 2)
    upward = own_block[:, None] + forced[None, :]
    downward = own_block[:, None] - forced[None, :]
    inside = (upward >= 0) & (upward < block_count)
    leader_pick = jnp.where(inside, upward, downward)
    leader = jnp.arange(STATIONS, dtype=jnp.int32) % ST_DEV == 0
    return jnp.where(leader[:, None], leader_pick, general).astype(jnp.int32)


def level_of(stream_key, shape, cuts, least, largest):
    level, own = 1.0, jax.random.fold_in(stream_key, 6)
    for axis_at, parts in cuts:
        steps = jnp.exp(jax.random.uniform(jax.random.fold_in(own, axis_at), (parts,), jnp.float32, least / len(cuts), largest / len(cuts)))
        level = level * jnp.repeat(steps, shape[axis_at] // parts).reshape([-1 if axis == axis_at else 1 for axis in range(len(shape))])
    return level


def scatter_about(rng, extent, width, limit, pieces=(), kind=jnp.bfloat16):
    entries = jax.random.normal(rng, extent, jnp.float32) * width
    if len(pieces) > 0:
        entries = level_of(rng, extent, pieces, -0.22, 0.18) * entries
    return jnp.clip(entries, min=-limit, max=limit).astype(kind)


def setup_inputs(seed: int = 0) -> dict:
    key_list = jax.random.split(jax.random.key(seed), 10)
    return {
        "q_time": scatter_about(key_list[0], (STATIONS, HOURS, ATT), 1.0, 6.0, ((0, 8), (1, 32))),
        "k_time": scatter_about(key_list[1], (STATIONS, HOURS, ATT), 1.0, 6.0, ((0, 8), (1, 32))),
        "v_time": scatter_about(key_list[2], (STATIONS, HOURS, ATT), 1.0, 6.0, ((0, 8), (1, 32))),
        "resid": scatter_about(key_list[3], (STATIONS, HOURS, MODEL_DIM), 1.0, 6.0, ((0, 8), (1, 32))),
        "w_out_time": scatter_about(key_list[4], (ATT, MODEL_DIM), ATT ** -0.5, 0.21875),
        "norm_gain": jnp.clip(1.0 + 0.18 * jax.random.normal(key_list[5], (MODEL_DIM,), jnp.float32), 0.1, 1.9),
        "w_qkv_site": scatter_about(key_list[6], (MODEL_DIM, 3 * ATT), MODEL_DIM ** -0.5, 0.15625),
        "grad_site": scatter_about(key_list[7], (STATIONS, HOURS, ATT), 4.0, 16.0, ((0, 8), (1, 32))),
        "nbr_blocks": draw_nbr_blocks(jax.random.fold_in(key_list[9], 71), 0),
    }


EPSILON = 1e-05

def rounded(values):
    return lax.optimization_barrier(values.astype(jnp.bfloat16))

def split_heads(values):
    return values.reshape(values.shape[:-1] + (HEADS, HEAD_SIZE))

def head_norm(values):
    shaped = split_heads(values)
    inverse = lax.rsqrt(lax.optimization_barrier(jnp.mean(shaped * shaped, axis=-1, keepdims=True)) + EPSILON)
    return (shaped * inverse, inverse)

def norm_back(normed, inverse, grads):
    return inverse * (grads - normed * lax.optimization_barrier(jnp.mean(normed * grads, axis=-1, keepdims=True)))

def reference(q_time, k_time, v_time, resid, w_out_time, norm_gain, w_qkv_site, grad_site, nbr_blocks):
    exact = lax.Precision.HIGHEST
    scale_factor = HEAD_SIZE ** (-0.5)
    att_width = HEADS * HEAD_SIZE
    row_count = STATIONS * HOURS
    positions = jnp.arange(HOURS, dtype=jnp.int32)
    in_band = jnp.abs(positions[:, None] - positions[None, :]) <= RADIUS

    def time_probs(q_row, k_row):
        q_normed, q_inverse = head_norm(q_row.astype(jnp.float32))
        k_normed, k_inverse = head_norm(k_row.astype(jnp.float32))
        scores = jnp.einsum('qhe,khe->hqk', q_normed, k_normed, precision=exact) * scale_factor
        exponent = jnp.where(in_band, jnp.exp(scores), 0.0)
        return (q_normed, q_inverse, k_normed, k_inverse, exponent / lax.optimization_barrier(jnp.sum(exponent, axis=-1, keepdims=True)))

    def time_forward(items):
        q_row, k_row, v_row = items
        probs = time_probs(q_row, k_row)[4]
        weights = rounded(probs).astype(jnp.float32)
        heads_out = jnp.einsum('hqk,khe->qhe', weights, split_heads(v_row.astype(jnp.float32)), precision=exact)
        return heads_out.reshape(HOURS, att_width).astype(jnp.bfloat16)
    out_time = lax.map(time_forward, (q_time, k_time, v_time))
    residual_sum = resid.reshape(row_count, MODEL_DIM).astype(jnp.float32) + jnp.dot(out_time.reshape(row_count, att_width), w_out_time, preferred_element_type=jnp.float32)
    inv_rms = lax.rsqrt(lax.optimization_barrier(jnp.mean(residual_sum * residual_sum, axis=1, keepdims=True)) + EPSILON)
    normed = (residual_sum * inv_rms * norm_gain).astype(jnp.bfloat16)
    projected = jnp.dot(normed, w_qkv_site, preferred_element_type=jnp.float32).reshape(STATIONS, HOURS, 3 * att_width)
    q_site = projected[..., :att_width]
    k_site = rounded(projected[..., att_width:2 * att_width])
    v_site = rounded(projected[..., 2 * att_width:])
    block_of = jnp.arange(STATIONS, dtype=jnp.int32) // ST_DEV
    allowed = (block_of[None, :] == block_of[:, None]) | jnp.any(nbr_blocks[:, :, None] == block_of[None, None, :], axis=1)

    def site_hour(items):
        q_row, k_row, v_row, g_row = items
        q_normed, q_inverse = head_norm(q_row)
        k_normed, k_inverse = head_norm(k_row.astype(jnp.float32))
        scores = jnp.einsum('ihe,jhe->hij', q_normed, k_normed, precision=exact) * scale_factor
        exponent = jnp.where(allowed, jnp.exp(scores), 0.0)
        probs = exponent / lax.optimization_barrier(jnp.sum(exponent, axis=-1, keepdims=True))
        weights = rounded(probs).astype(jnp.float32)
        v_heads = split_heads(v_row.astype(jnp.float32))
        g_heads = split_heads(g_row.astype(jnp.float32))
        heads_out = jnp.einsum('hij,jhe->ihe', weights, v_heads, precision=exact)
        d_probs = jnp.einsum('ihe,jhe->hij', g_heads, v_heads, precision=exact)
        d_scores = probs * (d_probs - lax.optimization_barrier(jnp.sum(probs * d_probs, axis=-1, keepdims=True)))
        d_query = norm_back(q_normed, q_inverse, jnp.einsum('hij,jhe->ihe', d_scores, k_normed, precision=exact) * scale_factor)
        d_key = norm_back(k_normed, k_inverse, jnp.einsum('hij,ihe->jhe', d_scores, q_normed, precision=exact) * scale_factor)
        d_value = jnp.einsum('hij,ihe->jhe', weights, g_heads, precision=exact)
        joined = jnp.concatenate([d_query.reshape(STATIONS, att_width), d_key.reshape(STATIONS, att_width), d_value.reshape(STATIONS, att_width)], axis=1)
        return (heads_out.reshape(STATIONS, att_width).astype(jnp.bfloat16), joined)
    site_swapped, grads_swapped = lax.map(site_hour, (jnp.swapaxes(q_site, 0, 1), jnp.swapaxes(k_site, 0, 1), jnp.swapaxes(v_site, 0, 1), jnp.swapaxes(grad_site, 0, 1)))
    site_out = jnp.swapaxes(site_swapped, 0, 1)
    d_projected = jnp.swapaxes(grads_swapped, 0, 1).reshape(row_count, 3 * att_width).astype(jnp.bfloat16)
    d_normed = jnp.dot(d_projected, w_qkv_site.T, preferred_element_type=jnp.float32)
    gained = norm_gain * d_normed
    d_stream = inv_rms * gained - residual_sum * inv_rms * inv_rms * inv_rms * lax.optimization_barrier(jnp.mean(residual_sum * gained, axis=1, keepdims=True))
    grad_resid = d_stream.astype(jnp.bfloat16)
    d_out = rounded(jnp.dot(grad_resid, w_out_time.T, preferred_element_type=jnp.float32)).reshape(STATIONS, HOURS, att_width)

    def time_backward(items):
        q_row, k_row, v_row, d_row = items
        q_normed, q_inverse, k_normed, k_inverse, probs = time_probs(q_row, k_row)
        weights = rounded(probs).astype(jnp.float32)
        v_heads = split_heads(v_row.astype(jnp.float32))
        d_heads = split_heads(d_row.astype(jnp.float32))
        d_probs = jnp.einsum('qhe,khe->hqk', d_heads, v_heads, precision=exact)
        d_scores = probs * (d_probs - lax.optimization_barrier(jnp.sum(probs * d_probs, axis=-1, keepdims=True)))
        d_query = norm_back(q_normed, q_inverse, jnp.einsum('hqk,khe->qhe', d_scores, k_normed, precision=exact) * scale_factor)
        d_key = norm_back(k_normed, k_inverse, jnp.einsum('hqk,qhe->khe', d_scores, q_normed, precision=exact) * scale_factor)
        d_value = jnp.einsum('hqk,qhe->khe', weights, d_heads, precision=exact)
        return (d_query.reshape(HOURS, att_width).astype(jnp.bfloat16), d_key.reshape(HOURS, att_width).astype(jnp.bfloat16), d_value.reshape(HOURS, att_width).astype(jnp.bfloat16))
    grad_q_time, grad_k_time, grad_v_time = lax.map(time_backward, (q_time, k_time, v_time, d_out))
    return (site_out, grad_q_time, grad_k_time, grad_v_time, grad_resid.reshape(STATIONS, HOURS, MODEL_DIM))
```

```python
import functools

import jax
import jax.numpy as jnp
from jax import lax
from jax.experimental import pallas as pl
from jax.experimental.pallas import tpu as pltpu
from jax.sharding import PartitionSpec as P

HEADS = 6
SIZE = 128
ROWS = 128
ATT = HEADS * SIZE
MODEL = 1536
EPSILON = 1e-05
SCALE = SIZE ** (-0.5)
LOG2E = 1.4426950408889634
LN2 = 0.6931471805599453
SLOTS = 5
WINDOW = SLOTS * ROWS
CHUNKS = 3
WIDTH = ATT // CHUNKS
PER = HEADS // CHUNKS
TILE = 256
BLOCK = 32
F32 = jnp.float32
BF16 = jnp.bfloat16
MESH = pl.DeviceIdType.MESH
OWN = slice(2 * ROWS, 3 * ROWS)


def dot(a, b):
    return jnp.dot(a, b, preferred_element_type=F32)


def dot_nt(a, b):
    return lax.dot_general(a, b, (((1,), (1,)), ((), ())), preferred_element_type=F32)


def lane_mean(x):
    return jnp.sum(x, axis=-1, keepdims=True) * (1.0 / x.shape[-1])


def head_cols(h, base=0):
    return pl.ds(pl.multiple_of(h * SIZE + base, SIZE), SIZE)


def tile_cols(n, base=0):
    return pl.ds(pl.multiple_of(n * TILE + base, TILE), TILE)


def loop(count, body):
    def step(i, carry):
        body(i)
        return carry

    lax.fori_loop(0, count, step, 0)


def kernel(
    tm_count,
    site_count,
    nbr_ref,
    gain_ref,
    q_hbm,
    k_hbm,
    v_hbm,
    resid_hbm,
    wo_hbm,
    wqkv_hbm,
    grad_hbm,
    so_hbm,
    gq_hbm,
    gk_hbm,
    gv_hbm,
    gr_hbm,
    qraw,
    kraw,
    qw,
    kw,
    vw,
    dw,
    dl,
    mask,
    rq_b,
    rk_b,
    itot,
    out_f,
    dcol,
    e_w,
    et_w,
    ow,
    rw,
    gw,
    wo,
    wqkv,
    rsum,
    inv_b,
    nb,
    qf,
    kvb,
    pk,
    pkb,
    prb,
    dqb,
    dkbase,
    dvbase,
    rko,
    dkv,
    dn,
    so_v,
    gq_v,
    gk_v,
    gv_v,
    gr_v,
    load_sem,
    store_sem,
    kv_send,
    kv_recv,
    kv_relay,
    q_send,
    q_recv,
    q_relay,
    r_send,
    r_recv,
    g_send,
    g_recv,
    o_send,
    o_recv,
    p_send,
    p_recv,
    d_send,
    d_recv,
    d_relay,
):
    tm = lax.axis_index("tm")
    st = lax.axis_index("site")
    core = lax.rem(tm, 2)
    sib = tm + 1 - 2 * core
    right_chip = lax.rem(tm + 2 - core, tm_count)
    left_chip = lax.rem(tm - 1 - core + tm_count, tm_count)
    up = lax.rem(st + 1, site_count)
    down = lax.rem(st + site_count - 1, site_count)
    time_dests = ((right_chip, core), (left_chip, 3 + core), (sib, 1 + 2 * core))
    relay_from = 1 + 2 * core
    relay_to = 4 * core
    rest = (4 * core, 3 - 2 * core, 4 - 4 * core)

    loads = [
        pltpu.make_async_copy(src, dst, load_sem.at[n])
        for n, (src, dst) in enumerate(
            (
                (k_hbm.at[0], kraw),
                (q_hbm.at[0], qraw),
                (v_hbm.at[0], vw.at[OWN]),
                (resid_hbm.at[0], rw.at[OWN]),
                (grad_hbm.at[0], gw.at[OWN]),
                (wo_hbm, wo),
                (wqkv_hbm, wqkv),
            )
        )
    ]
    for copy in loads:
        copy.start()

    barrier = pltpu.get_barrier_semaphore()
    for offset in (1, 2, tm_count - 1, tm_count - 2):
        pl.semaphore_signal(
            barrier, inc=1, device_id={"tm": lax.rem(tm + offset, tm_count)}, device_id_type=MESH
        )
    for peer in (up, down):
        pl.semaphore_signal(barrier, inc=1, device_id={"site": peer}, device_id_type=MESH)

    row = lax.broadcasted_iota(jnp.int32, (ROWS, ROWS), 0)
    lane = lax.broadcasted_iota(jnp.int32, (ROWS, ROWS), 1)
    for slot in range(SLOTS):
        shard = tm + slot - 2
        valid = jnp.where((shard >= 0) & (shard < tm_count), 1.0, 0.0).astype(F32)
        if slot == 0:
            band = jnp.where(lane >= row, valid, 0.0)
        elif slot == SLOTS - 1:
            band = jnp.where(lane <= row, valid, 0.0)
        else:
            band = jnp.full((ROWS, ROWS), valid, F32)
        mask[:, slot * ROWS : (slot + 1) * ROWS] = band

    def normalise(raw, store, inverse, factor):
        def body(h):
            cols = head_cols(h)
            x = raw[:, cols].astype(F32)
            r = lax.rsqrt(lane_mean(x * x) + EPSILON)
            inverse[:, cols] = jnp.broadcast_to(r, (ROWS, SIZE))
            store[OWN, cols] = (x * (r * factor)).astype(BF16)

        loop(HEADS, body)

    loads[0].wait()
    normalise(kraw, kw, rk_b, 1.0)
    loads[1].wait()
    normalise(qraw, qw, rq_b, SCALE * LOG2E)
    pl.semaphore_wait(barrier, 6)

    def remote(src, dst, send, recv, device):
        return pltpu.make_async_remote_copy(
            src_ref=src,
            dst_ref=dst,
            send_sem=send,
            recv_sem=recv,
            device_id=device,
            device_id_type=MESH,
        )

    def slot_rows(slot, size=ROWS):
        return pl.ds(pl.multiple_of(slot * size, size), size)

    def kv_copy(kind, ch, n):
        device, slot = time_dests[n]
        cols = tile_cols(ch)
        src = kw.at[OWN, cols] if kind == 0 else v_hbm.at[0, :, cols]
        dst = (kw if kind == 0 else vw).at[slot_rows(slot), cols]
        return remote(
            src, dst, kv_send.at[kind, ch, n], kv_recv.at[kind, ch, slot], {"tm": device}
        )

    def kv_pass(kind, ch):
        cols = tile_cols(ch)
        buffer = kw if kind == 0 else vw
        return remote(
            buffer.at[slot_rows(relay_from), cols],
            buffer.at[slot_rows(relay_to), cols],
            kv_relay.at[kind, ch],
            kv_recv.at[kind, ch, relay_to],
            {"tm": sib},
        )

    def kv_arrive(kind, ch, slot):
        cols = tile_cols(ch)
        here = (kw if kind == 0 else vw).at[slot_rows(slot), cols]
        remote(here, here, kv_relay.at[kind, ch], kv_recv.at[kind, ch, slot], {"tm": sib}).wait_recv()

    def q_copy(n):
        device, slot = time_dests[n]
        return remote(
            qw.at[OWN], qw.at[slot_rows(slot)], q_send.at[n], q_recv.at[slot], {"tm": device}
        )

    def q_pass():
        return remote(
            qw.at[slot_rows(relay_from)],
            qw.at[slot_rows(relay_to)],
            q_relay.at[0],
            q_recv.at[relay_to],
            {"tm": sib},
        )

    def q_arrive(slot):
        here = qw.at[slot_rows(slot)]
        remote(here, here, q_relay.at[0], q_recv.at[slot], {"tm": sib}).wait_recv()

    def site_copy(n, src, dst, send, recv):
        return remote(
            src, dst.at[n * ROWS : (n + 1) * ROWS], send, recv, {"site": (up, down)[n]}
        )

    def out_copy(ch, n):
        cols = tile_cols(ch)
        return remote(
            ow.at[OWN, cols],
            ow.at[n * ROWS : (n + 1) * ROWS, cols],
            o_send.at[ch, n],
            o_recv.at[ch, n],
            {"site": (up, down)[n]},
        )

    def resid_copy(n):
        return site_copy(n, resid_hbm.at[0], rw, r_send.at[n], r_recv.at[n])

    def grad_copy(n):
        return site_copy(n, grad_hbm.at[0], gw, g_send.at[n], g_recv.at[n])

    def pack_copy(n):
        return site_copy(n, pkb.at[n * ROWS : (n + 1) * ROWS], prb, p_send.at[n], p_recv.at[n])

    def d_copy(kind, ch, n):
        device, slot = time_dests[n]
        cols = tile_cols(ch)
        buffer, size = ((dw, ROWS), (dl, 16))[kind]
        return remote(
            buffer.at[2 * size : 3 * size, cols],
            buffer.at[slot_rows(slot, size), cols],
            d_send.at[kind, ch, n],
            d_recv.at[kind, ch, slot],
            {"tm": device},
        )

    def d_pass(kind, ch):
        cols = tile_cols(ch)
        buffer, size = ((dw, ROWS), (dl, 16))[kind]
        return remote(
            buffer.at[slot_rows(relay_from, size), cols],
            buffer.at[slot_rows(relay_to, size), cols],
            d_relay.at[kind, ch],
            d_recv.at[kind, ch, relay_to],
            {"tm": sib},
        )

    def d_arrive(kind, ch, slot):
        cols = tile_cols(ch)
        buffer, size = ((dw, ROWS), (dl, 16))[kind]
        here = buffer.at[slot_rows(slot, size), cols]
        remote(here, here, d_relay.at[kind, ch], d_recv.at[kind, ch, slot], {"tm": sib}).wait_recv()

    for ch in range(CHUNKS):
        for n in range(3):
            for kind in range(2):
                kv_copy(kind, ch, n).start()
        if ch == 0:
            for n in range(2):
                resid_copy(n).start()
    for n in range(3):
        q_copy(n).start()
    loads[2].wait()

    def forward(ch):
        for kind in range(2):
            kv_arrive(kind, ch, relay_from)
            kv_pass(kind, ch).start()
        for slot in rest:
            for kind in range(2):
                kv_arrive(kind, ch, slot)
        for part in range(PER):
            h = ch * PER + part
            cols = head_cols(h)
            weights = (
                jnp.exp2(dot_nt(qw[OWN, cols], kw[:, cols])) * mask[...]
            ).astype(BF16)
            e_w[h] = weights
            inverse = 1.0 / jnp.sum(weights.astype(F32), axis=-1, keepdims=True)
            heads_out = dot(weights, vw[:, cols]) * inverse
            itot[:, cols] = jnp.broadcast_to(inverse, (ROWS, SIZE))
            out_f[:, cols] = heads_out
            ow[OWN, cols] = heads_out.astype(BF16)
        for n in range(2):
            out_copy(ch, n).start()

    loop(CHUNKS, forward)
    for n in range(2):
        grad_copy(n).start()

    def project_out(first, count):
        rows = slice(first, first + count)

        def body(n):
            cols = tile_cols(n)
            rsum[rows, cols] = rw[rows, cols].astype(F32) + dot(ow[rows, :], wo[:, cols])

        loop(MODEL // TILE, body)

    def norm_rows(first, count):
        def body(b):
            rows = pl.ds(pl.multiple_of(first + b * BLOCK, BLOCK), BLOCK)
            x = rsum[rows, :]
            inverse = lax.rsqrt(lane_mean(x * x) + EPSILON)
            inv_b[rows, :] = jnp.broadcast_to(inverse, (BLOCK, SIZE))
            nb[rows, :] = (x * inverse * gain_ref[...]).astype(BF16)

        loop(count // BLOCK, body)

    def project_q(first, count):
        rows = slice(first, first + count)

        def body(n):
            qf[rows, tile_cols(n)] = dot(nb[rows, :], wqkv[:, tile_cols(n)])

        loop(ATT // TILE, body)

    def project_kv(first, count):
        rows = slice(first, first + count)

        def body(n):
            kvb[rows, tile_cols(n)] = dot(nb[rows, :], wqkv[:, tile_cols(n, ATT)]).astype(BF16)

        loop(2 * ATT // TILE, body)

    loads[3].wait()
    loads[5].wait()
    project_out(2 * ROWS, ROWS)
    norm_rows(2 * ROWS, ROWS)
    loads[6].wait()
    project_q(2 * ROWS, ROWS)
    project_kv(2 * ROWS, ROWS)
    q_arrive(relay_from)
    q_pass().start()

    for n in range(2):
        resid_copy(n).wait_recv()
        for ch in range(CHUNKS):
            out_copy(ch, n).wait_recv()
    project_out(0, 2 * ROWS)
    norm_rows(0, 2 * ROWS)
    project_kv(0, 2 * ROWS)
    loads[4].wait()

    first_named, second_named = nbr_ref[0, 0], nbr_ref[0, 1]
    seen = [
        jnp.where((first_named == peer) | (second_named == peer), 1.0, 0.0).astype(F32)
        for peer in (st - 1, st + 1)
    ]

    def site_head(h):
        cols = head_cols(h)
        q = qf[OWN, cols]
        grad = gw[OWN, cols].astype(F32)
        keys = [kvb[x * ROWS : (x + 1) * ROWS, cols].astype(F32) for x in range(3)]
        values = [
            kvb[x * ROWS : (x + 1) * ROWS, head_cols(h, ATT)].astype(F32) for x in range(3)
        ]
        q_inv = lax.rsqrt(lane_mean(q * q) + EPSILON)
        k_inv = [lax.rsqrt(lane_mean(k * k) + EPSILON) for k in keys]
        scores = [
            jnp.sum(q * k, axis=-1, keepdims=True) * (q_inv * r * SCALE)
            for k, r in zip(keys, k_inv)
        ]
        exps = [jnp.exp(s) for s in scores]
        exps = [exps[0] * seen[0], exps[1] * seen[1], exps[2]]
        inverse = 1.0 / (exps[0] + exps[1] + exps[2])
        probs = [e * inverse for e in exps]
        rounded = [p.astype(BF16).astype(F32) for p in probs]
        dprobs = [jnp.sum(grad * v, axis=-1, keepdims=True) for v in values]
        delta = probs[0] * dprobs[0] + probs[1] * dprobs[1] + probs[2] * dprobs[2]
        dscores = [p * (d - delta) for p, d in zip(probs, dprobs)]
        along = [d * s for d, s in zip(dscores, scores)]
        scaled = [d * (q_inv * SCALE) for d in dscores]
        for n in range(2):
            x = 1 - n
            rows = slice(n * ROWS, (n + 1) * ROWS)
            old = pk[rows, :]
            pk[rows, :] = jnp.where(
                lane == h,
                scaled[x],
                jnp.where(lane == h + 8, along[x], jnp.where(lane == h + 16, rounded[x], old)),
            )
        so_v[:, cols] = (
            rounded[0] * values[0] + rounded[1] * values[1] + rounded[2] * values[2]
        ).astype(BF16)
        dq = (
            scaled[0] * k_inv[0] * keys[0]
            + scaled[1] * k_inv[1] * keys[1]
            + scaled[2] * k_inv[2] * keys[2]
            - q * (q_inv * q_inv * (along[0] + along[1] + along[2]) * (1.0 / SIZE))
        )
        dqb[:, cols] = dq.astype(BF16)
        dkbase[:, cols] = (scaled[2] * k_inv[2]) * q - (
            k_inv[2] * k_inv[2] * along[2] * (1.0 / SIZE)
        ) * keys[2]
        dvbase[:, cols] = rounded[2] * grad
        rko[:, cols] = jnp.broadcast_to(k_inv[2], (ROWS, SIZE))

    pk[...] = jnp.zeros_like(pk)
    loop(HEADS, site_head)
    pkb[...] = pk[...].astype(BF16)
    for n in range(2):
        pack_copy(n).start()
    so_store = pltpu.make_async_copy(so_v, so_hbm.at[0], store_sem.at[0])
    so_store.start()

    def back_q(n):
        dn[:, tile_cols(n)] = dot_nt(dqb[...], wqkv[tile_cols(n), :ATT])

    loop(MODEL // TILE, back_q)
    project_q(0, 2 * ROWS)

    for slot in rest:
        q_arrive(slot)

    def key_side(h):
        cols = head_cols(h)
        et_w[h] = (jnp.exp2(dot_nt(kw[OWN, cols], qw[:, cols])) * mask[...]).astype(BF16)

    loop(HEADS, key_side)

    for n in range(2):
        grad_copy(n).wait_recv()
        pack_copy(n).wait_recv()

    def site_keys(h):
        cols = head_cols(h)
        pick_row = lax.broadcasted_iota(jnp.int32, (SIZE, 3 * SIZE), 0)
        pick_col = lax.broadcasted_iota(jnp.int32, (SIZE, 3 * SIZE), 1)
        pick = jnp.where(pick_row == pick_col // SIZE * 8 + h, 1.0, 0.0).astype(BF16)
        spread = dot(prb[...], pick)
        inverse = rko[:, cols]
        dkey, dvalue, along = dkbase[:, cols], dvbase[:, cols], 0.0
        gathered = 0.0
        for x in range(2):
            rows = slice(x * ROWS, (x + 1) * ROWS)
            gathered = gathered + spread[rows, :SIZE] * qf[rows, cols]
            along = along + spread[rows, SIZE : 2 * SIZE]
            dvalue = dvalue + spread[rows, 2 * SIZE :] * gw[rows, cols].astype(F32)
        own_key = kvb[OWN, cols].astype(F32)
        dkey = dkey + inverse * gathered - inverse * inverse * (1.0 / SIZE) * along * own_key
        dkv[:, cols] = dkey.astype(BF16)
        dkv[:, head_cols(h, ATT)] = dvalue.astype(BF16)

    loop(HEADS, site_keys)

    def back_kv(n):
        cols = tile_cols(n)
        dn[:, cols] += dot_nt(dkv[...], wqkv[cols, ATT:])

    loop(MODEL // TILE, back_kv)

    def back_norm(b):
        rows = pl.ds(pl.multiple_of(b * BLOCK, BLOCK), BLOCK)
        own = pl.ds(pl.multiple_of(2 * ROWS + b * BLOCK, BLOCK), BLOCK)
        inverse = inv_b[own, :][:, :1]
        x = rsum[own, :]
        gained = gain_ref[...] * dn[rows, :]
        average = lane_mean(x * gained)
        gr_v[rows, :] = (
            inverse * gained - x * (inverse * inverse * inverse * average)
        ).astype(BF16)

    loop(ROWS // BLOCK, back_norm)
    gr_store = pltpu.make_async_copy(gr_v, gr_hbm.at[0], store_sem.at[1])
    gr_store.start()

    def back_out(ch):
        cols = tile_cols(ch)
        d_rows = (dot_nt(gr_v[...], wo[cols, :]) * itot[:, cols]).astype(BF16)
        dw[OWN, cols] = d_rows
        product = out_f[:, cols] * d_rows.astype(F32)
        high = product.astype(BF16)
        low = (product - high.astype(F32)).astype(BF16)
        ones = jnp.ones((16, SIZE), BF16)
        kept = lax.broadcasted_iota(jnp.int32, (16, SIZE), 0)
        for part in range(PER):
            cut = slice(part * SIZE, (part + 1) * SIZE)
            here = head_cols(ch * PER + part)
            total = jnp.sum(product[:, cut], axis=-1, keepdims=True)
            dcol[:, here] = jnp.broadcast_to(total, (ROWS, SIZE))
            line = dot_nt(ones, high[:, cut]) + dot_nt(ones, low[:, cut])
            top = line.astype(BF16).astype(F32)
            dl[32:48, here] = jnp.where(
                kept == 0, top, jnp.where(kept == 1, line - top, 0.0)
            ).astype(BF16)
        for n in range(3):
            for kind in range(2):
                d_copy(kind, ch, n).start()

    loop(CHUNKS, back_out)

    def query_side(ch):
        for part in range(PER):
            h = ch * PER + part
            cols = head_cols(h)
            dprobs = dot_nt(dw[OWN, cols], vw[:, cols])
            dscores = e_w[h].astype(F32) * (dprobs - dcol[:, cols][:, :1])
            grads = dot(dscores.astype(BF16), kw[:, cols]) * SCALE
            inverse = rq_b[:, cols]
            normed = qraw[:, cols].astype(F32) * inverse
            gq_v[:, cols] = (inverse * (grads - normed * lane_mean(normed * grads))).astype(BF16)
        for kind in range(2):
            d_arrive(kind, ch, relay_from)
            d_pass(kind, ch).start()

    loop(CHUNKS, query_side)
    gq_store = pltpu.make_async_copy(gq_v, gq_hbm.at[0], store_sem.at[2])
    gq_store.start()

    def key_grads(ch):
        for slot in rest:
            for kind in range(2):
                d_arrive(kind, ch, slot)
        for part in range(PER):
            h = ch * PER + part
            cols = head_cols(h)
            d_rows = dw[:, cols]
            lines = []
            for slot in range(SLOTS):
                line = dl[slot * 16 : (slot + 1) * 16, cols].astype(F32)
                lines.append(line[0:1] + line[1:2])
            weights = et_w[h]
            dprobs = dot_nt(vw[OWN, cols], d_rows)
            dscores = weights.astype(F32) * (dprobs - jnp.concatenate(lines, axis=1))
            grads = dot(dscores.astype(BF16), qw[:, cols]) * LN2
            inverse = rk_b[:, cols]
            normed = kraw[:, cols].astype(F32) * inverse
            gk_v[:, cols] = (inverse * (grads - normed * lane_mean(normed * grads))).astype(BF16)
            gv_v[:, cols] = dot(weights, d_rows).astype(BF16)

    loop(CHUNKS, key_grads)
    gk_store = pltpu.make_async_copy(gk_v, gk_hbm.at[0], store_sem.at[3])
    gv_store = pltpu.make_async_copy(gv_v, gv_hbm.at[0], store_sem.at[4])
    gk_store.start()
    gv_store.start()

    for ch in range(CHUNKS):
        for kind in range(2):
            for n in range(3):
                kv_copy(kind, ch, n).wait_send()
                d_copy(kind, ch, n).wait_send()
            kv_pass(kind, ch).wait_send()
            d_pass(kind, ch).wait_send()
        for n in range(2):
            out_copy(ch, n).wait_send()
    for n in range(3):
        q_copy(n).wait_send()
    q_pass().wait_send()
    for n in range(2):
        resid_copy(n).wait_send()
        grad_copy(n).wait_send()
        pack_copy(n).wait_send()
    for copy in (so_store, gr_store, gq_store, gk_store, gv_store):
        copy.wait()


def shards(tm_count, site_count, q_time, k_time, v_time, resid, w_out_time, norm_gain, w_qkv_site, grad_site, nbr_blocks):
    assert q_time.shape == (1, ROWS, ATT) and resid.shape == (1, ROWS, MODEL)
    anywhere = pl.BlockSpec(memory_space=pl.ANY)
    narrow = jax.ShapeDtypeStruct((1, ROWS, ATT), BF16)
    wide = jax.ShapeDtypeStruct((1, ROWS, MODEL), BF16)
    vmem = pltpu.VMEM
    dma = pltpu.SemaphoreType.DMA
    return pl.pallas_call(
        functools.partial(kernel, tm_count, site_count),
        out_shape=(narrow, narrow, narrow, narrow, wide),
        in_specs=[
            pl.BlockSpec(memory_space=pltpu.SMEM),
            pl.BlockSpec(memory_space=pltpu.VMEM),
        ]
        + [anywhere] * 7,
        out_specs=(anywhere,) * 5,
        scratch_shapes=[
            vmem((ROWS, ATT), BF16),
            vmem((ROWS, ATT), BF16),
            vmem((WINDOW, ATT), BF16),
            vmem((WINDOW, ATT), BF16),
            vmem((WINDOW, ATT), BF16),
            vmem((WINDOW, ATT), BF16),
            vmem((SLOTS * 16, ATT), BF16),
            vmem((ROWS, WINDOW), F32),
            vmem((ROWS, ATT), F32),
            vmem((ROWS, ATT), F32),
            vmem((ROWS, ATT), F32),
            vmem((ROWS, ATT), F32),
            vmem((ROWS, ATT), F32),
            vmem((HEADS, ROWS, WINDOW), BF16),
            vmem((HEADS, ROWS, WINDOW), BF16),
            vmem((3 * ROWS, ATT), BF16),
            vmem((3 * ROWS, MODEL), BF16),
            vmem((3 * ROWS, ATT), BF16),
            vmem((ATT, MODEL), BF16),
            vmem((MODEL, 3 * ATT), BF16),
            vmem((3 * ROWS, MODEL), F32),
            vmem((3 * ROWS, SIZE), F32),
            vmem((3 * ROWS, MODEL), BF16),
            vmem((3 * ROWS, ATT), F32),
            vmem((3 * ROWS, 2 * ATT), BF16),
            vmem((2 * ROWS, SIZE), F32),
            vmem((2 * ROWS, SIZE), BF16),
            vmem((2 * ROWS, SIZE), BF16),
            vmem((ROWS, ATT), BF16),
            vmem((ROWS, ATT), F32),
            vmem((ROWS, ATT), F32),
            vmem((ROWS, ATT), F32),
            vmem((ROWS, 2 * ATT), BF16),
            vmem((ROWS, MODEL), F32),
            vmem((ROWS, ATT), BF16),
            vmem((ROWS, ATT), BF16),
            vmem((ROWS, ATT), BF16),
            vmem((ROWS, ATT), BF16),
            vmem((ROWS, MODEL), BF16),
            dma((7,)),
            dma((5,)),
            dma((2, CHUNKS, 3)),
            dma((2, CHUNKS, SLOTS)),
            dma((2, CHUNKS)),
            dma((3,)),
            dma((SLOTS,)),
            dma((1,)),
            dma((2,)),
            dma((2,)),
            dma((2,)),
            dma((2,)),
            dma((CHUNKS, 2)),
            dma((CHUNKS, 2)),
            dma((2,)),
            dma((2,)),
            dma((2, CHUNKS, 3)),
            dma((2, CHUNKS, SLOTS)),
            dma((2, CHUNKS)),
        ],
        compiler_params=pltpu.CompilerParams(
            collective_id=0, has_side_effects=True, vmem_limit_bytes=56 * 1024 * 1024
        ),
    )(
        nbr_blocks,
        norm_gain.reshape(1, MODEL),
        q_time,
        k_time,
        v_time,
        resid,
        w_out_time,
        w_qkv_site,
        grad_site,
    )


def solution(mesh):
    rows = P("site", "tm", None)
    return jax.shard_map(
        functools.partial(shards, mesh.shape["tm"], mesh.shape["site"]),
        mesh=mesh,
        in_specs=(rows, rows, rows, rows, P(), P(), P(), rows, P("site", None)),
        out_specs=(rows,) * 5,
        check_vma=False,
    )
```

```python
import functools

import jax
import jax.numpy as jnp
from jax import lax
from jax.experimental import pallas as pl
from jax.experimental.pallas import tpu as pltpu
from jax.sharding import PartitionSpec as P

HEADS = 6
SIZE = 128
ROWS = 128
ATT = HEADS * SIZE
MODEL = 1536
EPSILON = 1e-05
SCALE = SIZE ** (-0.5)
LOG2E = 1.4426950408889634
LN2 = 0.6931471805599453
SLOTS = 5
WINDOW = SLOTS * ROWS
CHUNKS = 3
WIDTH = ATT // CHUNKS
PER = HEADS // CHUNKS
TILE = 256
BLOCK = 32
F32 = jnp.float32
BF16 = jnp.bfloat16
MESH = pl.DeviceIdType.MESH
OWN = slice(2 * ROWS, 3 * ROWS)


def dot(a, b):
    return jnp.dot(a, b, preferred_element_type=F32)


def dot_nt(a, b):
    return lax.dot_general(a, b, (((1,), (1,)), ((), ())), preferred_element_type=F32)


def lane_mean(x):
    return jnp.sum(x, axis=-1, keepdims=True) * (1.0 / x.shape[-1])


def head_cols(h, base=0):
    return slice(h * SIZE + base, (h + 1) * SIZE + base)


def tile_cols(n, base=0):
    return slice(n * TILE + base, (n + 1) * TILE + base)


def loop(count, body):
    for i in range(count):
        body(i)


def kernel(
    tm_count,
    site_count,
    nbr_ref,
    gain_ref,
    q_hbm,
    k_hbm,
    v_hbm,
    resid_hbm,
    wo_hbm,
    wqkv_hbm,
    grad_hbm,
    so_hbm,
    gq_hbm,
    gk_hbm,
    gv_hbm,
    gr_hbm,
    qraw,
    kraw,
    qw,
    kw,
    vw,
    dw,
    dl,
    mask,
    rq_b,
    rk_b,
    itot,
    out_f,
    dcol,
    e_w,
    et_w,
    ow,
    rw,
    gw,
    wo,
    wqkv,
    rsum,
    inv_b,
    nb,
    qf,
    kvb,
    pick,
    pkb,
    prb,
    dqb,
    dkbase,
    dvbase,
    rko,
    dkv,
    dn,
    so_v,
    gq_v,
    gk_v,
    gv_v,
    gr_v,
    load_sem,
    store_sem,
    kv_send,
    kv_recv,
    kv_relay,
    q_send,
    q_recv,
    q_relay,
    r_send,
    r_recv,
    g_send,
    g_recv,
    o_send,
    o_recv,
    p_send,
    p_recv,
    d_send,
    d_recv,
    d_relay,
):
    tm = lax.axis_index("tm")
    st = lax.axis_index("site")
    core = lax.rem(tm, 2)
    sib = tm + 1 - 2 * core
    right_chip = lax.rem(tm + 2 - core, tm_count)
    left_chip = lax.rem(tm - 1 - core + tm_count, tm_count)
    up = lax.rem(st + 1, site_count)
    down = lax.rem(st + site_count - 1, site_count)
    time_dests = ((right_chip, core), (left_chip, 3 + core), (sib, 1 + 2 * core))
    relay_from = 1 + 2 * core
    relay_to = 4 * core
    rest = (4 * core, 3 - 2 * core, 4 - 4 * core)

    loads = [
        pltpu.make_async_copy(src, dst, load_sem.at[n])
        for n, (src, dst) in enumerate(
            (
                (k_hbm.at[0], kraw),
                (q_hbm.at[0], qraw),
                (v_hbm.at[0], vw.at[OWN]),
                (resid_hbm.at[0], rw.at[OWN]),
                (grad_hbm.at[0], gw.at[OWN]),
                (wo_hbm, wo),
                (wqkv_hbm, wqkv),
            )
        )
    ]
    for copy in loads:
        copy.start()

    barrier = pltpu.get_barrier_semaphore()
    for offset in (1, 2, tm_count - 1, tm_count - 2):
        pl.semaphore_signal(
            barrier, inc=1, device_id={"tm": lax.rem(tm + offset, tm_count)}, device_id_type=MESH
        )
    for peer in (up, down):
        pl.semaphore_signal(barrier, inc=1, device_id={"site": peer}, device_id_type=MESH)

    row = lax.broadcasted_iota(jnp.int32, (ROWS, ROWS), 0)
    lane = lax.broadcasted_iota(jnp.int32, (ROWS, ROWS), 1)
    for slot in range(SLOTS):
        shard = tm + slot - 2
        valid = jnp.where((shard >= 0) & (shard < tm_count), 1.0, 0.0).astype(F32)
        if slot == 0:
            band = jnp.where(lane >= row, valid, 0.0)
        elif slot == SLOTS - 1:
            band = jnp.where(lane <= row, valid, 0.0)
        else:
            band = jnp.full((ROWS, ROWS), valid, F32)
        mask[:, slot * ROWS : (slot + 1) * ROWS] = band

    for h in range(HEADS):
        for n in range(3):
            pick[:, head_cols(3 * h + n)] = jnp.where(row == 8 * n + h, 1.0, 0.0).astype(BF16)

    def normalise(raw, store, inverse, factor):
        def body(h):
            cols = head_cols(h)
            x = raw[:, cols].astype(F32)
            r = lax.rsqrt(lane_mean(x * x) + EPSILON)
            inverse[:, cols] = jnp.broadcast_to(r, (ROWS, SIZE))
            store[OWN, cols] = (x * (r * factor)).astype(BF16)

        loop(HEADS, body)

    def remote(src, dst, send, recv, device):
        return pltpu.make_async_remote_copy(
            src_ref=src,
            dst_ref=dst,
            send_sem=send,
            recv_sem=recv,
            device_id=device,
            device_id_type=MESH,
        )

    def slot_rows(slot, size=ROWS):
        return pl.ds(pl.multiple_of(slot * size, size), size)

    def kv_copy(kind, ch, n):
        device, slot = time_dests[n]
        cols = tile_cols(ch)
        src = kw.at[OWN, cols] if kind == 0 else v_hbm.at[0, :, cols]
        dst = (kw if kind == 0 else vw).at[slot_rows(slot), cols]
        return remote(
            src, dst, kv_send.at[kind, ch, n], kv_recv.at[kind, ch, slot], {"tm": device}
        )

    def kv_pass(kind, ch):
        cols = tile_cols(ch)
        buffer = kw if kind == 0 else vw
        return remote(
            buffer.at[slot_rows(relay_from), cols],
            buffer.at[slot_rows(relay_to), cols],
            kv_relay.at[kind, ch],
            kv_recv.at[kind, ch, relay_to],
            {"tm": sib},
        )

    def kv_arrive(kind, ch, slot):
        cols = tile_cols(ch)
        here = (kw if kind == 0 else vw).at[slot_rows(slot), cols]
        remote(here, here, kv_relay.at[kind, ch], kv_recv.at[kind, ch, slot], {"tm": sib}).wait_recv()

    def q_copy(n):
        device, slot = time_dests[n]
        return remote(
            qw.at[OWN], qw.at[slot_rows(slot)], q_send.at[n], q_recv.at[slot], {"tm": device}
        )

    def q_pass():
        return remote(
            qw.at[slot_rows(relay_from)],
            qw.at[slot_rows(relay_to)],
            q_relay.at[0],
            q_recv.at[relay_to],
            {"tm": sib},
        )

    def q_arrive(slot):
        here = qw.at[slot_rows(slot)]
        remote(here, here, q_relay.at[0], q_recv.at[slot], {"tm": sib}).wait_recv()

    def site_copy(n, src, dst, send, recv):
        return remote(
            src, dst.at[n * ROWS : (n + 1) * ROWS], send, recv, {"site": (up, down)[n]}
        )

    def out_copy(ch, n):
        cols = tile_cols(ch)
        return remote(
            ow.at[OWN, cols],
            ow.at[n * ROWS : (n + 1) * ROWS, cols],
            o_send.at[ch, n],
            o_recv.at[ch, n],
            {"site": (up, down)[n]},
        )

    def resid_copy(n):
        return site_copy(n, resid_hbm.at[0], rw, r_send.at[n], r_recv.at[n])

    def grad_copy(half, n):
        cols = slice(half * (ATT // 2), (half + 1) * (ATT // 2))
        return remote(
            grad_hbm.at[0, :, cols],
            gw.at[n * ROWS : (n + 1) * ROWS, cols],
            g_send.at[half, n],
            g_recv.at[half, n],
            {"site": (up, down)[n]},
        )

    def pack_copy(n):
        return site_copy(n, pkb.at[n * ROWS : (n + 1) * ROWS], prb, p_send.at[n], p_recv.at[n])

    def d_copy(kind, ch, n):
        device, slot = time_dests[n]
        cols = tile_cols(ch)
        buffer, size = ((dw, ROWS), (dl, 8))[kind]
        return remote(
            buffer.at[2 * size : 3 * size, cols],
            buffer.at[slot_rows(slot, size), cols],
            d_send.at[kind, ch, n],
            d_recv.at[kind, ch, slot],
            {"tm": device},
        )

    def d_pass(kind, ch):
        cols = tile_cols(ch)
        buffer, size = ((dw, ROWS), (dl, 8))[kind]
        return remote(
            buffer.at[slot_rows(relay_from, size), cols],
            buffer.at[slot_rows(relay_to, size), cols],
            d_relay.at[kind, ch],
            d_recv.at[kind, ch, relay_to],
            {"tm": sib},
        )

    def d_arrive(kind, ch, slot):
        cols = tile_cols(ch)
        buffer, size = ((dw, ROWS), (dl, 8))[kind]
        here = buffer.at[slot_rows(slot, size), cols]
        remote(here, here, d_relay.at[kind, ch], d_recv.at[kind, ch, slot], {"tm": sib}).wait_recv()

    pl.semaphore_wait(barrier, 6)
    for n in range(3):
        kv_copy(1, 0, n).start()
    for n in range(2):
        resid_copy(n).start()
    loads[0].wait()
    normalise(kraw, kw, rk_b, 1.0)
    for ch in range(CHUNKS):
        for kind in range(2) if ch == 0 else (1, 0):
            if (kind, ch) != (1, 0):
                for n in range(3):
                    kv_copy(kind, ch, n).start()
    for n in range(3):
        if n == 0:
            loads[1].wait()
            normalise(qraw, qw, rq_b, SCALE * LOG2E)
        q_copy(n).start()
    loads[2].wait()
    loads[3].wait()
    loads[5].wait()

    def project_out(ch, first, count):
        rows = slice(first, first + count)
        squares = 0.0
        for n in range(MODEL // TILE):
            cols = tile_cols(n)
            before = rw[rows, cols].astype(F32) if ch == 0 else rsum[rows, cols]
            x = before + dot(ow[rows, tile_cols(ch)], wo[tile_cols(ch), cols])
            rsum[rows, cols] = x
            if ch == CHUNKS - 1:
                nb[rows, cols] = (x * gain_ref[cols][None, :]).astype(BF16)
                squares = squares + x[:, :SIZE] * x[:, :SIZE] + x[:, SIZE:] * x[:, SIZE:]
        if ch == CHUNKS - 1:
            mean = jnp.sum(squares, axis=-1, keepdims=True) * (1.0 / MODEL)
            inv_b[rows, :] = jnp.broadcast_to(lax.rsqrt(mean + EPSILON), (count, SIZE))

    def forward(ch):
        for kind in (1, 0):
            kv_arrive(kind, ch, relay_from)
            kv_pass(kind, ch).start()
        for slot in rest:
            for kind in range(2):
                kv_arrive(kind, ch, slot)
        for part in range(PER):
            h = ch * PER + part
            cols = head_cols(h)
            weights = (
                jnp.exp2(dot_nt(qw[OWN, cols], kw[:, cols])) * mask[...]
            ).astype(BF16)
            e_w[h] = weights
            inverse = 1.0 / jnp.sum(weights.astype(F32), axis=-1, keepdims=True)
            heads_out = dot(weights, vw[:, cols]) * inverse
            itot[:, cols] = jnp.broadcast_to(inverse, (ROWS, SIZE))
            out_f[:, cols] = heads_out
            ow[OWN, cols] = heads_out.astype(BF16)
        for n in range(2):
            out_copy(ch, n).start()
        project_out(ch, 2 * ROWS, ROWS)

    loop(CHUNKS, forward)
    for n in range(2):
        grad_copy(0, n).start()

    def project_q(first, count):
        rows = slice(first, first + count)

        def body(n):
            inverse = jnp.concatenate([inv_b[rows, :]] * 2, axis=1)
            qf[rows, tile_cols(n)] = dot(nb[rows, :], wqkv[:, tile_cols(n)]) * inverse

        loop(ATT // TILE, body)

    def project_kv(first, count):
        rows = slice(first, first + count)

        def body(n):
            inverse = jnp.concatenate([inv_b[rows, :]] * 2, axis=1)
            product = dot(nb[rows, :], wqkv[:, tile_cols(n, ATT)])
            kvb[rows, tile_cols(n)] = (product * inverse).astype(BF16)

        loop(2 * ATT // TILE, body)

    loads[6].wait()
    project_q(2 * ROWS, ROWS)
    project_kv(2 * ROWS, ROWS)
    loads[4].wait()

    first_named, second_named = nbr_ref[0, 0], nbr_ref[0, 1]
    seen = [
        jnp.where((first_named == peer) | (second_named == peer), 1.0, 0.0).astype(F32)
        for peer in (st - 1, st + 1)
    ]

    def site_key(h, x):
        return kvb[x * ROWS : (x + 1) * ROWS, head_cols(h)].astype(F32)

    def site_value(h, x):
        return kvb[x * ROWS : (x + 1) * ROWS, head_cols(h, ATT)].astype(F32)

    def site_scores(h, x):
        key = site_key(h, x)
        k_inv = lax.rsqrt(lane_mean(key * key) + EPSILON)
        score = jnp.sum(qf[OWN, head_cols(h)] * key, axis=-1, keepdims=True)
        grad = gw[OWN, head_cols(h)].astype(F32)
        dprob = jnp.sum(grad * site_value(h, x), axis=-1, keepdims=True)
        return k_inv, score, dprob

    own_stats = []
    for h in range(HEADS):
        q = qf[OWN, head_cols(h)]
        q_inv = lax.rsqrt(lane_mean(q * q) + EPSILON)
        own_stats.append((q_inv, site_scores(h, 2)))

    q_arrive(relay_from)
    q_pass().start()

    for n in range(2):
        resid_copy(n).wait_recv()
    for ch in range(CHUNKS):
        for n in range(2):
            out_copy(ch, n).wait_recv()
        project_out(ch, 0, 2 * ROWS)
    project_kv(0, 2 * ROWS)

    site_stats = []
    packs = [jnp.zeros((ROWS, SIZE), F32) for _ in range(2)]
    for h in range(HEADS):
        q_inv, own = own_stats[h]
        k_inv, scores, dprobs = zip(site_scores(h, 0), site_scores(h, 1), own)
        scores = [s * (q_inv * r * SCALE) for s, r in zip(scores, k_inv)]
        exps = [jnp.exp(s) for s in scores]
        exps = [exps[0] * seen[0], exps[1] * seen[1], exps[2]]
        inverse = 1.0 / (exps[0] + exps[1] + exps[2])
        probs = [e * inverse for e in exps]
        rounded = [p.astype(BF16).astype(F32) for p in probs]
        delta = probs[0] * dprobs[0] + probs[1] * dprobs[1] + probs[2] * dprobs[2]
        dscores = [p * (d - delta) for p, d in zip(probs, dprobs)]
        along = [d * s for d, s in zip(dscores, scores)]
        scaled = [d * (q_inv * SCALE) for d in dscores]
        for n in range(2):
            x = 1 - n
            for place, value in enumerate((scaled[x], along[x], rounded[x])):
                packs[n] = jnp.where(lane == h + 8 * place, value, packs[n])
        site_stats.append((q_inv, k_inv, rounded, along, scaled))
    for n in range(2):
        pkb[n * ROWS : (n + 1) * ROWS, :] = packs[n].astype(BF16)
        pack_copy(n).start()
    for n in range(2):
        grad_copy(1, n).start()

    def site_head(h):
        cols = head_cols(h)
        q_inv, k_inv, rounded, along, scaled = site_stats[h]
        q = qf[OWN, cols]
        keys = [site_key(h, x) for x in range(3)]
        values = [site_value(h, x) for x in range(3)]
        dq = (
            scaled[0] * k_inv[0] * keys[0]
            + scaled[1] * k_inv[1] * keys[1]
            + scaled[2] * k_inv[2] * keys[2]
            - q * (q_inv * q_inv * (along[0] + along[1] + along[2]) * (1.0 / SIZE))
        )
        dqb[:, cols] = dq.astype(BF16)
        so_v[:, cols] = (
            rounded[0] * values[0] + rounded[1] * values[1] + rounded[2] * values[2]
        ).astype(BF16)
        dkbase[:, cols] = (scaled[2] * k_inv[2]) * q - (
            k_inv[2] * k_inv[2] * along[2] * (1.0 / SIZE)
        ) * keys[2]
        dvbase[:, cols] = rounded[2] * gw[OWN, cols].astype(F32)
        rko[:, cols] = jnp.broadcast_to(k_inv[2], (ROWS, SIZE))

    loop(HEADS, site_head)
    so_store = pltpu.make_async_copy(so_v, so_hbm.at[0], store_sem.at[0])
    so_store.start()

    def back_q(n):
        dn[:, tile_cols(n)] = dot_nt(dqb[...], wqkv[tile_cols(n), :ATT])

    loop(MODEL // TILE, back_q)
    project_q(0, 2 * ROWS)

    for slot in rest:
        q_arrive(slot)

    def key_side(h):
        cols = head_cols(h)
        et_w[h] = (jnp.exp2(dot_nt(kw[OWN, cols], qw[:, cols])) * mask[...]).astype(BF16)

    loop(HEADS, key_side)

    for n in range(2):
        pack_copy(n).wait_recv()

    def site_keys(h):
        cols = head_cols(h)
        if h % (HEADS // 2) == 0:
            for n in range(2):
                grad_copy(h // (HEADS // 2), n).wait_recv()
        spread = dot(prb[...], pick[:, 3 * h * SIZE : 3 * (h + 1) * SIZE])
        inverse = rko[:, cols]
        dkey, dvalue, along = dkbase[:, cols], dvbase[:, cols], 0.0
        gathered = 0.0
        for x in range(2):
            rows = slice(x * ROWS, (x + 1) * ROWS)
            gathered = gathered + spread[rows, :SIZE] * qf[rows, cols]
            along = along + spread[rows, SIZE : 2 * SIZE]
            dvalue = dvalue + spread[rows, 2 * SIZE :] * gw[rows, cols].astype(F32)
        own_key = kvb[OWN, cols].astype(F32)
        dkey = dkey + inverse * gathered - inverse * inverse * (1.0 / SIZE) * along * own_key
        dkv[:, cols] = dkey.astype(BF16)
        dkv[:, head_cols(h, ATT)] = dvalue.astype(BF16)

    loop(HEADS, site_keys)

    product = 0.0
    for n in range(MODEL // TILE):
        cols = tile_cols(n)
        gained = gain_ref[cols][None, :] * (dn[:, cols] + dot_nt(dkv[...], wqkv[cols, ATT:]))
        dn[:, cols] = gained
        both = rsum[OWN, cols] * gained
        product = product + both[:, :SIZE] + both[:, SIZE:]
    average = jnp.sum(product, axis=-1, keepdims=True) * (1.0 / MODEL)
    inverse = inv_b[OWN, :]
    factor = inverse * inverse * inverse * average
    inverse = jnp.concatenate([inverse] * 2, axis=1)
    factor = jnp.concatenate([factor] * 2, axis=1)
    for n in range(MODEL // TILE):
        cols = tile_cols(n)
        gr_v[:, cols] = (inverse * dn[:, cols] - rsum[OWN, cols] * factor).astype(BF16)
    gr_store = pltpu.make_async_copy(gr_v, gr_hbm.at[0], store_sem.at[1])
    gr_store.start()

    def back_out(ch):
        cols = tile_cols(ch)
        d_rows = (dot_nt(gr_v[...], wo[cols, :]) * itot[:, cols]).astype(BF16)
        dw[OWN, cols] = d_rows
        product = out_f[:, cols] * d_rows.astype(F32)
        high = product.astype(BF16)
        low = (product - high.astype(F32)).astype(BF16)
        ones = jnp.ones((8, SIZE), BF16)
        kept = lax.broadcasted_iota(jnp.int32, (8, SIZE), 0)
        for part in range(PER):
            cut = slice(part * SIZE, (part + 1) * SIZE)
            here = head_cols(ch * PER + part)
            total = jnp.sum(product[:, cut], axis=-1, keepdims=True)
            dcol[:, here] = jnp.broadcast_to(total, (ROWS, SIZE))
            line = dot_nt(ones, high[:, cut]) + dot_nt(ones, low[:, cut])
            top = line.astype(BF16).astype(F32)
            dl[16:24, here] = jnp.where(
                kept == 0, top, jnp.where(kept == 1, line - top, 0.0)
            ).astype(BF16)
        for n in range(3):
            for kind in range(2):
                d_copy(kind, ch, n).start()

    loop(CHUNKS, back_out)

    def query_side(ch):
        for part in range(PER):
            h = ch * PER + part
            cols = head_cols(h)
            dprobs = dot_nt(dw[OWN, cols], vw[:, cols])
            dscores = e_w[h].astype(F32) * (dprobs - dcol[:, cols][:, :1])
            grads = dot(dscores.astype(BF16), kw[:, cols]) * SCALE
            inverse = rq_b[:, cols]
            normed = qraw[:, cols].astype(F32) * inverse
            gq_v[:, cols] = (inverse * (grads - normed * lane_mean(normed * grads))).astype(BF16)
        for kind in range(2):
            d_arrive(kind, ch, relay_from)
            d_pass(kind, ch).start()

    loop(CHUNKS, query_side)
    gq_store = pltpu.make_async_copy(gq_v, gq_hbm.at[0], store_sem.at[2])
    gq_store.start()

    def key_grads(ch):
        for slot in rest:
            for kind in range(2):
                d_arrive(kind, ch, slot)
        for part in range(PER):
            h = ch * PER + part
            cols = head_cols(h)
            d_rows = dw[:, cols]
            lines = []
            for slot in range(SLOTS):
                line = dl[slot * 8 : (slot + 1) * 8, cols].astype(F32)
                lines.append(line[0:1] + line[1:2])
            weights = et_w[h]
            dprobs = dot_nt(vw[OWN, cols], d_rows)
            dscores = weights.astype(F32) * (dprobs - jnp.concatenate(lines, axis=1))
            grads = dot(dscores.astype(BF16), qw[:, cols]) * LN2
            inverse = rk_b[:, cols]
            normed = kraw[:, cols].astype(F32) * inverse
            gk_v[:, cols] = (inverse * (grads - normed * lane_mean(normed * grads))).astype(BF16)
            gv_v[:, cols] = dot(weights, d_rows).astype(BF16)

    loop(CHUNKS, key_grads)
    gk_store = pltpu.make_async_copy(gk_v, gk_hbm.at[0], store_sem.at[3])
    gv_store = pltpu.make_async_copy(gv_v, gv_hbm.at[0], store_sem.at[4])
    gk_store.start()
    gv_store.start()

    for ch in range(CHUNKS):
        for kind in range(2):
            for n in range(3):
                kv_copy(kind, ch, n).wait_send()
                d_copy(kind, ch, n).wait_send()
            kv_pass(kind, ch).wait_send()
            d_pass(kind, ch).wait_send()
        for n in range(2):
            out_copy(ch, n).wait_send()
    for n in range(3):
        q_copy(n).wait_send()
    q_pass().wait_send()
    for n in range(2):
        resid_copy(n).wait_send()
        grad_copy(0, n).wait_send()
        grad_copy(1, n).wait_send()
        pack_copy(n).wait_send()
    for copy in (so_store, gr_store, gq_store, gk_store, gv_store):
        copy.wait()


def hand_over(*refs):
    sems = refs[-1]
    count = (len(refs) - 1) // 2
    copies = [
        pltpu.make_async_copy(refs[n], refs[count + n], sems.at[n]) for n in range(count)
    ]
    for copy in copies:
        copy.start()
    for copy in copies:
        copy.wait()


def shards(tm_count, site_count, q_time, k_time, v_time, resid, w_out_time, norm_gain, w_qkv_site, grad_site, nbr_blocks):
    assert q_time.shape == (1, ROWS, ATT) and resid.shape == (1, ROWS, MODEL)
    anywhere = pl.BlockSpec(memory_space=pl.ANY)
    narrow = jax.ShapeDtypeStruct((1, ROWS, ATT), BF16)
    wide = jax.ShapeDtypeStruct((1, ROWS, MODEL), BF16)
    vmem = pltpu.VMEM
    dma = pltpu.SemaphoreType.DMA
    results = pl.pallas_call(
        functools.partial(kernel, tm_count, site_count),
        out_shape=(narrow, narrow, narrow, narrow, wide),
        in_specs=[
            pl.BlockSpec(memory_space=pltpu.SMEM),
            pl.BlockSpec(memory_space=pltpu.VMEM),
        ]
        + [anywhere] * 7,
        out_specs=(anywhere,) * 5,
        scratch_shapes=[
            vmem((ROWS, ATT), BF16),
            vmem((ROWS, ATT), BF16),
            vmem((WINDOW, ATT), BF16),
            vmem((WINDOW, ATT), BF16),
            vmem((WINDOW, ATT), BF16),
            vmem((WINDOW, ATT), BF16),
            vmem((SLOTS * 8, ATT), BF16),
            vmem((ROWS, WINDOW), F32),
            vmem((ROWS, ATT), F32),
            vmem((ROWS, ATT), F32),
            vmem((ROWS, ATT), F32),
            vmem((ROWS, ATT), F32),
            vmem((ROWS, ATT), F32),
            vmem((HEADS, ROWS, WINDOW), BF16),
            vmem((HEADS, ROWS, WINDOW), BF16),
            vmem((3 * ROWS, ATT), BF16),
            vmem((3 * ROWS, MODEL), BF16),
            vmem((3 * ROWS, ATT), BF16),
            vmem((ATT, MODEL), BF16),
            vmem((MODEL, 3 * ATT), BF16),
            vmem((3 * ROWS, MODEL), F32),
            vmem((3 * ROWS, SIZE), F32),
            vmem((3 * ROWS, MODEL), BF16),
            vmem((3 * ROWS, ATT), F32),
            vmem((3 * ROWS, 2 * ATT), BF16),
            vmem((SIZE, 3 * ATT), BF16),
            vmem((2 * ROWS, SIZE), BF16),
            vmem((2 * ROWS, SIZE), BF16),
            vmem((ROWS, ATT), BF16),
            vmem((ROWS, ATT), F32),
            vmem((ROWS, ATT), F32),
            vmem((ROWS, ATT), F32),
            vmem((ROWS, 2 * ATT), BF16),
            vmem((ROWS, MODEL), F32),
            vmem((ROWS, ATT), BF16),
            vmem((ROWS, ATT), BF16),
            vmem((ROWS, ATT), BF16),
            vmem((ROWS, ATT), BF16),
            vmem((ROWS, MODEL), BF16),
            dma((7,)),
            dma((5,)),
            dma((2, CHUNKS, 3)),
            dma((2, CHUNKS, SLOTS)),
            dma((2, CHUNKS)),
            dma((3,)),
            dma((SLOTS,)),
            dma((1,)),
            dma((2,)),
            dma((2,)),
            dma((2, 2)),
            dma((2, 2)),
            dma((CHUNKS, 2)),
            dma((CHUNKS, 2)),
            dma((2,)),
            dma((2,)),
            dma((2, CHUNKS, 3)),
            dma((2, CHUNKS, SLOTS)),
            dma((2, CHUNKS)),
        ],
        compiler_params=pltpu.CompilerParams(
            collective_id=0, has_side_effects=True, vmem_limit_bytes=56 * 1024 * 1024
        ),
    )(
        nbr_blocks,
        norm_gain,
        q_time,
        k_time,
        v_time,
        resid,
        w_out_time,
        w_qkv_site,
        grad_site,
    )
    return pl.pallas_call(
        hand_over,
        out_shape=(narrow, narrow, narrow, narrow, wide),
        in_specs=[anywhere] * 5,
        out_specs=(anywhere,) * 5,
        scratch_shapes=[dma((5,))],
    )(*results)


def solution(mesh):
    rows = P("site", "tm", None)
    return jax.shard_map(
        functools.partial(shards, mesh.shape["tm"], mesh.shape["site"]),
        mesh=mesh,
        in_specs=(rows, rows, rows, rows, P(), P(), P(), rows, P("site", None)),
        out_specs=(rows,) * 5,
        check_vma=False,
    )
```

```python
import functools

import jax
import jax.numpy as jnp
from jax import lax
from jax.experimental import pallas as pl
from jax.experimental.pallas import tpu as pltpu
from jax.sharding import PartitionSpec as P

HEADS = 6
SIZE = 128
ROWS = 128
ATT = HEADS * SIZE
MODEL = 1536
EPSILON = 1e-05
SCALE = SIZE ** (-0.5)
LOG2E = 1.4426950408889634
LN2 = 0.6931471805599453
SLOTS = 5
WINDOW = SLOTS * ROWS
CHUNKS = 3
WIDTH = ATT // CHUNKS
PER = HEADS // CHUNKS
TILE = 256
BLOCK = 32
F32 = jnp.float32
BF16 = jnp.bfloat16
MESH = pl.DeviceIdType.MESH
OWN = slice(2 * ROWS, 3 * ROWS)


def dot(a, b):
    return jnp.dot(a, b, preferred_element_type=F32)


def dot_nt(a, b):
    return lax.dot_general(a, b, (((1,), (1,)), ((), ())), preferred_element_type=F32)


def lane_mean(x):
    return jnp.sum(x, axis=-1, keepdims=True) * (1.0 / x.shape[-1])


def head_cols(h, base=0):
    return slice(h * SIZE + base, (h + 1) * SIZE + base)


def tile_cols(n, base=0):
    return slice(n * TILE + base, (n + 1) * TILE + base)


def loop(count, body):
    for i in range(count):
        body(i)


def kernel(
    tm_count,
    site_count,
    nbr_ref,
    gain_ref,
    q_hbm,
    k_hbm,
    v_hbm,
    resid_hbm,
    wo_hbm,
    wqkv_hbm,
    grad_hbm,
    so_hbm,
    gq_hbm,
    gk_hbm,
    gv_hbm,
    gr_hbm,
    qraw,
    kraw,
    qw,
    kw,
    vw,
    dw,
    dl,
    mask,
    rq_b,
    rk_b,
    itot,
    out_f,
    dcol,
    e_w,
    et_w,
    ow,
    rw,
    gw,
    wo,
    wqkv,
    rsum,
    inv_b,
    nb,
    qf,
    kvb,
    pick,
    pkb,
    prb,
    dqb,
    dkbase,
    dvbase,
    rko,
    dkv,
    dn,
    so_v,
    gq_v,
    gk_v,
    gv_v,
    gr_v,
    load_sem,
    store_sem,
    kv_send,
    kv_recv,
    kv_relay,
    q_send,
    q_recv,
    q_relay,
    r_send,
    r_recv,
    g_send,
    g_recv,
    o_send,
    o_recv,
    p_send,
    p_recv,
    d_send,
    d_recv,
    d_relay,
):
    tm = lax.axis_index("tm")
    st = lax.axis_index("site")
    core = lax.rem(tm, 2)
    sib = tm + 1 - 2 * core
    right_chip = lax.rem(tm + 2 - core, tm_count)
    left_chip = lax.rem(tm - 1 - core + tm_count, tm_count)
    up = lax.rem(st + 1, site_count)
    down = lax.rem(st + site_count - 1, site_count)
    time_dests = ((right_chip, core), (left_chip, 3 + core), (sib, 1 + 2 * core))
    relay_from = 1 + 2 * core
    relay_to = 4 * core
    rest = (4 * core, 3 - 2 * core, 4 - 4 * core)

    loads = [
        pltpu.make_async_copy(src, dst, load_sem.at[n])
        for n, (src, dst) in enumerate(
            (
                (k_hbm.at[0], kraw),
                (q_hbm.at[0], qraw),
                (v_hbm.at[0], vw.at[OWN]),
                (resid_hbm.at[0], rw.at[OWN]),
                (grad_hbm.at[0], gw.at[OWN]),
                (wo_hbm, wo),
                (wqkv_hbm, wqkv),
            )
        )
    ]
    for copy in loads:
        copy.start()

    barrier = pltpu.get_barrier_semaphore()
    for offset in (1, 2, tm_count - 1, tm_count - 2):
        pl.semaphore_signal(
            barrier, inc=1, device_id={"tm": lax.rem(tm + offset, tm_count)}, device_id_type=MESH
        )
    for peer in (up, down):
        pl.semaphore_signal(barrier, inc=1, device_id={"site": peer}, device_id_type=MESH)

    row = lax.broadcasted_iota(jnp.int32, (ROWS, ROWS), 0)
    lane = lax.broadcasted_iota(jnp.int32, (ROWS, ROWS), 1)
    for slot in range(SLOTS):
        shard = tm + slot - 2
        valid = jnp.where((shard >= 0) & (shard < tm_count), 1.0, 0.0).astype(F32)
        if slot == 0:
            band = jnp.where(lane >= row, valid, 0.0)
        elif slot == SLOTS - 1:
            band = jnp.where(lane <= row, valid, 0.0)
        else:
            band = jnp.full((ROWS, ROWS), valid, F32)
        mask[:, slot * ROWS : (slot + 1) * ROWS] = band

    for h in range(HEADS):
        for n in range(3):
            pick[:, head_cols(3 * h + n)] = jnp.where(row == 8 * n + h, 1.0, 0.0).astype(BF16)

    def normalise(raw, store, inverse, factor):
        def body(h):
            cols = head_cols(h)
            x = raw[:, cols].astype(F32)
            r = lax.rsqrt(lane_mean(x * x) + EPSILON)
            inverse[:, cols] = jnp.broadcast_to(r, (ROWS, SIZE))
            store[OWN, cols] = (x * (r * factor)).astype(BF16)

        loop(HEADS, body)

    def remote(src, dst, send, recv, device):
        return pltpu.make_async_remote_copy(
            src_ref=src,
            dst_ref=dst,
            send_sem=send,
            recv_sem=recv,
            device_id=device,
            device_id_type=MESH,
        )

    def slot_rows(slot, size=ROWS):
        return pl.ds(pl.multiple_of(slot * size, size), size)

    def kv_copy(kind, ch, n):
        device, slot = time_dests[n]
        cols = tile_cols(ch)
        src = kw.at[OWN, cols] if kind == 0 else v_hbm.at[0, :, cols]
        dst = (kw if kind == 0 else vw).at[slot_rows(slot), cols]
        return remote(
            src, dst, kv_send.at[kind, ch, n], kv_recv.at[kind, ch, slot], {"tm": device}
        )

    def kv_pass(kind, ch):
        cols = tile_cols(ch)
        buffer = kw if kind == 0 else vw
        return remote(
            buffer.at[slot_rows(relay_from), cols],
            buffer.at[slot_rows(relay_to), cols],
            kv_relay.at[kind, ch],
            kv_recv.at[kind, ch, relay_to],
            {"tm": sib},
        )

    def kv_arrive(kind, ch, slot):
        cols = tile_cols(ch)
        here = (kw if kind == 0 else vw).at[slot_rows(slot), cols]
        remote(here, here, kv_relay.at[kind, ch], kv_recv.at[kind, ch, slot], {"tm": sib}).wait_recv()

    def q_copy(n):
        device, slot = time_dests[n]
        return remote(
            qw.at[OWN], qw.at[slot_rows(slot)], q_send.at[n], q_recv.at[slot], {"tm": device}
        )

    def q_pass():
        return remote(
            qw.at[slot_rows(relay_from)],
            qw.at[slot_rows(relay_to)],
            q_relay.at[0],
            q_recv.at[relay_to],
            {"tm": sib},
        )

    def q_arrive(slot):
        here = qw.at[slot_rows(slot)]
        remote(here, here, q_relay.at[0], q_recv.at[slot], {"tm": sib}).wait_recv()

    def site_copy(n, src, dst, send, recv):
        return remote(
            src, dst.at[n * ROWS : (n + 1) * ROWS], send, recv, {"site": (up, down)[n]}
        )

    def out_copy(ch, n):
        cols = tile_cols(ch)
        return remote(
            ow.at[OWN, cols],
            ow.at[n * ROWS : (n + 1) * ROWS, cols],
            o_send.at[ch, n],
            o_recv.at[ch, n],
            {"site": (up, down)[n]},
        )

    def resid_copy(n):
        return site_copy(n, resid_hbm.at[0], rw, r_send.at[n], r_recv.at[n])

    def grad_copy(half, n):
        cols = slice(half * (ATT // 2), (half + 1) * (ATT // 2))
        return remote(
            grad_hbm.at[0, :, cols],
            gw.at[n * ROWS : (n + 1) * ROWS, cols],
            g_send.at[half, n],
            g_recv.at[half, n],
            {"site": (up, down)[n]},
        )

    def pack_copy(n):
        return site_copy(n, pkb.at[n * ROWS : (n + 1) * ROWS], prb, p_send.at[n], p_recv.at[n])

    def d_copy(kind, ch, n):
        device, slot = time_dests[n]
        cols = tile_cols(ch)
        buffer, size = ((dw, ROWS), (dl, 8))[kind]
        return remote(
            buffer.at[2 * size : 3 * size, cols],
            buffer.at[slot_rows(slot, size), cols],
            d_send.at[kind, ch, n],
            d_recv.at[kind, ch, slot],
            {"tm": device},
        )

    def d_pass(kind, ch):
        cols = tile_cols(ch)
        buffer, size = ((dw, ROWS), (dl, 8))[kind]
        return remote(
            buffer.at[slot_rows(relay_from, size), cols],
            buffer.at[slot_rows(relay_to, size), cols],
            d_relay.at[kind, ch],
            d_recv.at[kind, ch, relay_to],
            {"tm": sib},
        )

    def d_arrive(kind, ch, slot):
        cols = tile_cols(ch)
        buffer, size = ((dw, ROWS), (dl, 8))[kind]
        here = buffer.at[slot_rows(slot, size), cols]
        remote(here, here, d_relay.at[kind, ch], d_recv.at[kind, ch, slot], {"tm": sib}).wait_recv()

    pl.semaphore_wait(barrier, 6)
    for n in range(3):
        kv_copy(1, 0, n).start()
    for n in range(2):
        resid_copy(n).start()
    loads[0].wait()
    normalise(kraw, kw, rk_b, 1.0)
    for ch in range(CHUNKS):
        for kind in range(2) if ch == 0 else (1, 0):
            if (kind, ch) != (1, 0):
                for n in range(3):
                    kv_copy(kind, ch, n).start()
    for n in range(3):
        if n == 0:
            loads[1].wait()
            normalise(qraw, qw, rq_b, SCALE * LOG2E)
        q_copy(n).start()
    loads[2].wait()
    loads[3].wait()
    loads[5].wait()

    def project_out(ch, first, count):
        rows = slice(first, first + count)
        squares = 0.0
        for n in range(MODEL // TILE):
            cols = tile_cols(n)
            before = rw[rows, cols].astype(F32) if ch == 0 else rsum[rows, cols]
            x = before + dot(ow[rows, tile_cols(ch)], wo[tile_cols(ch), cols])
            rsum[rows, cols] = x
            if ch == CHUNKS - 1:
                nb[rows, cols] = (x * gain_ref[cols][None, :]).astype(BF16)
                squares = squares + x[:, :SIZE] * x[:, :SIZE] + x[:, SIZE:] * x[:, SIZE:]
        if ch == CHUNKS - 1:
            mean = jnp.sum(squares, axis=-1, keepdims=True) * (1.0 / MODEL)
            inv_b[rows, :] = jnp.broadcast_to(lax.rsqrt(mean + EPSILON), (count, SIZE))

    def forward(ch):
        for kind in (1, 0):
            kv_arrive(kind, ch, relay_from)
            kv_pass(kind, ch).start()
        for slot in rest:
            for kind in range(2):
                kv_arrive(kind, ch, slot)
        for part in range(PER):
            h = ch * PER + part
            cols = head_cols(h)
            weights = (
                jnp.exp2(dot_nt(qw[OWN, cols], kw[:, cols])) * mask[...]
            ).astype(BF16)
            e_w[h] = weights
            inverse = 1.0 / jnp.sum(weights.astype(F32), axis=-1, keepdims=True)
            heads_out = dot(weights, vw[:, cols]) * inverse
            itot[:, cols] = jnp.broadcast_to(inverse, (ROWS, SIZE))
            out_f[:, cols] = heads_out
            ow[OWN, cols] = heads_out.astype(BF16)
        for n in range(2):
            out_copy(ch, n).start()
        project_out(ch, 2 * ROWS, ROWS)

    loop(CHUNKS, forward)
    for n in range(2):
        grad_copy(0, n).start()

    def project_q(first, count):
        rows = slice(first, first + count)

        def body(n):
            inverse = jnp.concatenate([inv_b[rows, :]] * 2, axis=1)
            qf[rows, tile_cols(n)] = dot(nb[rows, :], wqkv[:, tile_cols(n)]) * inverse

        loop(ATT // TILE, body)

    def project_kv(first, count):
        rows = slice(first, first + count)

        def body(n):
            inverse = jnp.concatenate([inv_b[rows, :]] * 2, axis=1)
            product = dot(nb[rows, :], wqkv[:, tile_cols(n, ATT)])
            kvb[rows, tile_cols(n)] = (product * inverse).astype(BF16)

        loop(2 * ATT // TILE, body)

    loads[6].wait()
    project_q(2 * ROWS, ROWS)
    project_kv(2 * ROWS, ROWS)
    loads[4].wait()

    first_named, second_named = nbr_ref[0, 0], nbr_ref[0, 1]
    seen = [
        jnp.where((first_named == peer) | (second_named == peer), 1.0, 0.0).astype(F32)
        for peer in (st - 1, st + 1)
    ]

    def site_key(h, x):
        return kvb[x * ROWS : (x + 1) * ROWS, head_cols(h)].astype(F32)

    def site_value(h, x):
        return kvb[x * ROWS : (x + 1) * ROWS, head_cols(h, ATT)].astype(F32)

    def site_scores(h, x):
        key = site_key(h, x)
        k_inv = lax.rsqrt(lane_mean(key * key) + EPSILON)
        score = jnp.sum(qf[OWN, head_cols(h)] * key, axis=-1, keepdims=True)
        grad = gw[OWN, head_cols(h)].astype(F32)
        dprob = jnp.sum(grad * site_value(h, x), axis=-1, keepdims=True)
        return k_inv, score, dprob

    own_stats = []
    for h in range(HEADS):
        q = qf[OWN, head_cols(h)]
        q_inv = lax.rsqrt(lane_mean(q * q) + EPSILON)
        own_stats.append((q_inv, site_scores(h, 2)))

    q_arrive(relay_from)
    q_pass().start()

    for n in range(2):
        resid_copy(n).wait_recv()
    for ch in range(CHUNKS):
        for n in range(2):
            out_copy(ch, n).wait_recv()
        project_out(ch, 0, 2 * ROWS)
    project_kv(0, 2 * ROWS)

    site_stats = []
    packs = [jnp.zeros((ROWS, SIZE), F32) for _ in range(2)]
    for h in range(HEADS):
        q_inv, own = own_stats[h]
        k_inv, scores, dprobs = zip(site_scores(h, 0), site_scores(h, 1), own)
        scores = [s * (q_inv * r * SCALE) for s, r in zip(scores, k_inv)]
        exps = [jnp.exp(s) for s in scores]
        exps = [exps[0] * seen[0], exps[1] * seen[1], exps[2]]
        inverse = 1.0 / (exps[0] + exps[1] + exps[2])
        probs = [e * inverse for e in exps]
        rounded = [p.astype(BF16).astype(F32) for p in probs]
        delta = probs[0] * dprobs[0] + probs[1] * dprobs[1] + probs[2] * dprobs[2]
        dscores = [p * (d - delta) for p, d in zip(probs, dprobs)]
        along = [d * s for d, s in zip(dscores, scores)]
        scaled = [d * (q_inv * SCALE) for d in dscores]
        for n in range(2):
            x = 1 - n
            for place, value in enumerate((scaled[x], along[x], rounded[x])):
                packs[n] = jnp.where(lane == h + 8 * place, value, packs[n])
        site_stats.append((q_inv, k_inv, rounded, along, scaled))
    for n in range(2):
        pkb[n * ROWS : (n + 1) * ROWS, :] = packs[n].astype(BF16)
        pack_copy(n).start()
    for n in range(2):
        grad_copy(1, n).start()

    def site_head(h):
        cols = head_cols(h)
        q_inv, k_inv, rounded, along, scaled = site_stats[h]
        q = qf[OWN, cols]
        keys = [site_key(h, x) for x in range(3)]
        values = [site_value(h, x) for x in range(3)]
        dq = (
            scaled[0] * k_inv[0] * keys[0]
            + scaled[1] * k_inv[1] * keys[1]
            + scaled[2] * k_inv[2] * keys[2]
            - q * (q_inv * q_inv * (along[0] + along[1] + along[2]) * (1.0 / SIZE))
        )
        dqb[:, cols] = dq.astype(BF16)
        so_v[:, cols] = (
            rounded[0] * values[0] + rounded[1] * values[1] + rounded[2] * values[2]
        ).astype(BF16)
        dkbase[:, cols] = (scaled[2] * k_inv[2]) * q - (
            k_inv[2] * k_inv[2] * along[2] * (1.0 / SIZE)
        ) * keys[2]
        dvbase[:, cols] = rounded[2] * gw[OWN, cols].astype(F32)
        rko[:, cols] = jnp.broadcast_to(k_inv[2], (ROWS, SIZE))

    loop(HEADS, site_head)
    so_store = pltpu.make_async_copy(so_v, so_hbm.at[0], store_sem.at[0])
    so_store.start()

    def back_q(n):
        dn[:, tile_cols(n)] = dot_nt(dqb[...], wqkv[tile_cols(n), :ATT])

    loop(MODEL // TILE, back_q)
    project_q(0, 2 * ROWS)

    for slot in rest:
        q_arrive(slot)

    def key_side(h):
        cols = head_cols(h)
        et_w[h] = (jnp.exp2(dot_nt(kw[OWN, cols], qw[:, cols])) * mask[...]).astype(BF16)

    loop(HEADS, key_side)

    for n in range(2):
        pack_copy(n).wait_recv()

    def site_keys(h):
        cols = head_cols(h)
        if h % (HEADS // 2) == 0:
            for n in range(2):
                grad_copy(h // (HEADS // 2), n).wait_recv()
        spread = dot(prb[...], pick[:, 3 * h * SIZE : 3 * (h + 1) * SIZE])
        inverse = rko[:, cols]
        dkey, dvalue, along = dkbase[:, cols], dvbase[:, cols], 0.0
        gathered = 0.0
        for x in range(2):
            rows = slice(x * ROWS, (x + 1) * ROWS)
            gathered = gathered + spread[rows, :SIZE] * qf[rows, cols]
            along = along + spread[rows, SIZE : 2 * SIZE]
            dvalue = dvalue + spread[rows, 2 * SIZE :] * gw[rows, cols].astype(F32)
        own_key = kvb[OWN, cols].astype(F32)
        dkey = dkey + inverse * gathered - inverse * inverse * (1.0 / SIZE) * along * own_key
        dkv[:, cols] = dkey.astype(BF16)
        dkv[:, head_cols(h, ATT)] = dvalue.astype(BF16)

    loop(HEADS, site_keys)

    product = 0.0
    for n in range(MODEL // TILE):
        cols = tile_cols(n)
        gained = gain_ref[cols][None, :] * (dn[:, cols] + dot_nt(dkv[...], wqkv[cols, ATT:]))
        dn[:, cols] = gained
        both = rsum[OWN, cols] * gained
        product = product + both[:, :SIZE] + both[:, SIZE:]
    average = jnp.sum(product, axis=-1, keepdims=True) * (1.0 / MODEL)
    inverse = inv_b[OWN, :]
    factor = inverse * inverse * inverse * average
    inverse = jnp.concatenate([inverse] * 2, axis=1)
    factor = jnp.concatenate([factor] * 2, axis=1)
    for n in range(MODEL // TILE):
        cols = tile_cols(n)
        gr_v[:, cols] = (inverse * dn[:, cols] - rsum[OWN, cols] * factor).astype(BF16)
    gr_store = pltpu.make_async_copy(gr_v, gr_hbm.at[0], store_sem.at[1])
    gr_store.start()

    def back_out(ch):
        cols = tile_cols(ch)
        d_rows = (dot_nt(gr_v[...], wo[cols, :]) * itot[:, cols]).astype(BF16)
        dw[OWN, cols] = d_rows
        product = out_f[:, cols] * d_rows.astype(F32)
        high = product.astype(BF16)
        low = (product - high.astype(F32)).astype(BF16)
        ones = jnp.ones((8, SIZE), BF16)
        kept = lax.broadcasted_iota(jnp.int32, (8, SIZE), 0)
        for part in range(PER):
            cut = slice(part * SIZE, (part + 1) * SIZE)
            here = head_cols(ch * PER + part)
            total = jnp.sum(product[:, cut], axis=-1, keepdims=True)
            dcol[:, here] = jnp.broadcast_to(total, (ROWS, SIZE))
            line = dot_nt(ones, high[:, cut]) + dot_nt(ones, low[:, cut])
            top = line.astype(BF16).astype(F32)
            dl[16:24, here] = jnp.where(
                kept == 0, top, jnp.where(kept == 1, line - top, 0.0)
            ).astype(BF16)
        for n in range(3):
            for kind in range(2):
                d_copy(kind, ch, n).start()

    loop(CHUNKS, back_out)

    def query_side(ch):
        for part in range(PER):
            h = ch * PER + part
            cols = head_cols(h)
            dprobs = dot_nt(dw[OWN, cols], vw[:, cols])
            dscores = e_w[h].astype(F32) * (dprobs - dcol[:, cols][:, :1])
            grads = dot(dscores.astype(BF16), kw[:, cols]) * SCALE
            inverse = rq_b[:, cols]
            normed = qraw[:, cols].astype(F32) * inverse
            gq_v[:, cols] = (inverse * (grads - normed * lane_mean(normed * grads))).astype(BF16)
        for kind in range(2):
            d_arrive(kind, ch, relay_from)
            d_pass(kind, ch).start()

    loop(CHUNKS, query_side)
    gq_store = pltpu.make_async_copy(gq_v, gq_hbm.at[0], store_sem.at[2])
    gq_store.start()

    def key_grads(ch):
        for slot in rest:
            for kind in range(2):
                d_arrive(kind, ch, slot)
        for part in range(PER):
            h = ch * PER + part
            cols = head_cols(h)
            d_rows = dw[:, cols]
            lines = []
            for slot in range(SLOTS):
                line = dl[slot * 8 : (slot + 1) * 8, cols].astype(F32)
                lines.append(line[0:1] + line[1:2])
            weights = et_w[h]
            dprobs = dot_nt(vw[OWN, cols], d_rows)
            dscores = weights.astype(F32) * (dprobs - jnp.concatenate(lines, axis=1))
            grads = dot(dscores.astype(BF16), qw[:, cols]) * LN2
            inverse = rk_b[:, cols]
            normed = kraw[:, cols].astype(F32) * inverse
            gk_v[:, cols] = (inverse * (grads - normed * lane_mean(normed * grads))).astype(BF16)
            gv_v[:, cols] = dot(weights, d_rows).astype(BF16)

    loop(CHUNKS, key_grads)
    gk_store = pltpu.make_async_copy(gk_v, gk_hbm.at[0], store_sem.at[3])
    gv_store = pltpu.make_async_copy(gv_v, gv_hbm.at[0], store_sem.at[4])
    gk_store.start()
    gv_store.start()

    for ch in range(CHUNKS):
        for kind in range(2):
            for n in range(3):
                kv_copy(kind, ch, n).wait_send()
                d_copy(kind, ch, n).wait_send()
            kv_pass(kind, ch).wait_send()
            d_pass(kind, ch).wait_send()
        for n in range(2):
            out_copy(ch, n).wait_send()
    for n in range(3):
        q_copy(n).wait_send()
    q_pass().wait_send()
    for n in range(2):
        resid_copy(n).wait_send()
        grad_copy(0, n).wait_send()
        grad_copy(1, n).wait_send()
        pack_copy(n).wait_send()
    for copy in (so_store, gr_store, gq_store, gk_store, gv_store):
        copy.wait()


def hand_over(*refs):
    count = len(refs) // 3
    sems = refs[-1]
    taken = [
        pltpu.make_async_copy(refs[n], refs[2 * count + n], sems.at[0, n]) for n in range(count)
    ]
    given = [
        pltpu.make_async_copy(refs[2 * count + n], refs[count + n], sems.at[1, n])
        for n in range(count)
    ]
    for copy in taken:
        copy.start()
    for n in range(count):
        taken[n].wait()
        given[n].start()
    for copy in given:
        copy.wait()


def shards(tm_count, site_count, q_time, k_time, v_time, resid, w_out_time, norm_gain, w_qkv_site, grad_site, nbr_blocks):
    assert q_time.shape == (1, ROWS, ATT) and resid.shape == (1, ROWS, MODEL)
    anywhere = pl.BlockSpec(memory_space=pl.ANY)
    narrow = jax.ShapeDtypeStruct((1, ROWS, ATT), BF16)
    wide = jax.ShapeDtypeStruct((1, ROWS, MODEL), BF16)
    vmem = pltpu.VMEM
    dma = pltpu.SemaphoreType.DMA
    results = pl.pallas_call(
        functools.partial(kernel, tm_count, site_count),
        out_shape=(narrow, narrow, narrow, narrow, wide),
        in_specs=[
            pl.BlockSpec(memory_space=pltpu.SMEM),
            pl.BlockSpec(memory_space=pltpu.VMEM),
        ]
        + [anywhere] * 7,
        out_specs=(anywhere,) * 5,
        scratch_shapes=[
            vmem((ROWS, ATT), BF16),
            vmem((ROWS, ATT), BF16),
            vmem((WINDOW, ATT), BF16),
            vmem((WINDOW, ATT), BF16),
            vmem((WINDOW, ATT), BF16),
            vmem((WINDOW, ATT), BF16),
            vmem((SLOTS * 8, ATT), BF16),
            vmem((ROWS, WINDOW), F32),
            vmem((ROWS, ATT), F32),
            vmem((ROWS, ATT), F32),
            vmem((ROWS, ATT), F32),
            vmem((ROWS, ATT), F32),
            vmem((ROWS, ATT), F32),
            vmem((HEADS, ROWS, WINDOW), BF16),
            vmem((HEADS, ROWS, WINDOW), BF16),
            vmem((3 * ROWS, ATT), BF16),
            vmem((3 * ROWS, MODEL), BF16),
            vmem((3 * ROWS, ATT), BF16),
            vmem((ATT, MODEL), BF16),
            vmem((MODEL, 3 * ATT), BF16),
            vmem((3 * ROWS, MODEL), F32),
            vmem((3 * ROWS, SIZE), F32),
            vmem((3 * ROWS, MODEL), BF16),
            vmem((3 * ROWS, ATT), F32),
            vmem((3 * ROWS, 2 * ATT), BF16),
            vmem((SIZE, 3 * ATT), BF16),
            vmem((2 * ROWS, SIZE), BF16),
            vmem((2 * ROWS, SIZE), BF16),
            vmem((ROWS, ATT), BF16),
            vmem((ROWS, ATT), F32),
            vmem((ROWS, ATT), F32),
            vmem((ROWS, ATT), F32),
            vmem((ROWS, 2 * ATT), BF16),
            vmem((ROWS, MODEL), F32),
            vmem((ROWS, ATT), BF16),
            vmem((ROWS, ATT), BF16),
            vmem((ROWS, ATT), BF16),
            vmem((ROWS, ATT), BF16),
            vmem((ROWS, MODEL), BF16),
            dma((7,)),
            dma((5,)),
            dma((2, CHUNKS, 3)),
            dma((2, CHUNKS, SLOTS)),
            dma((2, CHUNKS)),
            dma((3,)),
            dma((SLOTS,)),
            dma((1,)),
            dma((2,)),
            dma((2,)),
            dma((2, 2)),
            dma((2, 2)),
            dma((CHUNKS, 2)),
            dma((CHUNKS, 2)),
            dma((2,)),
            dma((2,)),
            dma((2, CHUNKS, 3)),
            dma((2, CHUNKS, SLOTS)),
            dma((2, CHUNKS)),
        ],
        compiler_params=pltpu.CompilerParams(
            collective_id=0, has_side_effects=True, vmem_limit_bytes=56 * 1024 * 1024
        ),
    )(
        nbr_blocks,
        norm_gain,
        q_time,
        k_time,
        v_time,
        resid,
        w_out_time,
        w_qkv_site,
        grad_site,
    )
    return pl.pallas_call(
        hand_over,
        out_shape=(narrow, narrow, narrow, narrow, wide),
        in_specs=[anywhere] * 5,
        out_specs=(anywhere,) * 5,
        scratch_shapes=[vmem(shape.shape, BF16) for shape in (narrow,) * 4 + (wide,)]
        + [dma((2, 5))],
    )(*results)


def solution(mesh):
    rows = P("site", "tm", None)
    return jax.shard_map(
        functools.partial(shards, mesh.shape["tm"], mesh.shape["site"]),
        mesh=mesh,
        in_specs=(rows, rows, rows, rows, P(), P(), P(), rows, P("site", None)),
        out_specs=(rows,) * 5,
        check_vma=False,
    )
```

```python
import functools

import jax
import jax.numpy as jnp
from jax import lax
from jax.experimental import pallas as pl
from jax.experimental.pallas import tpu as pltpu
from jax.sharding import PartitionSpec as P

HEADS = 6
SIZE = 128
ROWS = 128
ATT = HEADS * SIZE
MODEL = 1536
EPSILON = 1e-05
SCALE = SIZE ** (-0.5)
LOG2E = 1.4426950408889634
LN2 = 0.6931471805599453
SLOTS = 5
WINDOW = SLOTS * ROWS
CHUNKS = 3
WIDTH = ATT // CHUNKS
PER = HEADS // CHUNKS
TILE = 256
BLOCK = 32
F32 = jnp.float32
BF16 = jnp.bfloat16
MESH = pl.DeviceIdType.MESH
OWN = slice(2 * ROWS, 3 * ROWS)


def dot(a, b):
    return jnp.dot(a, b, preferred_element_type=F32)


def dot_nt(a, b):
    return lax.dot_general(a, b, (((1,), (1,)), ((), ())), preferred_element_type=F32)


def lane_mean(x):
    return jnp.sum(x, axis=-1, keepdims=True) * (1.0 / x.shape[-1])


def head_cols(h, base=0):
    return slice(h * SIZE + base, (h + 1) * SIZE + base)


def tile_cols(n, base=0):
    return slice(n * TILE + base, (n + 1) * TILE + base)


def loop(count, body):
    for i in range(count):
        body(i)


def kernel(
    tm_count,
    site_count,
    nbr_hbm,
    gain_hbm,
    q_hbm,
    k_hbm,
    v_hbm,
    resid_hbm,
    wo_hbm,
    wqkv_hbm,
    grad_hbm,
    so_hbm,
    gq_hbm,
    gk_hbm,
    gv_hbm,
    gr_hbm,
    nbr_ref,
    gain_ref,
    qraw,
    kraw,
    qw,
    kw,
    vw,
    dw,
    dl,
    mask,
    rq_b,
    rk_b,
    itot,
    out_f,
    dcol,
    e_w,
    et_w,
    ow,
    rw,
    gw,
    wo,
    wqkv,
    eye,
    wo_t,
    wkv_t,
    rsum,
    inv_b,
    nb,
    qf,
    kvb,
    pick,
    pkb,
    prb,
    dqb,
    dkbase,
    dvbase,
    rko,
    dkv,
    dn,
    so_v,
    gq_v,
    gk_v,
    gv_v,
    gr_v,
    load_sem,
    store_sem,
    kv_send,
    kv_recv,
    kv_relay,
    q_send,
    q_recv,
    q_relay,
    r_send,
    r_recv,
    g_send,
    g_recv,
    o_send,
    o_recv,
    p_send,
    p_recv,
    d_send,
    d_recv,
    d_relay,
):
    tm = lax.axis_index("tm")
    st = lax.axis_index("site")
    core = lax.rem(tm, 2)
    sib = tm + 1 - 2 * core
    right_chip = lax.rem(tm + 2 - core, tm_count)
    left_chip = lax.rem(tm - 1 - core + tm_count, tm_count)
    up = lax.rem(st + 1, site_count)
    down = lax.rem(st + site_count - 1, site_count)
    time_dests = ((right_chip, core), (left_chip, 3 + core), (sib, 1 + 2 * core))
    relay_from = 1 + 2 * core
    relay_to = 4 * core
    rest = (4 * core, 3 - 2 * core, 4 - 4 * core)

    loads = [
        pltpu.make_async_copy(src, dst, load_sem.at[n])
        for n, (src, dst) in enumerate(
            (
                (k_hbm.at[0], kraw),
                (q_hbm.at[0], qraw),
                (v_hbm.at[0], vw.at[OWN]),
                (resid_hbm.at[0], rw.at[OWN]),
                (grad_hbm.at[0], gw.at[OWN]),
                (wo_hbm, wo),
                (wqkv_hbm, wqkv),
                (gain_hbm, gain_ref),
                (nbr_hbm, nbr_ref),
            )
        )
    ]
    for copy in loads:
        copy.start()

    barrier = pltpu.get_barrier_semaphore()
    for offset in (1, 2, tm_count - 1, tm_count - 2):
        pl.semaphore_signal(
            barrier, inc=1, device_id={"tm": lax.rem(tm + offset, tm_count)}, device_id_type=MESH
        )
    for peer in (up, down):
        pl.semaphore_signal(barrier, inc=1, device_id={"site": peer}, device_id_type=MESH)

    row = lax.broadcasted_iota(jnp.int32, (ROWS, ROWS), 0)
    lane = lax.broadcasted_iota(jnp.int32, (ROWS, ROWS), 1)
    for slot in range(SLOTS):
        shard = tm + slot - 2
        valid = jnp.where((shard >= 0) & (shard < tm_count), 1.0, 0.0).astype(F32)
        if slot == 0:
            band = jnp.where(lane >= row, valid, 0.0)
        elif slot == SLOTS - 1:
            band = jnp.where(lane <= row, valid, 0.0)
        else:
            band = jnp.full((ROWS, ROWS), valid, F32)
        mask[:, slot * ROWS : (slot + 1) * ROWS] = band

    for h in range(HEADS):
        for n in range(3):
            pick[:, head_cols(3 * h + n)] = jnp.where(row == 8 * n + h, 1.0, 0.0).astype(BF16)

    def normalise(raw, store, inverse, factor):
        def body(h):
            cols = head_cols(h)
            x = raw[:, cols].astype(F32)
            r = lax.rsqrt(lane_mean(x * x) + EPSILON)
            inverse[:, cols] = jnp.broadcast_to(r, (ROWS, SIZE))
            store[OWN, cols] = (x * (r * factor)).astype(BF16)

        loop(HEADS, body)

    wide_row = lax.broadcasted_iota(jnp.int32, (TILE, TILE), 0)
    wide_lane = lax.broadcasted_iota(jnp.int32, (TILE, TILE), 1)
    eye[...] = jnp.where(wide_row == wide_lane, 1.0, 0.0).astype(BF16)

    def transpose(source, base, target, first, last):
        def body(n, carry):
            rows = pl.ds(pl.multiple_of(n * TILE, TILE), TILE)
            cols = pl.ds(pl.multiple_of(n * TILE + base, TILE), TILE)
            target[rows, :] = dot_nt(eye[...], source[:, cols]).astype(BF16)
            return carry

        lax.fori_loop(first, last, body, 0)

    def remote(src, dst, send, recv, device):
        return pltpu.make_async_remote_copy(
            src_ref=src,
            dst_ref=dst,
            send_sem=send,
            recv_sem=recv,
            device_id=device,
            device_id_type=MESH,
        )

    def slot_rows(slot, size=ROWS):
        return pl.ds(pl.multiple_of(slot * size, size), size)

    def kv_copy(kind, ch, n):
        device, slot = time_dests[n]
        cols = tile_cols(ch)
        src = kw.at[OWN, cols] if kind == 0 else v_hbm.at[0, :, cols]
        dst = (kw if kind == 0 else vw).at[slot_rows(slot), cols]
        return remote(
            src, dst, kv_send.at[kind, ch, n], kv_recv.at[kind, ch, slot], {"tm": device}
        )

    def kv_pass(kind, ch):
        cols = tile_cols(ch)
        buffer = kw if kind == 0 else vw
        return remote(
            buffer.at[slot_rows(relay_from), cols],
            buffer.at[slot_rows(relay_to), cols],
            kv_relay.at[kind, ch],
            kv_recv.at[kind, ch, relay_to],
            {"tm": sib},
        )

    def kv_arrive(kind, ch, slot):
        cols = tile_cols(ch)
        here = (kw if kind == 0 else vw).at[slot_rows(slot), cols]
        remote(here, here, kv_relay.at[kind, ch], kv_recv.at[kind, ch, slot], {"tm": sib}).wait_recv()

    def q_copy(n):
        device, slot = time_dests[n]
        return remote(
            qw.at[OWN], qw.at[slot_rows(slot)], q_send.at[n], q_recv.at[slot], {"tm": device}
        )

    def q_pass():
        return remote(
            qw.at[slot_rows(relay_from)],
            qw.at[slot_rows(relay_to)],
            q_relay.at[0],
            q_recv.at[relay_to],
            {"tm": sib},
        )

    def q_arrive(slot):
        here = qw.at[slot_rows(slot)]
        remote(here, here, q_relay.at[0], q_recv.at[slot], {"tm": sib}).wait_recv()

    def site_copy(n, src, dst, send, recv):
        return remote(
            src, dst.at[n * ROWS : (n + 1) * ROWS], send, recv, {"site": (up, down)[n]}
        )

    def out_copy(ch, n):
        cols = tile_cols(ch)
        return remote(
            ow.at[OWN, cols],
            ow.at[n * ROWS : (n + 1) * ROWS, cols],
            o_send.at[ch, n],
            o_recv.at[ch, n],
            {"site": (up, down)[n]},
        )

    def resid_copy(n):
        return site_copy(n, resid_hbm.at[0], rw, r_send.at[n], r_recv.at[n])

    def grad_copy(n):
        return site_copy(n, grad_hbm.at[0], gw, g_send.at[n], g_recv.at[n])

    def pack_copy(n):
        return site_copy(n, pkb.at[n * ROWS : (n + 1) * ROWS], prb, p_send.at[n], p_recv.at[n])

    def d_copy(kind, ch, n):
        device, slot = time_dests[n]
        cols = tile_cols(ch)
        buffer, size = ((dw, ROWS), (dl, 8))[kind]
        return remote(
            buffer.at[2 * size : 3 * size, cols],
            buffer.at[slot_rows(slot, size), cols],
            d_send.at[kind, ch, n],
            d_recv.at[kind, ch, slot],
            {"tm": device},
        )

    def d_pass(kind, ch):
        cols = tile_cols(ch)
        buffer, size = ((dw, ROWS), (dl, 8))[kind]
        return remote(
            buffer.at[slot_rows(relay_from, size), cols],
            buffer.at[slot_rows(relay_to, size), cols],
            d_relay.at[kind, ch],
            d_recv.at[kind, ch, relay_to],
            {"tm": sib},
        )

    def d_arrive(kind, ch, slot):
        cols = tile_cols(ch)
        buffer, size = ((dw, ROWS), (dl, 8))[kind]
        here = buffer.at[slot_rows(slot, size), cols]
        remote(here, here, d_relay.at[kind, ch], d_recv.at[kind, ch, slot], {"tm": sib}).wait_recv()

    pl.semaphore_wait(barrier, 6)
    for n in range(3):
        kv_copy(1, 0, n).start()
    for n in range(2):
        resid_copy(n).start()
    loads[0].wait()
    normalise(kraw, kw, rk_b, 1.0)
    for ch in range(CHUNKS):
        for kind in range(2) if ch == 0 else (1, 0):
            if (kind, ch) != (1, 0):
                for n in range(3):
                    kv_copy(kind, ch, n).start()
    for n in range(3):
        if n == 0:
            loads[1].wait()
            normalise(qraw, qw, rq_b, SCALE * LOG2E)
        q_copy(n).start()
    loads[2].wait()
    loads[3].wait()
    loads[5].wait()
    loads[7].wait()
    loads[8].wait()
    transpose(wo, 0, wo_t, 0, MODEL // TILE)
    loads[6].wait()

    def project_out(ch, first, count):
        rows = slice(first, first + count)
        squares = 0.0
        for n in range(MODEL // TILE):
            cols = tile_cols(n)
            before = rw[rows, cols].astype(F32) if ch == 0 else rsum[rows, cols]
            x = before + dot(ow[rows, tile_cols(ch)], wo[tile_cols(ch), cols])
            rsum[rows, cols] = x
            if ch == CHUNKS - 1:
                nb[rows, cols] = (x * gain_ref[cols][None, :]).astype(BF16)
                squares = squares + x[:, :SIZE] * x[:, :SIZE] + x[:, SIZE:] * x[:, SIZE:]
        if ch == CHUNKS - 1:
            mean = jnp.sum(squares, axis=-1, keepdims=True) * (1.0 / MODEL)
            inv_b[rows, :] = jnp.broadcast_to(lax.rsqrt(mean + EPSILON), (count, SIZE))

    def forward(ch):
        for kind in (1, 0):
            kv_arrive(kind, ch, relay_from)
            kv_pass(kind, ch).start()
        for slot in rest:
            for kind in range(2):
                kv_arrive(kind, ch, slot)
        for part in range(PER):
            h = ch * PER + part
            cols = head_cols(h)
            weights = (
                jnp.exp2(dot_nt(qw[OWN, cols], kw[:, cols])) * mask[...]
            ).astype(BF16)
            e_w[h] = weights
            inverse = 1.0 / jnp.sum(weights.astype(F32), axis=-1, keepdims=True)
            heads_out = dot(weights, vw[:, cols]) * inverse
            itot[:, cols] = jnp.broadcast_to(inverse, (ROWS, SIZE))
            out_f[:, cols] = heads_out
            ow[OWN, cols] = heads_out.astype(BF16)
        for n in range(2):
            out_copy(ch, n).start()
        project_out(ch, 2 * ROWS, ROWS)
        if ch < CHUNKS - 1:
            transpose(wqkv, ATT, wkv_t, 3 * ch, 3 * ch + 3)

    loop(CHUNKS, forward)
    for n in range(2):
        grad_copy(n).start()

    def project_q(first, count):
        rows = slice(first, first + count)

        def body(n):
            inverse = jnp.concatenate([inv_b[rows, :]] * 2, axis=1)
            qf[rows, tile_cols(n)] = dot(nb[rows, :], wqkv[:, tile_cols(n)]) * inverse

        loop(ATT // TILE, body)

    def project_kv(first, count):
        rows = slice(first, first + count)

        def body(n):
            inverse = jnp.concatenate([inv_b[rows, :]] * 2, axis=1)
            product = dot(nb[rows, :], wqkv[:, tile_cols(n, ATT)])
            kvb[rows, tile_cols(n)] = (product * inverse).astype(BF16)

        loop(2 * ATT // TILE, body)

    project_q(2 * ROWS, ROWS)
    project_kv(2 * ROWS, ROWS)
    loads[4].wait()

    first_named, second_named = nbr_ref[0, 0], nbr_ref[0, 1]
    seen = [
        jnp.where((first_named == peer) | (second_named == peer), 1.0, 0.0).astype(F32)
        for peer in (st - 1, st + 1)
    ]

    def site_key(h, x):
        return kvb[x * ROWS : (x + 1) * ROWS, head_cols(h)].astype(F32)

    def site_value(h, x):
        return kvb[x * ROWS : (x + 1) * ROWS, head_cols(h, ATT)].astype(F32)

    def site_scores(h, x):
        key = site_key(h, x)
        k_inv = lax.rsqrt(lane_mean(key * key) + EPSILON)
        score = jnp.sum(qf[OWN, head_cols(h)] * key, axis=-1, keepdims=True)
        grad = gw[OWN, head_cols(h)].astype(F32)
        dprob = jnp.sum(grad * site_value(h, x), axis=-1, keepdims=True)
        return k_inv, score, dprob

    own_stats = []
    for h in range(HEADS):
        q = qf[OWN, head_cols(h)]
        q_inv = lax.rsqrt(lane_mean(q * q) + EPSILON)
        own_stats.append((q_inv, site_scores(h, 2)))

    q_arrive(relay_from)
    q_pass().start()

    for n in range(2):
        resid_copy(n).wait_recv()
    for ch in range(CHUNKS):
        for n in range(2):
            out_copy(ch, n).wait_recv()
        project_out(ch, 0, 2 * ROWS)
    project_kv(0, 2 * ROWS)

    site_stats = []
    packs = [jnp.zeros((ROWS, SIZE), F32) for _ in range(2)]
    for h in range(HEADS):
        q_inv, own = own_stats[h]
        k_inv, scores, dprobs = zip(site_scores(h, 0), site_scores(h, 1), own)
        scores = [s * (q_inv * r * SCALE) for s, r in zip(scores, k_inv)]
        exps = [jnp.exp(s) for s in scores]
        exps = [exps[0] * seen[0], exps[1] * seen[1], exps[2]]
        inverse = 1.0 / (exps[0] + exps[1] + exps[2])
        probs = [e * inverse for e in exps]
        rounded = [p.astype(BF16).astype(F32) for p in probs]
        delta = probs[0] * dprobs[0] + probs[1] * dprobs[1] + probs[2] * dprobs[2]
        dscores = [p * (d - delta) for p, d in zip(probs, dprobs)]
        along = [d * s for d, s in zip(dscores, scores)]
        scaled = [d * (q_inv * SCALE) for d in dscores]
        for n in range(2):
            x = 1 - n
            for place, value in enumerate((scaled[x], along[x], rounded[x])):
                packs[n] = jnp.where(lane == h + 8 * place, value, packs[n])
        site_stats.append((q_inv, k_inv, rounded, along, scaled))
    for n in range(2):
        pkb[n * ROWS : (n + 1) * ROWS, :] = packs[n].astype(BF16)
        pack_copy(n).start()

    def site_head(h):
        cols = head_cols(h)
        q_inv, k_inv, rounded, along, scaled = site_stats[h]
        q = qf[OWN, cols]
        keys = [site_key(h, x) for x in range(3)]
        values = [site_value(h, x) for x in range(3)]
        dq = (
            scaled[0] * k_inv[0] * keys[0]
            + scaled[1] * k_inv[1] * keys[1]
            + scaled[2] * k_inv[2] * keys[2]
            - q * (q_inv * q_inv * (along[0] + along[1] + along[2]) * (1.0 / SIZE))
        )
        dqb[:, cols] = dq.astype(BF16)
        so_v[:, cols] = (
            rounded[0] * values[0] + rounded[1] * values[1] + rounded[2] * values[2]
        ).astype(BF16)
        dkbase[:, cols] = (scaled[2] * k_inv[2]) * q - (
            k_inv[2] * k_inv[2] * along[2] * (1.0 / SIZE)
        ) * keys[2]
        dvbase[:, cols] = rounded[2] * gw[OWN, cols].astype(F32)
        rko[:, cols] = jnp.broadcast_to(k_inv[2], (ROWS, SIZE))

    loop(HEADS, site_head)
    so_store = pltpu.make_async_copy(so_v, so_hbm.at[0], store_sem.at[0])
    so_store.start()

    def back_q(n):
        dn[:, tile_cols(n)] = dot_nt(dqb[...], wqkv[tile_cols(n), :ATT])

    loop(MODEL // TILE, back_q)
    project_q(0, 2 * ROWS)

    for slot in rest:
        q_arrive(slot)

    def key_side(h):
        cols = head_cols(h)
        et_w[h] = (jnp.exp2(dot_nt(kw[OWN, cols], qw[:, cols])) * mask[...]).astype(BF16)

    loop(HEADS, key_side)

    for n in range(2):
        grad_copy(n).wait_recv()
        pack_copy(n).wait_recv()

    def site_keys(h):
        cols = head_cols(h)
        spread = dot(prb[...], pick[:, 3 * h * SIZE : 3 * (h + 1) * SIZE])
        inverse = rko[:, cols]
        dkey, dvalue, along = dkbase[:, cols], dvbase[:, cols], 0.0
        gathered = 0.0
        for x in range(2):
            rows = slice(x * ROWS, (x + 1) * ROWS)
            gathered = gathered + spread[rows, :SIZE] * qf[rows, cols]
            along = along + spread[rows, SIZE : 2 * SIZE]
            dvalue = dvalue + spread[rows, 2 * SIZE :] * gw[rows, cols].astype(F32)
        own_key = kvb[OWN, cols].astype(F32)
        dkey = dkey + inverse * gathered - inverse * inverse * (1.0 / SIZE) * along * own_key
        dkv[:, cols] = dkey.astype(BF16)
        dkv[:, head_cols(h, ATT)] = dvalue.astype(BF16)

    loop(HEADS, site_keys)

    product = 0.0
    for n in range(MODEL // TILE):
        cols = tile_cols(n)
        gained = gain_ref[cols][None, :] * (dn[:, cols] + dot(dkv[...], wkv_t[:, cols]))
        dn[:, cols] = gained
        both = rsum[OWN, cols] * gained
        product = product + both[:, :SIZE] + both[:, SIZE:]
    average = jnp.sum(product, axis=-1, keepdims=True) * (1.0 / MODEL)
    inverse = inv_b[OWN, :]
    factor = inverse * inverse * inverse * average
    inverse = jnp.concatenate([inverse] * 2, axis=1)
    factor = jnp.concatenate([factor] * 2, axis=1)
    for n in range(MODEL // TILE):
        cols = tile_cols(n)
        gr_v[:, cols] = (inverse * dn[:, cols] - rsum[OWN, cols] * factor).astype(BF16)
    gr_store = pltpu.make_async_copy(gr_v, gr_hbm.at[0], store_sem.at[1])
    gr_store.start()

    def back_out(ch):
        cols = tile_cols(ch)
        d_rows = (dot(gr_v[...], wo_t[:, cols]) * itot[:, cols]).astype(BF16)
        dw[OWN, cols] = d_rows
        product = out_f[:, cols] * d_rows.astype(F32)
        high = product.astype(BF16)
        low = (product - high.astype(F32)).astype(BF16)
        ones = jnp.ones((8, SIZE), BF16)
        kept = lax.broadcasted_iota(jnp.int32, (8, SIZE), 0)
        for part in range(PER):
            cut = slice(part * SIZE, (part + 1) * SIZE)
            here = head_cols(ch * PER + part)
            total = jnp.sum(product[:, cut], axis=-1, keepdims=True)
            dcol[:, here] = jnp.broadcast_to(total, (ROWS, SIZE))
            line = dot_nt(ones, high[:, cut]) + dot_nt(ones, low[:, cut])
            top = line.astype(BF16).astype(F32)
            dl[16:24, here] = jnp.where(
                kept == 0, top, jnp.where(kept == 1, line - top, 0.0)
            ).astype(BF16)
        for n in range(3):
            for kind in range(2):
                d_copy(kind, ch, n).start()

    loop(CHUNKS, back_out)

    def query_side(ch):
        for part in range(PER):
            h = ch * PER + part
            cols = head_cols(h)
            dprobs = dot_nt(dw[OWN, cols], vw[:, cols])
            dscores = e_w[h].astype(F32) * (dprobs - dcol[:, cols][:, :1])
            grads = dot(dscores.astype(BF16), kw[:, cols]) * SCALE
            inverse = rq_b[:, cols]
            normed = qraw[:, cols].astype(F32) * inverse
            gq_v[:, cols] = (inverse * (grads - normed * lane_mean(normed * grads))).astype(BF16)
        for kind in range(2):
            d_arrive(kind, ch, relay_from)
            d_pass(kind, ch).start()

    loop(CHUNKS, query_side)
    gq_store = pltpu.make_async_copy(gq_v, gq_hbm.at[0], store_sem.at[2])
    gq_store.start()

    def key_grads(ch):
        for slot in rest:
            for kind in range(2):
                d_arrive(kind, ch, slot)
        for part in range(PER):
            h = ch * PER + part
            cols = head_cols(h)
            d_rows = dw[:, cols]
            lines = []
            for slot in range(SLOTS):
                line = dl[slot * 8 : (slot + 1) * 8, cols].astype(F32)
                lines.append(line[0:1] + line[1:2])
            weights = et_w[h]
            dprobs = dot_nt(vw[OWN, cols], d_rows)
            dscores = weights.astype(F32) * (dprobs - jnp.concatenate(lines, axis=1))
            grads = dot(dscores.astype(BF16), qw[:, cols]) * LN2
            inverse = rk_b[:, cols]
            normed = kraw[:, cols].astype(F32) * inverse
            gk_v[:, cols] = (inverse * (grads - normed * lane_mean(normed * grads))).astype(BF16)
            gv_v[:, cols] = dot(weights, d_rows).astype(BF16)

    loop(CHUNKS, key_grads)
    gk_store = pltpu.make_async_copy(gk_v, gk_hbm.at[0], store_sem.at[3])
    gv_store = pltpu.make_async_copy(gv_v, gv_hbm.at[0], store_sem.at[4])
    gk_store.start()
    gv_store.start()

    for ch in range(CHUNKS):
        for kind in range(2):
            for n in range(3):
                kv_copy(kind, ch, n).wait_send()
                d_copy(kind, ch, n).wait_send()
            kv_pass(kind, ch).wait_send()
            d_pass(kind, ch).wait_send()
        for n in range(2):
            out_copy(ch, n).wait_send()
    for n in range(3):
        q_copy(n).wait_send()
    q_pass().wait_send()
    for n in range(2):
        resid_copy(n).wait_send()
        grad_copy(n).wait_send()
        pack_copy(n).wait_send()
    for copy in (so_store, gr_store, gq_store, gk_store, gv_store):
        copy.wait()


def hand_over(*refs):
    sems = refs[-1]
    count = len(refs) // 2
    copies = [
        pltpu.make_async_copy(refs[n], refs[count + n], sems.at[n]) for n in range(count)
    ]
    for copy in copies:
        copy.start()
    for copy in copies:
        copy.wait()


def shards(tm_count, site_count, q_time, k_time, v_time, resid, w_out_time, norm_gain, w_qkv_site, grad_site, nbr_blocks):
    assert q_time.shape == (1, ROWS, ATT) and resid.shape == (1, ROWS, MODEL)
    anywhere = pl.BlockSpec(memory_space=pl.ANY)
    narrow = jax.ShapeDtypeStruct((1, ROWS, ATT), BF16)
    wide = jax.ShapeDtypeStruct((1, ROWS, MODEL), BF16)
    vmem = pltpu.VMEM
    dma = pltpu.SemaphoreType.DMA
    results = pl.pallas_call(
        functools.partial(kernel, tm_count, site_count),
        out_shape=(narrow, narrow, narrow, narrow, wide),
        in_specs=[pl.BlockSpec(memory_space=pltpu.HBM)] * 9,
        out_specs=(anywhere,) * 5,
        scratch_shapes=[
            pltpu.SMEM((1, 2), jnp.int32),
            vmem((MODEL,), F32),
            vmem((ROWS, ATT), BF16),
            vmem((ROWS, ATT), BF16),
            vmem((WINDOW, ATT), BF16),
            vmem((WINDOW, ATT), BF16),
            vmem((WINDOW, ATT), BF16),
            vmem((WINDOW, ATT), BF16),
            vmem((SLOTS * 8, ATT), BF16),
            vmem((ROWS, WINDOW), F32),
            vmem((ROWS, ATT), F32),
            vmem((ROWS, ATT), F32),
            vmem((ROWS, ATT), F32),
            vmem((ROWS, ATT), F32),
            vmem((ROWS, ATT), F32),
            vmem((HEADS, ROWS, WINDOW), BF16),
            vmem((HEADS, ROWS, WINDOW), BF16),
            vmem((3 * ROWS, ATT), BF16),
            vmem((3 * ROWS, MODEL), BF16),
            vmem((3 * ROWS, ATT), BF16),
            vmem((ATT, MODEL), BF16),
            vmem((MODEL, 3 * ATT), BF16),
            vmem((TILE, TILE), BF16),
            vmem((MODEL, ATT), BF16),
            vmem((2 * ATT, MODEL), BF16),
            vmem((3 * ROWS, MODEL), F32),
            vmem((3 * ROWS, SIZE), F32),
            vmem((3 * ROWS, MODEL), BF16),
            vmem((3 * ROWS, ATT), F32),
            vmem((3 * ROWS, 2 * ATT), BF16),
            vmem((SIZE, 3 * ATT), BF16),
            vmem((2 * ROWS, SIZE), BF16),
            vmem((2 * ROWS, SIZE), BF16),
            vmem((ROWS, ATT), BF16),
            vmem((ROWS, ATT), F32),
            vmem((ROWS, ATT), F32),
            vmem((ROWS, ATT), F32),
            vmem((ROWS, 2 * ATT), BF16),
            vmem((ROWS, MODEL), F32),
            vmem((ROWS, ATT), BF16),
            vmem((ROWS, ATT), BF16),
            vmem((ROWS, ATT), BF16),
            vmem((ROWS, ATT), BF16),
            vmem((ROWS, MODEL), BF16),
            dma((9,)),
            dma((5,)),
            dma((2, CHUNKS, 3)),
            dma((2, CHUNKS, SLOTS)),
            dma((2, CHUNKS)),
            dma((3,)),
            dma((SLOTS,)),
            dma((1,)),
            dma((2,)),
            dma((2,)),
            dma((2,)),
            dma((2,)),
            dma((CHUNKS, 2)),
            dma((CHUNKS, 2)),
            dma((2,)),
            dma((2,)),
            dma((2, CHUNKS, 3)),
            dma((2, CHUNKS, SLOTS)),
            dma((2, CHUNKS)),
        ],
        compiler_params=pltpu.CompilerParams(
            collective_id=0, has_side_effects=True, vmem_limit_bytes=48 * 1024 * 1024
        ),
    )(
        *(
            pltpu.with_memory_space_constraint(x, pltpu.HBM)
            for x in (nbr_blocks, norm_gain, q_time, k_time, v_time, resid, w_out_time, w_qkv_site, grad_site)
        ),
    )
    return pl.pallas_call(
        hand_over,
        out_shape=(narrow, narrow, narrow, narrow, wide),
        in_specs=[anywhere] * 5,
        out_specs=(anywhere,) * 5,
        scratch_shapes=[dma((5,))],
        compiler_params=pltpu.CompilerParams(vmem_limit_bytes=1024 * 1024),
    )(*results)


def solution(mesh):
    rows = P("site", "tm", None)
    return jax.shard_map(
        functools.partial(shards, mesh.shape["tm"], mesh.shape["site"]),
        mesh=mesh,
        in_specs=(rows, rows, rows, rows, P(), P(), P(), rows, P("site", None)),
        out_specs=(rows,) * 5,
        check_vma=False,
    )
```

```python
import functools

import jax
import jax.numpy as jnp
from jax import lax
from jax.experimental import pallas as pl
from jax.experimental.pallas import tpu as pltpu
from jax.sharding import PartitionSpec as P

HEADS = 6
SIZE = 128
ROWS = 128
ATT = HEADS * SIZE
MODEL = 1536
EPSILON = 1e-05
SCALE = SIZE ** (-0.5)
LOG2E = 1.4426950408889634
LN2 = 0.6931471805599453
SLOTS = 5
WINDOW = SLOTS * ROWS
CHUNKS = 3
WIDTH = ATT // CHUNKS
PER = HEADS // CHUNKS
TILE = 256
BLOCK = 32
F32 = jnp.float32
BF16 = jnp.bfloat16
MESH = pl.DeviceIdType.MESH
OWN = slice(2 * ROWS, 3 * ROWS)


def dot(a, b):
    return jnp.dot(a, b, preferred_element_type=F32)


def dot_nt(a, b):
    return lax.dot_general(a, b, (((1,), (1,)), ((), ())), preferred_element_type=F32)


def lane_mean(x):
    return jnp.sum(x, axis=-1, keepdims=True) * (1.0 / x.shape[-1])


def head_cols(h, base=0):
    return slice(h * SIZE + base, (h + 1) * SIZE + base)


def tile_cols(n, base=0):
    return slice(n * TILE + base, (n + 1) * TILE + base)


def loop(count, body):
    for i in range(count):
        body(i)


def kernel(
    tm_count,
    site_count,
    nbr_hbm,
    gain_hbm,
    q_hbm,
    k_hbm,
    v_hbm,
    resid_hbm,
    wo_hbm,
    wqkv_hbm,
    grad_hbm,
    so_hbm,
    gq_hbm,
    gk_hbm,
    gv_hbm,
    gr_hbm,
    nbr_ref,
    gain_ref,
    qraw,
    kraw,
    qw,
    kw,
    vw,
    dw,
    dl,
    mask,
    rq_b,
    rk_b,
    itot,
    out_f,
    dcol,
    e_w,
    et_w,
    ow,
    rw,
    gw,
    wo,
    wqkv,
    eye,
    wo_t,
    wkv_t,
    rsum,
    inv_b,
    nb,
    qf,
    kvb,
    pick,
    pkb,
    prb,
    dqb,
    dkbase,
    dvbase,
    rko,
    dkv,
    dn,
    so_v,
    gq_v,
    gk_v,
    gv_v,
    gr_v,
    load_sem,
    store_sem,
    kv_send,
    kv_recv,
    kv_relay,
    q_send,
    q_recv,
    q_relay,
    r_send,
    r_recv,
    g_send,
    g_recv,
    o_send,
    o_recv,
    p_send,
    p_recv,
    d_send,
    d_recv,
    d_relay,
):
    tm = lax.axis_index("tm")
    st = lax.axis_index("site")
    core = lax.rem(tm, 2)
    sib = tm + 1 - 2 * core
    right_chip = lax.rem(tm + 2 - core, tm_count)
    left_chip = lax.rem(tm - 1 - core + tm_count, tm_count)
    up = lax.rem(st + 1, site_count)
    down = lax.rem(st + site_count - 1, site_count)
    time_dests = ((right_chip, core), (left_chip, 3 + core), (sib, 1 + 2 * core))
    relay_from = 1 + 2 * core
    relay_to = 4 * core
    rest = (4 * core, 3 - 2 * core, 4 - 4 * core)

    loads = [
        pltpu.make_async_copy(src, dst, load_sem.at[n])
        for n, (src, dst) in enumerate(
            (
                (k_hbm.at[0], kraw),
                (q_hbm.at[0], qraw),
                (v_hbm.at[0], vw.at[OWN]),
                (resid_hbm.at[0], rw.at[OWN]),
                (grad_hbm.at[0], gw.at[OWN]),
                (wo_hbm, wo),
                (wqkv_hbm, wqkv),
                (gain_hbm, gain_ref),
                (nbr_hbm, nbr_ref),
            )
        )
    ]
    for copy in loads:
        copy.start()

    barrier = pltpu.get_barrier_semaphore()
    for offset in (1, 2, tm_count - 1, tm_count - 2):
        pl.semaphore_signal(
            barrier, inc=1, device_id={"tm": lax.rem(tm + offset, tm_count)}, device_id_type=MESH
        )
    for peer in (up, down):
        pl.semaphore_signal(barrier, inc=1, device_id={"site": peer}, device_id_type=MESH)

    row = lax.broadcasted_iota(jnp.int32, (ROWS, ROWS), 0)
    lane = lax.broadcasted_iota(jnp.int32, (ROWS, ROWS), 1)
    for slot in range(SLOTS):
        shard = tm + slot - 2
        valid = jnp.where((shard >= 0) & (shard < tm_count), 1.0, 0.0).astype(F32)
        if slot == 0:
            band = jnp.where(lane >= row, valid, 0.0)
        elif slot == SLOTS - 1:
            band = jnp.where(lane <= row, valid, 0.0)
        else:
            band = jnp.full((ROWS, ROWS), valid, F32)
        mask[:, slot * ROWS : (slot + 1) * ROWS] = band

    for h in range(HEADS):
        for n in range(3):
            pick[:, head_cols(3 * h + n)] = jnp.where(row == 8 * n + h, 1.0, 0.0).astype(BF16)

    def normalise(raw, store, inverse, factor):
        def body(h):
            cols = head_cols(h)
            x = raw[:, cols].astype(F32)
            r = lax.rsqrt(lane_mean(x * x) + EPSILON)
            inverse[:, cols] = jnp.broadcast_to(r, (ROWS, SIZE))
            store[OWN, cols] = (x * (r * factor)).astype(BF16)

        loop(HEADS, body)

    wide_row = lax.broadcasted_iota(jnp.int32, (TILE, TILE), 0)
    wide_lane = lax.broadcasted_iota(jnp.int32, (TILE, TILE), 1)
    eye[...] = jnp.where(wide_row == wide_lane, 1.0, 0.0).astype(BF16)

    def transpose(source, base, target, first, last):
        def body(n, carry):
            rows = pl.ds(pl.multiple_of(n * TILE, TILE), TILE)
            cols = pl.ds(pl.multiple_of(n * TILE + base, TILE), TILE)
            target[rows, :] = dot_nt(eye[...], source[:, cols]).astype(BF16)
            return carry

        lax.fori_loop(first, last, body, 0)

    def remote(src, dst, send, recv, device):
        return pltpu.make_async_remote_copy(
            src_ref=src,
            dst_ref=dst,
            send_sem=send,
            recv_sem=recv,
            device_id=device,
            device_id_type=MESH,
        )

    def slot_rows(slot, size=ROWS):
        return pl.ds(pl.multiple_of(slot * size, size), size)

    def kv_copy(kind, ch, n):
        device, slot = time_dests[n]
        cols = tile_cols(ch)
        src = kw.at[OWN, cols] if kind == 0 else v_hbm.at[0, :, cols]
        dst = (kw if kind == 0 else vw).at[slot_rows(slot), cols]
        return remote(
            src, dst, kv_send.at[kind, ch, n], kv_recv.at[kind, ch, slot], {"tm": device}
        )

    def kv_pass(kind, ch):
        cols = tile_cols(ch)
        buffer = kw if kind == 0 else vw
        return remote(
            buffer.at[slot_rows(relay_from), cols],
            buffer.at[slot_rows(relay_to), cols],
            kv_relay.at[kind, ch],
            kv_recv.at[kind, ch, relay_to],
            {"tm": sib},
        )

    def kv_arrive(kind, ch, slot):
        cols = tile_cols(ch)
        here = (kw if kind == 0 else vw).at[slot_rows(slot), cols]
        remote(here, here, kv_relay.at[kind, ch], kv_recv.at[kind, ch, slot], {"tm": sib}).wait_recv()

    def q_copy(n):
        device, slot = time_dests[n]
        return remote(
            qw.at[OWN], qw.at[slot_rows(slot)], q_send.at[n], q_recv.at[slot], {"tm": device}
        )

    def q_pass():
        return remote(
            qw.at[slot_rows(relay_from)],
            qw.at[slot_rows(relay_to)],
            q_relay.at[0],
            q_recv.at[relay_to],
            {"tm": sib},
        )

    def q_arrive(slot):
        here = qw.at[slot_rows(slot)]
        remote(here, here, q_relay.at[0], q_recv.at[slot], {"tm": sib}).wait_recv()

    def site_copy(n, src, dst, send, recv):
        return remote(
            src, dst.at[n * ROWS : (n + 1) * ROWS], send, recv, {"site": (up, down)[n]}
        )

    def out_copy(ch, n):
        cols = tile_cols(ch)
        return remote(
            ow.at[OWN, cols],
            ow.at[n * ROWS : (n + 1) * ROWS, cols],
            o_send.at[ch, n],
            o_recv.at[ch, n],
            {"site": (up, down)[n]},
        )

    def resid_copy(n):
        return site_copy(n, resid_hbm.at[0], rw, r_send.at[n], r_recv.at[n])

    def grad_copy(n):
        return site_copy(n, grad_hbm.at[0], gw, g_send.at[n], g_recv.at[n])

    def pack_copy(n):
        return site_copy(n, pkb.at[n * ROWS : (n + 1) * ROWS], prb, p_send.at[n], p_recv.at[n])

    def d_copy(kind, ch, n):
        device, slot = time_dests[n]
        cols = tile_cols(ch)
        buffer, size = ((dw, ROWS), (dl, 8))[kind]
        return remote(
            buffer.at[2 * size : 3 * size, cols],
            buffer.at[slot_rows(slot, size), cols],
            d_send.at[kind, ch, n],
            d_recv.at[kind, ch, slot],
            {"tm": device},
        )

    def d_pass(kind, ch):
        cols = tile_cols(ch)
        buffer, size = ((dw, ROWS), (dl, 8))[kind]
        return remote(
            buffer.at[slot_rows(relay_from, size), cols],
            buffer.at[slot_rows(relay_to, size), cols],
            d_relay.at[kind, ch],
            d_recv.at[kind, ch, relay_to],
            {"tm": sib},
        )

    def d_arrive(kind, ch, slot):
        cols = tile_cols(ch)
        buffer, size = ((dw, ROWS), (dl, 8))[kind]
        here = buffer.at[slot_rows(slot, size), cols]
        remote(here, here, d_relay.at[kind, ch], d_recv.at[kind, ch, slot], {"tm": sib}).wait_recv()

    pl.semaphore_wait(barrier, 6)
    for n in range(3):
        kv_copy(1, 0, n).start()
    for n in range(2):
        resid_copy(n).start()
    loads[0].wait()
    normalise(kraw, kw, rk_b, 1.0)
    for ch in range(CHUNKS):
        for kind in range(2) if ch == 0 else (1, 0):
            if (kind, ch) != (1, 0):
                for n in range(3):
                    kv_copy(kind, ch, n).start()
    for n in range(3):
        if n == 0:
            loads[1].wait()
            normalise(qraw, qw, rq_b, SCALE * LOG2E)
        q_copy(n).start()
    loads[2].wait()
    loads[3].wait()
    loads[5].wait()
    loads[7].wait()
    loads[8].wait()
    transpose(wo, 0, wo_t, 0, MODEL // TILE)
    loads[6].wait()

    def project_out(ch, first, count):
        rows = slice(first, first + count)
        squares = 0.0
        for n in range(MODEL // TILE):
            cols = tile_cols(n)
            before = rw[rows, cols].astype(F32) if ch == 0 else rsum[rows, cols]
            x = before + dot(ow[rows, tile_cols(ch)], wo[tile_cols(ch), cols])
            rsum[rows, cols] = x
            if ch == CHUNKS - 1:
                nb[rows, cols] = (x * gain_ref[cols][None, :]).astype(BF16)
                squares = squares + x[:, :SIZE] * x[:, :SIZE] + x[:, SIZE:] * x[:, SIZE:]
        if ch == CHUNKS - 1:
            mean = jnp.sum(squares, axis=-1, keepdims=True) * (1.0 / MODEL)
            inv_b[rows, :] = jnp.broadcast_to(lax.rsqrt(mean + EPSILON), (count, SIZE))

    def forward(ch):
        for kind in (1, 0):
            kv_arrive(kind, ch, relay_from)
            kv_pass(kind, ch).start()
        for slot in rest:
            for kind in range(2):
                kv_arrive(kind, ch, slot)
        for part in range(PER):
            h = ch * PER + part
            cols = head_cols(h)
            weights = (
                jnp.exp2(dot_nt(qw[OWN, cols], kw[:, cols])) * mask[...]
            ).astype(BF16)
            e_w[h] = weights
            inverse = 1.0 / jnp.sum(weights.astype(F32), axis=-1, keepdims=True)
            heads_out = dot(weights, vw[:, cols]) * inverse
            itot[:, cols] = jnp.broadcast_to(inverse, (ROWS, SIZE))
            out_f[:, cols] = heads_out
            ow[OWN, cols] = heads_out.astype(BF16)
        for n in range(2):
            out_copy(ch, n).start()
        project_out(ch, 2 * ROWS, ROWS)
        if ch < CHUNKS - 1:
            transpose(wqkv, ATT, wkv_t, 3 * ch, 3 * ch + 3)

    loop(CHUNKS, forward)
    for n in range(2):
        grad_copy(n).start()

    def project_q(first, count):
        rows = slice(first, first + count)

        def body(n):
            inverse = jnp.concatenate([inv_b[rows, :]] * 2, axis=1)
            qf[rows, tile_cols(n)] = dot(nb[rows, :], wqkv[:, tile_cols(n)]) * inverse

        loop(ATT // TILE, body)

    def project_kv(first, count):
        rows = slice(first, first + count)

        def body(n):
            inverse = jnp.concatenate([inv_b[rows, :]] * 2, axis=1)
            product = dot(nb[rows, :], wqkv[:, tile_cols(n, ATT)])
            kvb[rows, tile_cols(n)] = (product * inverse).astype(BF16)

        loop(2 * ATT // TILE, body)

    project_q(2 * ROWS, ROWS)
    project_kv(2 * ROWS, ROWS)
    loads[4].wait()

    first_named, second_named = nbr_ref[0, 0], nbr_ref[0, 1]
    seen = [
        jnp.where((first_named == peer) | (second_named == peer), 1.0, 0.0).astype(F32)
        for peer in (st - 1, st + 1)
    ]

    def site_key(h, x):
        return kvb[x * ROWS : (x + 1) * ROWS, head_cols(h)].astype(F32)

    def site_value(h, x):
        return kvb[x * ROWS : (x + 1) * ROWS, head_cols(h, ATT)].astype(F32)

    def site_scores(h, x):
        key = site_key(h, x)
        k_inv = lax.rsqrt(lane_mean(key * key) + EPSILON)
        score = jnp.sum(qf[OWN, head_cols(h)] * key, axis=-1, keepdims=True)
        grad = gw[OWN, head_cols(h)].astype(F32)
        dprob = jnp.sum(grad * site_value(h, x), axis=-1, keepdims=True)
        return k_inv, score, dprob

    own_stats = []
    for h in range(HEADS):
        q = qf[OWN, head_cols(h)]
        q_inv = lax.rsqrt(lane_mean(q * q) + EPSILON)
        own_stats.append((q_inv, site_scores(h, 2)))

    for n in range(2):
        resid_copy(n).wait_recv()
    for ch in range(CHUNKS):
        for n in range(2):
            out_copy(ch, n).wait_recv()
        project_out(ch, 0, 2 * ROWS)
    project_kv(0, 2 * ROWS)

    site_stats = []
    packs = [jnp.zeros((ROWS, SIZE), F32) for _ in range(2)]
    for h in range(HEADS):
        q_inv, own = own_stats[h]
        k_inv, scores, dprobs = zip(site_scores(h, 0), site_scores(h, 1), own)
        scores = [s * (q_inv * r * SCALE) for s, r in zip(scores, k_inv)]
        exps = [jnp.exp(s) for s in scores]
        exps = [exps[0] * seen[0], exps[1] * seen[1], exps[2]]
        inverse = 1.0 / (exps[0] + exps[1] + exps[2])
        probs = [e * inverse for e in exps]
        rounded = [p.astype(BF16).astype(F32) for p in probs]
        delta = probs[0] * dprobs[0] + probs[1] * dprobs[1] + probs[2] * dprobs[2]
        dscores = [p * (d - delta) for p, d in zip(probs, dprobs)]
        along = [d * s for d, s in zip(dscores, scores)]
        scaled = [d * (q_inv * SCALE) for d in dscores]
        for n in range(2):
            x = 1 - n
            for place, value in enumerate((scaled[x], along[x], rounded[x])):
                packs[n] = jnp.where(lane == h + 8 * place, value, packs[n])
        site_stats.append((q_inv, k_inv, rounded, along, scaled))
    for n in range(2):
        pkb[n * ROWS : (n + 1) * ROWS, :] = packs[n].astype(BF16)
        pack_copy(n).start()

    q_arrive(relay_from)
    q_pass().start()

    def site_head(h):
        cols = head_cols(h)
        q_inv, k_inv, rounded, along, scaled = site_stats[h]
        q = qf[OWN, cols]
        keys = [site_key(h, x) for x in range(3)]
        values = [site_value(h, x) for x in range(3)]
        dq = (
            scaled[0] * k_inv[0] * keys[0]
            + scaled[1] * k_inv[1] * keys[1]
            + scaled[2] * k_inv[2] * keys[2]
            - q * (q_inv * q_inv * (along[0] + along[1] + along[2]) * (1.0 / SIZE))
        )
        dqb[:, cols] = dq.astype(BF16)
        so_v[:, cols] = (
            rounded[0] * values[0] + rounded[1] * values[1] + rounded[2] * values[2]
        ).astype(BF16)
        dkbase[:, cols] = (scaled[2] * k_inv[2]) * q - (
            k_inv[2] * k_inv[2] * along[2] * (1.0 / SIZE)
        ) * keys[2]
        dvbase[:, cols] = rounded[2] * gw[OWN, cols].astype(F32)
        rko[:, cols] = jnp.broadcast_to(k_inv[2], (ROWS, SIZE))

    loop(HEADS, site_head)
    so_store = pltpu.make_async_copy(so_v, so_hbm.at[0], store_sem.at[0])
    so_store.start()

    def back_q(n):
        dn[:, tile_cols(n)] = dot_nt(dqb[...], wqkv[tile_cols(n), :ATT])

    loop(MODEL // TILE, back_q)
    project_q(0, 2 * ROWS)

    for slot in rest:
        q_arrive(slot)

    def key_side(h):
        cols = head_cols(h)
        et_w[h] = (jnp.exp2(dot_nt(kw[OWN, cols], qw[:, cols])) * mask[...]).astype(BF16)

    loop(HEADS, key_side)

    for n in range(2):
        grad_copy(n).wait_recv()
        pack_copy(n).wait_recv()

    def site_keys(h):
        cols = head_cols(h)
        spread = dot(prb[...], pick[:, 3 * h * SIZE : 3 * (h + 1) * SIZE])
        inverse = rko[:, cols]
        dkey, dvalue, along = dkbase[:, cols], dvbase[:, cols], 0.0
        gathered = 0.0
        for x in range(2):
            rows = slice(x * ROWS, (x + 1) * ROWS)
            gathered = gathered + spread[rows, :SIZE] * qf[rows, cols]
            along = along + spread[rows, SIZE : 2 * SIZE]
            dvalue = dvalue + spread[rows, 2 * SIZE :] * gw[rows, cols].astype(F32)
        own_key = kvb[OWN, cols].astype(F32)
        dkey = dkey + inverse * gathered - inverse * inverse * (1.0 / SIZE) * along * own_key
        dkv[:, cols] = dkey.astype(BF16)
        dkv[:, head_cols(h, ATT)] = dvalue.astype(BF16)

    loop(HEADS, site_keys)

    product = 0.0
    for n in range(MODEL // TILE):
        cols = tile_cols(n)
        gained = gain_ref[cols][None, :] * (dn[:, cols] + dot(dkv[...], wkv_t[:, cols]))
        dn[:, cols] = gained
        both = rsum[OWN, cols] * gained
        product = product + both[:, :SIZE] + both[:, SIZE:]
    average = jnp.sum(product, axis=-1, keepdims=True) * (1.0 / MODEL)
    inverse = inv_b[OWN, :]
    factor = inverse * inverse * inverse * average
    inverse = jnp.concatenate([inverse] * 2, axis=1)
    factor = jnp.concatenate([factor] * 2, axis=1)
    for n in range(MODEL // TILE):
        cols = tile_cols(n)
        gr_v[:, cols] = (inverse * dn[:, cols] - rsum[OWN, cols] * factor).astype(BF16)
    gr_store = pltpu.make_async_copy(gr_v, gr_hbm.at[0], store_sem.at[1])
    gr_store.start()

    def back_out(ch):
        cols = tile_cols(ch)
        d_rows = (dot(gr_v[...], wo_t[:, cols]) * itot[:, cols]).astype(BF16)
        dw[OWN, cols] = d_rows
        product = out_f[:, cols] * d_rows.astype(F32)
        high = product.astype(BF16)
        low = (product - high.astype(F32)).astype(BF16)
        ones = jnp.ones((8, SIZE), BF16)
        kept = lax.broadcasted_iota(jnp.int32, (8, SIZE), 0)
        for part in range(PER):
            cut = slice(part * SIZE, (part + 1) * SIZE)
            here = head_cols(ch * PER + part)
            total = jnp.sum(product[:, cut], axis=-1, keepdims=True)
            dcol[:, here] = jnp.broadcast_to(total, (ROWS, SIZE))
            line = dot_nt(ones, high[:, cut]) + dot_nt(ones, low[:, cut])
            top = line.astype(BF16).astype(F32)
            dl[16:24, here] = jnp.where(
                kept == 0, top, jnp.where(kept == 1, line - top, 0.0)
            ).astype(BF16)
        for n in range(3):
            for kind in range(2):
                d_copy(kind, ch, n).start()

    loop(CHUNKS, back_out)

    def query_side(ch):
        for part in range(PER):
            h = ch * PER + part
            cols = head_cols(h)
            dprobs = dot_nt(dw[OWN, cols], vw[:, cols])
            dscores = e_w[h].astype(F32) * (dprobs - dcol[:, cols][:, :1])
            grads = dot(dscores.astype(BF16), kw[:, cols]) * SCALE
            inverse = rq_b[:, cols]
            normed = qraw[:, cols].astype(F32) * inverse
            gq_v[:, cols] = (inverse * (grads - normed * lane_mean(normed * grads))).astype(BF16)
        for kind in range(2):
            d_arrive(kind, ch, relay_from)
            d_pass(kind, ch).start()

    loop(CHUNKS, query_side)
    gq_store = pltpu.make_async_copy(gq_v, gq_hbm.at[0], store_sem.at[2])
    gq_store.start()

    def key_grads(ch):
        for slot in rest:
            for kind in range(2):
                d_arrive(kind, ch, slot)
        for part in range(PER):
            h = ch * PER + part
            cols = head_cols(h)
            d_rows = dw[:, cols]
            lines = []
            for slot in range(SLOTS):
                line = dl[slot * 8 : (slot + 1) * 8, cols].astype(F32)
                lines.append(line[0:1] + line[1:2])
            weights = et_w[h]
            dprobs = dot_nt(vw[OWN, cols], d_rows)
            dscores = weights.astype(F32) * (dprobs - jnp.concatenate(lines, axis=1))
            grads = dot(dscores.astype(BF16), qw[:, cols]) * LN2
            inverse = rk_b[:, cols]
            normed = kraw[:, cols].astype(F32) * inverse
            gk_v[:, cols] = (inverse * (grads - normed * lane_mean(normed * grads))).astype(BF16)
            gv_v[:, cols] = dot(weights, d_rows).astype(BF16)

    loop(CHUNKS, key_grads)
    gk_store = pltpu.make_async_copy(gk_v, gk_hbm.at[0], store_sem.at[3])
    gv_store = pltpu.make_async_copy(gv_v, gv_hbm.at[0], store_sem.at[4])
    gk_store.start()
    gv_store.start()

    for ch in range(CHUNKS):
        for kind in range(2):
            for n in range(3):
                kv_copy(kind, ch, n).wait_send()
                d_copy(kind, ch, n).wait_send()
            kv_pass(kind, ch).wait_send()
            d_pass(kind, ch).wait_send()
        for n in range(2):
            out_copy(ch, n).wait_send()
    for n in range(3):
        q_copy(n).wait_send()
    q_pass().wait_send()
    for n in range(2):
        resid_copy(n).wait_send()
        grad_copy(n).wait_send()
        pack_copy(n).wait_send()
    for copy in (so_store, gr_store, gq_store, gk_store, gv_store):
        copy.wait()


def hand_over(*refs):
    sems = refs[-1]
    count = len(refs) // 2
    copies = [
        pltpu.make_async_copy(refs[n], refs[count + n], sems.at[n]) for n in range(count)
    ]
    for copy in copies:
        copy.start()
    for copy in copies:
        copy.wait()


def shards(tm_count, site_count, q_time, k_time, v_time, resid, w_out_time, norm_gain, w_qkv_site, grad_site, nbr_blocks):
    assert q_time.shape == (1, ROWS, ATT) and resid.shape == (1, ROWS, MODEL)
    anywhere = pl.BlockSpec(memory_space=pl.ANY)
    narrow = jax.ShapeDtypeStruct((1, ROWS, ATT), BF16)
    wide = jax.ShapeDtypeStruct((1, ROWS, MODEL), BF16)
    vmem = pltpu.VMEM
    dma = pltpu.SemaphoreType.DMA
    results = pl.pallas_call(
        functools.partial(kernel, tm_count, site_count),
        out_shape=(narrow, narrow, narrow, narrow, wide),
        in_specs=[pl.BlockSpec(memory_space=pltpu.HBM)] * 9,
        out_specs=(anywhere,) * 5,
        scratch_shapes=[
            pltpu.SMEM((1, 2), jnp.int32),
            vmem((MODEL,), F32),
            vmem((ROWS, ATT), BF16),
            vmem((ROWS, ATT), BF16),
            vmem((WINDOW, ATT), BF16),
            vmem((WINDOW, ATT), BF16),
            vmem((WINDOW, ATT), BF16),
            vmem((WINDOW, ATT), BF16),
            vmem((SLOTS * 8, ATT), BF16),
            vmem((ROWS, WINDOW), F32),
            vmem((ROWS, ATT), F32),
            vmem((ROWS, ATT), F32),
            vmem((ROWS, ATT), F32),
            vmem((ROWS, ATT), F32),
            vmem((ROWS, ATT), F32),
            vmem((HEADS, ROWS, WINDOW), BF16),
            vmem((HEADS, ROWS, WINDOW), BF16),
            vmem((3 * ROWS, ATT), BF16),
            vmem((3 * ROWS, MODEL), BF16),
            vmem((3 * ROWS, ATT), BF16),
            vmem((ATT, MODEL), BF16),
            vmem((MODEL, 3 * ATT), BF16),
            vmem((TILE, TILE), BF16),
            vmem((MODEL, ATT), BF16),
            vmem((2 * ATT, MODEL), BF16),
            vmem((3 * ROWS, MODEL), F32),
            vmem((3 * ROWS, SIZE), F32),
            vmem((3 * ROWS, MODEL), BF16),
            vmem((3 * ROWS, ATT), F32),
            vmem((3 * ROWS, 2 * ATT), BF16),
            vmem((SIZE, 3 * ATT), BF16),
            vmem((2 * ROWS, SIZE), BF16),
            vmem((2 * ROWS, SIZE), BF16),
            vmem((ROWS, ATT), BF16),
            vmem((ROWS, ATT), F32),
            vmem((ROWS, ATT), F32),
            vmem((ROWS, ATT), F32),
            vmem((ROWS, 2 * ATT), BF16),
            vmem((ROWS, MODEL), F32),
            vmem((ROWS, ATT), BF16),
            vmem((ROWS, ATT), BF16),
            vmem((ROWS, ATT), BF16),
            vmem((ROWS, ATT), BF16),
            vmem((ROWS, MODEL), BF16),
            dma((9,)),
            dma((5,)),
            dma((2, CHUNKS, 3)),
            dma((2, CHUNKS, SLOTS)),
            dma((2, CHUNKS)),
            dma((3,)),
            dma((SLOTS,)),
            dma((1,)),
            dma((2,)),
            dma((2,)),
            dma((2,)),
            dma((2,)),
            dma((CHUNKS, 2)),
            dma((CHUNKS, 2)),
            dma((2,)),
            dma((2,)),
            dma((2, CHUNKS, 3)),
            dma((2, CHUNKS, SLOTS)),
            dma((2, CHUNKS)),
        ],
        compiler_params=pltpu.CompilerParams(
            collective_id=0, has_side_effects=True, vmem_limit_bytes=48 * 1024 * 1024
        ),
    )(
        *(
            pltpu.with_memory_space_constraint(x, pltpu.HBM)
            for x in (nbr_blocks, norm_gain, q_time, k_time, v_time, resid, w_out_time, w_qkv_site, grad_site)
        ),
    )
    return pl.pallas_call(
        hand_over,
        out_shape=(narrow, narrow, narrow, narrow, wide),
        in_specs=[anywhere] * 5,
        out_specs=(anywhere,) * 5,
        scratch_shapes=[dma((5,))],
        compiler_params=pltpu.CompilerParams(vmem_limit_bytes=1024 * 1024),
    )(*results)


def solution(mesh):
    rows = P("site", "tm", None)
    return jax.shard_map(
        functools.partial(shards, mesh.shape["tm"], mesh.shape["site"]),
        mesh=mesh,
        in_specs=(rows, rows, rows, rows, P(), P(), P(), rows, P("site", None)),
        out_specs=(rows,) * 5,
        check_vma=False,
    )
```

```python
import functools

import jax
import jax.numpy as jnp
from jax import lax
from jax.experimental import pallas as pl
from jax.experimental.pallas import tpu as pltpu
from jax.sharding import PartitionSpec as P

HEADS = 6
SIZE = 128
ROWS = 128
ATT = HEADS * SIZE
MODEL = 1536
EPSILON = 1e-05
SCALE = SIZE ** (-0.5)
LOG2E = 1.4426950408889634
LN2 = 0.6931471805599453
SLOTS = 5
WINDOW = SLOTS * ROWS
CHUNKS = 3
WIDTH = ATT // CHUNKS
PER = HEADS // CHUNKS
TILE = 256
BLOCK = 32
F32 = jnp.float32
BF16 = jnp.bfloat16
MESH = pl.DeviceIdType.MESH
OWN = slice(2 * ROWS, 3 * ROWS)


def dot(a, b):
    return jnp.dot(a, b, preferred_element_type=F32)


def dot_nt(a, b):
    return lax.dot_general(a, b, (((1,), (1,)), ((), ())), preferred_element_type=F32)


def lane_mean(x):
    return jnp.sum(x, axis=-1, keepdims=True) * (1.0 / x.shape[-1])


def head_cols(h, base=0):
    return slice(h * SIZE + base, (h + 1) * SIZE + base)


def tile_cols(n, base=0):
    return slice(n * TILE + base, (n + 1) * TILE + base)


def loop(count, body):
    for i in range(count):
        body(i)


def kernel(
    tm_count,
    site_count,
    nbr_hbm,
    gain_hbm,
    q_hbm,
    k_hbm,
    v_hbm,
    resid_hbm,
    wo_hbm,
    wqkv_hbm,
    grad_hbm,
    so_out,
    gq_out,
    gk_out,
    gv_out,
    gr_out,
    nbr_ref,
    gain_ref,
    qraw,
    kraw,
    qw,
    kw,
    vw,
    dw,
    dl,
    mask,
    rq_b,
    rk_b,
    itot,
    out_f,
    dcol,
    e_w,
    et_w,
    ow,
    rw,
    gw,
    wo,
    wqkv,
    eye,
    wo_t,
    wkv_t,
    rsum,
    inv_b,
    nb,
    qf,
    kvb,
    pick,
    pool,
    pkb,
    prb,
    dqb,
    dkbase,
    dvbase,
    rko,
    dkv,
    dn,
    load_sem,
    kv_send,
    kv_recv,
    kv_relay,
    q_send,
    q_recv,
    q_relay,
    r_send,
    r_recv,
    g_send,
    g_recv,
    o_send,
    o_recv,
    p_send,
    p_recv,
    d_send,
    d_recv,
    d_relay,
):
    so_v, gq_v, gk_v, gv_v, gr_v = (ref.at[0] for ref in (so_out, gq_out, gk_out, gv_out, gr_out))
    tm = lax.axis_index("tm")
    st = lax.axis_index("site")
    core = lax.rem(tm, 2)
    sib = tm + 1 - 2 * core
    right_chip = lax.rem(tm + 2 - core, tm_count)
    left_chip = lax.rem(tm - 1 - core + tm_count, tm_count)
    up = lax.rem(st + 1, site_count)
    down = lax.rem(st + site_count - 1, site_count)
    time_dests = ((right_chip, core), (left_chip, 3 + core), (sib, 1 + 2 * core))
    relay_from = 1 + 2 * core
    relay_to = 4 * core
    rest = (4 * core, 3 - 2 * core, 4 - 4 * core)

    loads = [
        pltpu.make_async_copy(src, dst, load_sem.at[n])
        for n, (src, dst) in enumerate(
            (
                (k_hbm.at[0], kraw),
                (q_hbm.at[0], qraw),
                (v_hbm.at[0], vw.at[OWN]),
                (resid_hbm.at[0], rw.at[OWN]),
                (grad_hbm.at[0], gw.at[OWN]),
                (wo_hbm, wo),
                (wqkv_hbm, wqkv),
                (gain_hbm, gain_ref),
                (nbr_hbm, nbr_ref),
            )
        )
    ]
    for copy in loads:
        copy.start()

    barrier = pltpu.get_barrier_semaphore()
    for offset in (1, 2, tm_count - 1, tm_count - 2):
        pl.semaphore_signal(
            barrier, inc=1, device_id={"tm": lax.rem(tm + offset, tm_count)}, device_id_type=MESH
        )
    for peer in (up, down):
        pl.semaphore_signal(barrier, inc=1, device_id={"site": peer}, device_id_type=MESH)

    row = lax.broadcasted_iota(jnp.int32, (ROWS, ROWS), 0)
    lane = lax.broadcasted_iota(jnp.int32, (ROWS, ROWS), 1)
    for slot in range(SLOTS):
        shard = tm + slot - 2
        valid = jnp.where((shard >= 0) & (shard < tm_count), 1.0, 0.0).astype(F32)
        if slot == 0:
            band = jnp.where(lane >= row, valid, 0.0)
        elif slot == SLOTS - 1:
            band = jnp.where(lane <= row, valid, 0.0)
        else:
            band = jnp.full((ROWS, ROWS), valid, F32)
        mask[:, slot * ROWS : (slot + 1) * ROWS] = band

    for h in range(HEADS):
        for n in range(3):
            pick[:, head_cols(3 * h + n)] = jnp.where(row == 8 * n + h, 1.0, 0.0).astype(BF16)

    for h in range(HEADS):
        pool[head_cols(h), :] = jnp.where(lane == h, 1.0, 0.0).astype(BF16)

    def normalise(raw, store, inverse, factor):
        def body(h):
            cols = head_cols(h)
            x = raw[:, cols].astype(F32)
            r = lax.rsqrt(lane_mean(x * x) + EPSILON)
            inverse[:, cols] = jnp.broadcast_to(r, (ROWS, SIZE))
            store[OWN, cols] = (x * (r * factor)).astype(BF16)

        loop(HEADS, body)

    wide_row = lax.broadcasted_iota(jnp.int32, (TILE, TILE), 0)
    wide_lane = lax.broadcasted_iota(jnp.int32, (TILE, TILE), 1)
    eye[...] = jnp.where(wide_row == wide_lane, 1.0, 0.0).astype(BF16)

    def transpose(source, base, target, first, last):
        def body(n, carry):
            rows = pl.ds(pl.multiple_of(n * TILE, TILE), TILE)
            cols = pl.ds(pl.multiple_of(n * TILE + base, TILE), TILE)
            target[rows, :] = dot_nt(eye[...], source[:, cols]).astype(BF16)
            return carry

        lax.fori_loop(first, last, body, 0)

    def remote(src, dst, send, recv, device):
        return pltpu.make_async_remote_copy(
            src_ref=src,
            dst_ref=dst,
            send_sem=send,
            recv_sem=recv,
            device_id=device,
            device_id_type=MESH,
        )

    def slot_rows(slot, size=ROWS):
        return pl.ds(pl.multiple_of(slot * size, size), size)

    def kv_copy(kind, ch, n):
        device, slot = time_dests[n]
        cols = tile_cols(ch)
        src = kw.at[OWN, cols] if kind == 0 else v_hbm.at[0, :, cols]
        dst = (kw if kind == 0 else vw).at[slot_rows(slot), cols]
        return remote(
            src, dst, kv_send.at[kind, ch, n], kv_recv.at[kind, ch, slot], {"tm": device}
        )

    def kv_pass(kind, ch):
        cols = tile_cols(ch)
        buffer = kw if kind == 0 else vw
        return remote(
            buffer.at[slot_rows(relay_from), cols],
            buffer.at[slot_rows(relay_to), cols],
            kv_relay.at[kind, ch],
            kv_recv.at[kind, ch, relay_to],
            {"tm": sib},
        )

    def kv_arrive(kind, ch, slot):
        cols = tile_cols(ch)
        here = (kw if kind == 0 else vw).at[slot_rows(slot), cols]
        remote(here, here, kv_relay.at[kind, ch], kv_recv.at[kind, ch, slot], {"tm": sib}).wait_recv()

    def q_copy(n):
        device, slot = time_dests[n]
        return remote(
            qw.at[OWN], qw.at[slot_rows(slot)], q_send.at[n], q_recv.at[slot], {"tm": device}
        )

    def q_pass():
        return remote(
            qw.at[slot_rows(relay_from)],
            qw.at[slot_rows(relay_to)],
            q_relay.at[0],
            q_recv.at[relay_to],
            {"tm": sib},
        )

    def q_arrive(slot):
        here = qw.at[slot_rows(slot)]
        remote(here, here, q_relay.at[0], q_recv.at[slot], {"tm": sib}).wait_recv()

    def site_copy(n, src, dst, send, recv):
        return remote(
            src, dst.at[n * ROWS : (n + 1) * ROWS], send, recv, {"site": (up, down)[n]}
        )

    def out_copy(ch, n):
        cols = tile_cols(ch)
        return remote(
            ow.at[OWN, cols],
            ow.at[n * ROWS : (n + 1) * ROWS, cols],
            o_send.at[ch, n],
            o_recv.at[ch, n],
            {"site": (up, down)[n]},
        )

    def resid_copy(n):
        return site_copy(n, resid_hbm.at[0], rw, r_send.at[n], r_recv.at[n])

    def grad_copy(n):
        return site_copy(n, grad_hbm.at[0], gw, g_send.at[n], g_recv.at[n])

    def pack_copy(n):
        return site_copy(n, pkb.at[n * ROWS : (n + 1) * ROWS], prb, p_send.at[n], p_recv.at[n])

    def d_copy(kind, ch, n):
        device, slot = time_dests[n]
        cols = tile_cols(ch)
        buffer, size = ((dw, ROWS), (dl, 8))[kind]
        return remote(
            buffer.at[2 * size : 3 * size, cols],
            buffer.at[slot_rows(slot, size), cols],
            d_send.at[kind, ch, n],
            d_recv.at[kind, ch, slot],
            {"tm": device},
        )

    def d_pass(kind, ch):
        cols = tile_cols(ch)
        buffer, size = ((dw, ROWS), (dl, 8))[kind]
        return remote(
            buffer.at[slot_rows(relay_from, size), cols],
            buffer.at[slot_rows(relay_to, size), cols],
            d_relay.at[kind, ch],
            d_recv.at[kind, ch, relay_to],
            {"tm": sib},
        )

    def d_arrive(kind, ch, slot):
        cols = tile_cols(ch)
        buffer, size = ((dw, ROWS), (dl, 8))[kind]
        here = buffer.at[slot_rows(slot, size), cols]
        remote(here, here, d_relay.at[kind, ch], d_recv.at[kind, ch, slot], {"tm": sib}).wait_recv()

    pl.semaphore_wait(barrier, 6)
    for n in range(3):
        kv_copy(1, 0, n).start()
    for n in range(2):
        resid_copy(n).start()
    loads[0].wait()
    normalise(kraw, kw, rk_b, 1.0)
    for ch in range(CHUNKS):
        for kind in range(2) if ch == 0 else (1, 0):
            if (kind, ch) != (1, 0):
                for n in range(3):
                    kv_copy(kind, ch, n).start()
    for n in range(3):
        if n == 0:
            loads[1].wait()
            normalise(qraw, qw, rq_b, SCALE * LOG2E)
        q_copy(n).start()
    loads[2].wait()
    loads[3].wait()
    loads[5].wait()
    loads[7].wait()
    loads[8].wait()
    transpose(wo, 0, wo_t, 0, MODEL // TILE)
    loads[6].wait()

    def project_out(ch, first, count):
        rows = slice(first, first + count)
        squares = 0.0
        for n in range(MODEL // TILE):
            cols = tile_cols(n)
            before = rw[rows, cols].astype(F32) if ch == 0 else rsum[rows, cols]
            x = before + dot(ow[rows, tile_cols(ch)], wo[tile_cols(ch), cols])
            rsum[rows, cols] = x
            if ch == CHUNKS - 1:
                nb[rows, cols] = (x * gain_ref[cols][None, :]).astype(BF16)
                squares = squares + x[:, :SIZE] * x[:, :SIZE] + x[:, SIZE:] * x[:, SIZE:]
        if ch == CHUNKS - 1:
            mean = jnp.sum(squares, axis=-1, keepdims=True) * (1.0 / MODEL)
            inv_b[rows, :] = jnp.broadcast_to(lax.rsqrt(mean + EPSILON), (count, SIZE))

    def forward(ch):
        for kind in (1, 0):
            kv_arrive(kind, ch, relay_from)
            kv_pass(kind, ch).start()
        for slot in rest:
            for kind in range(2):
                kv_arrive(kind, ch, slot)
        for part in range(PER):
            h = ch * PER + part
            cols = head_cols(h)
            weights = (
                jnp.exp2(dot_nt(qw[OWN, cols], kw[:, cols])) * mask[...]
            ).astype(BF16)
            e_w[h] = weights
            inverse = 1.0 / jnp.sum(weights.astype(F32), axis=-1, keepdims=True)
            heads_out = dot(weights, vw[:, cols]) * inverse
            itot[:, cols] = jnp.broadcast_to(inverse, (ROWS, SIZE))
            out_f[:, cols] = heads_out
            ow[OWN, cols] = heads_out.astype(BF16)
        for n in range(2):
            out_copy(ch, n).start()
        project_out(ch, 2 * ROWS, ROWS)
        if ch < CHUNKS - 1:
            transpose(wqkv, ATT, wkv_t, 3 * ch, 3 * ch + 3)

    loop(CHUNKS, forward)
    for n in range(2):
        grad_copy(n).start()

    def project_q(first, count):
        rows = slice(first, first + count)

        def body(n):
            inverse = jnp.concatenate([inv_b[rows, :]] * 2, axis=1)
            qf[rows, tile_cols(n)] = dot(nb[rows, :], wqkv[:, tile_cols(n)]) * inverse

        loop(ATT // TILE, body)

    def project_kv(first, count):
        rows = slice(first, first + count)

        def body(n):
            inverse = jnp.concatenate([inv_b[rows, :]] * 2, axis=1)
            product = dot(nb[rows, :], wqkv[:, tile_cols(n, ATT)])
            kvb[rows, tile_cols(n)] = (product * inverse).astype(BF16)

        loop(2 * ATT // TILE, body)

    project_q(2 * ROWS, ROWS)
    project_kv(2 * ROWS, ROWS)
    loads[4].wait()

    first_named, second_named = nbr_ref[0, 0], nbr_ref[0, 1]
    seen = [
        jnp.where((first_named == peer) | (second_named == peer), 1.0, 0.0).astype(F32)
        for peer in (st - 1, st + 1)
    ]

    def site_key(h, x):
        return kvb[x * ROWS : (x + 1) * ROWS, head_cols(h)].astype(F32)

    def site_value(h, x):
        return kvb[x * ROWS : (x + 1) * ROWS, head_cols(h, ATT)].astype(F32)

    def head_sums(x):
        high = x.astype(BF16)
        low = (x - high.astype(F32)).astype(BF16)
        return dot(high, pool[...]) + dot(low, pool[...])

    def site_sums(rows, copies):
        keys = kvb[rows, :ATT].astype(F32)
        values = kvb[rows, ATT:].astype(F32)
        queries = jnp.concatenate([qf[OWN, :]] * copies, axis=0)
        grads = jnp.concatenate([gw[OWN, :].astype(F32)] * copies, axis=0)
        k_inv = lax.rsqrt(head_sums(keys * keys) * (1.0 / SIZE) + EPSILON)
        return k_inv, head_sums(queries * keys), head_sums(grads * values)

    q_inv = lax.rsqrt(head_sums(qf[OWN, :] * qf[OWN, :]) * (1.0 / SIZE) + EPSILON)
    own_sums = site_sums(OWN, 1)

    for n in range(2):
        resid_copy(n).wait_recv()
    for ch in range(CHUNKS):
        for n in range(2):
            out_copy(ch, n).wait_recv()
        project_out(ch, 0, 2 * ROWS)
    project_kv(0, 2 * ROWS)

    near_sums = site_sums(slice(0, 2 * ROWS), 2)
    k_inv, scores, dprobs = (
        [near[:ROWS], near[ROWS:], own] for near, own in zip(near_sums, own_sums)
    )
    scores = [s * (q_inv * r * SCALE) for s, r in zip(scores, k_inv)]
    exps = [jnp.exp(s) for s in scores]
    exps = [exps[0] * seen[0], exps[1] * seen[1], exps[2]]
    inverse = 1.0 / (exps[0] + exps[1] + exps[2])
    probs = [e * inverse for e in exps]
    rounded = [p.astype(BF16).astype(F32) for p in probs]
    delta = probs[0] * dprobs[0] + probs[1] * dprobs[1] + probs[2] * dprobs[2]
    dscores = [p * (d - delta) for p, d in zip(probs, dprobs)]
    along = [d * s for d, s in zip(dscores, scores)]
    scaled = [d * (q_inv * SCALE) for d in dscores]
    for n in range(2):
        x = 1 - n
        pack = 0.0
        for place, value in enumerate((scaled[x], along[x], rounded[x])):
            value = jnp.where(lane < HEADS, value, 0.0)
            pack = pack + (pltpu.roll(value, 8 * place, 1) if place else value)
        pkb[n * ROWS : (n + 1) * ROWS, :] = pack.astype(BF16)
        pack_copy(n).start()
    by_key = [d * r for d, r in zip(scaled, k_inv)]
    by_query = q_inv * q_inv * (along[0] + along[1] + along[2]) * (1.0 / SIZE)
    by_own_key = k_inv[2] * k_inv[2] * along[2] * (1.0 / SIZE)

    q_arrive(relay_from)
    q_pass().start()

    def site_head(h):
        cols = head_cols(h)
        q = qf[OWN, cols]
        keys = [site_key(h, x) for x in range(3)]
        values = [site_value(h, x) for x in range(3)]

        def of_head(compact):
            return compact[:, h : h + 1]

        weights = [of_head(w) for w in rounded]
        factors = [of_head(f) for f in by_key]
        dq = (
            factors[0] * keys[0]
            + factors[1] * keys[1]
            + factors[2] * keys[2]
            - of_head(by_query) * q
        )
        dqb[:, cols] = dq.astype(BF16)
        so_v[:, cols] = (
            weights[0] * values[0] + weights[1] * values[1] + weights[2] * values[2]
        ).astype(BF16)
        dkbase[:, cols] = factors[2] * q - of_head(by_own_key) * keys[2]
        dvbase[:, cols] = weights[2] * gw[OWN, cols].astype(F32)
        rko[:, cols] = jnp.broadcast_to(of_head(k_inv[2]), (ROWS, SIZE))

    loop(HEADS, site_head)

    def back_q(n):
        dn[:, tile_cols(n)] = dot_nt(dqb[...], wqkv[tile_cols(n), :ATT])

    loop(MODEL // TILE, back_q)
    project_q(0, 2 * ROWS)

    for slot in rest:
        q_arrive(slot)

    def key_side(h):
        cols = head_cols(h)
        et_w[h] = (jnp.exp2(dot_nt(kw[OWN, cols], qw[:, cols])) * mask[...]).astype(BF16)

    loop(HEADS, key_side)

    for n in range(2):
        grad_copy(n).wait_recv()
        pack_copy(n).wait_recv()

    def site_keys(h):
        cols = head_cols(h)
        spread = dot(prb[...], pick[:, 3 * h * SIZE : 3 * (h + 1) * SIZE])
        inverse = rko[:, cols]
        dkey, dvalue, along = dkbase[:, cols], dvbase[:, cols], 0.0
        gathered = 0.0
        for x in range(2):
            rows = slice(x * ROWS, (x + 1) * ROWS)
            gathered = gathered + spread[rows, :SIZE] * qf[rows, cols]
            along = along + spread[rows, SIZE : 2 * SIZE]
            dvalue = dvalue + spread[rows, 2 * SIZE :] * gw[rows, cols].astype(F32)
        own_key = kvb[OWN, cols].astype(F32)
        dkey = dkey + inverse * gathered - inverse * inverse * (1.0 / SIZE) * along * own_key
        dkv[:, cols] = dkey.astype(BF16)
        dkv[:, head_cols(h, ATT)] = dvalue.astype(BF16)

    loop(HEADS, site_keys)

    product = 0.0
    for n in range(MODEL // TILE):
        cols = tile_cols(n)
        gained = gain_ref[cols][None, :] * (dn[:, cols] + dot(dkv[...], wkv_t[:, cols]))
        dn[:, cols] = gained
        both = rsum[OWN, cols] * gained
        product = product + both[:, :SIZE] + both[:, SIZE:]
    average = jnp.sum(product, axis=-1, keepdims=True) * (1.0 / MODEL)
    inverse = inv_b[OWN, :]
    factor = inverse * inverse * inverse * average
    inverse = jnp.concatenate([inverse] * 2, axis=1)
    factor = jnp.concatenate([factor] * 2, axis=1)
    for n in range(MODEL // TILE):
        cols = tile_cols(n)
        gr_v[:, cols] = (inverse * dn[:, cols] - rsum[OWN, cols] * factor).astype(BF16)

    def back_out(ch):
        cols = tile_cols(ch)
        d_rows = (dot(gr_v[...], wo_t[:, cols]) * itot[:, cols]).astype(BF16)
        dw[OWN, cols] = d_rows
        for n in range(3):
            d_copy(0, ch, n).start()
        product = out_f[:, cols] * d_rows.astype(F32)
        high = product.astype(BF16)
        low = (product - high.astype(F32)).astype(BF16)
        ones = jnp.ones((8, SIZE), BF16)
        kept = lax.broadcasted_iota(jnp.int32, (8, SIZE), 0)
        for part in range(PER):
            cut = slice(part * SIZE, (part + 1) * SIZE)
            here = head_cols(ch * PER + part)
            total = jnp.sum(product[:, cut], axis=-1, keepdims=True)
            dcol[:, here] = jnp.broadcast_to(total, (ROWS, SIZE))
            line = dot_nt(ones, high[:, cut]) + dot_nt(ones, low[:, cut])
            top = line.astype(BF16).astype(F32)
            dl[16:24, here] = jnp.where(
                kept == 0, top, jnp.where(kept == 1, line - top, 0.0)
            ).astype(BF16)
        for n in range(3):
            d_copy(1, ch, n).start()

    loop(CHUNKS, back_out)

    def query_side(ch):
        for part in range(PER):
            h = ch * PER + part
            cols = head_cols(h)
            dprobs = dot_nt(dw[OWN, cols], vw[:, cols])
            dscores = e_w[h].astype(F32) * (dprobs - dcol[:, cols][:, :1])
            grads = dot(dscores.astype(BF16), kw[:, cols]) * SCALE
            inverse = rq_b[:, cols]
            normed = qraw[:, cols].astype(F32) * inverse
            gq_v[:, cols] = (inverse * (grads - normed * lane_mean(normed * grads))).astype(BF16)
        for kind in range(2):
            d_arrive(kind, ch, relay_from)
            d_pass(kind, ch).start()

    loop(CHUNKS, query_side)

    def key_grads(ch):
        for slot in rest:
            for kind in range(2):
                d_arrive(kind, ch, slot)
        for part in range(PER):
            h = ch * PER + part
            cols = head_cols(h)
            d_rows = dw[:, cols]
            lines = []
            for slot in range(SLOTS):
                line = dl[slot * 8 : (slot + 1) * 8, cols].astype(F32)
                lines.append(line[0:1] + line[1:2])
            weights = et_w[h]
            dprobs = dot_nt(vw[OWN, cols], d_rows)
            dscores = weights.astype(F32) * (dprobs - jnp.concatenate(lines, axis=1))
            grads = dot(dscores.astype(BF16), qw[:, cols]) * LN2
            inverse = rk_b[:, cols]
            normed = kraw[:, cols].astype(F32) * inverse
            gk_v[:, cols] = (inverse * (grads - normed * lane_mean(normed * grads))).astype(BF16)
            gv_v[:, cols] = dot(weights, d_rows).astype(BF16)

    loop(CHUNKS, key_grads)

    for ch in range(CHUNKS):
        for kind in range(2):
            for n in range(3):
                kv_copy(kind, ch, n).wait_send()
                d_copy(kind, ch, n).wait_send()
            kv_pass(kind, ch).wait_send()
            d_pass(kind, ch).wait_send()
        for n in range(2):
            out_copy(ch, n).wait_send()
    for n in range(3):
        q_copy(n).wait_send()
    q_pass().wait_send()
    for n in range(2):
        resid_copy(n).wait_send()
        grad_copy(n).wait_send()
        pack_copy(n).wait_send()


def hand_over(*refs):
    sems = refs[-1]
    count = len(refs) // 2
    copies = [
        pltpu.make_async_copy(refs[n], refs[count + n], sems.at[n]) for n in range(count)
    ]
    for copy in copies:
        copy.start()
    for copy in copies:
        copy.wait()


def shards(tm_count, site_count, q_time, k_time, v_time, resid, w_out_time, norm_gain, w_qkv_site, grad_site, nbr_blocks):
    assert q_time.shape == (1, ROWS, ATT) and resid.shape == (1, ROWS, MODEL)
    anywhere = pl.BlockSpec(memory_space=pl.ANY)
    narrow = jax.ShapeDtypeStruct((1, ROWS, ATT), BF16)
    wide = jax.ShapeDtypeStruct((1, ROWS, MODEL), BF16)
    vmem = pltpu.VMEM
    dma = pltpu.SemaphoreType.DMA
    results = pl.pallas_call(
        functools.partial(kernel, tm_count, site_count),
        out_shape=(narrow, narrow, narrow, narrow, wide),
        in_specs=[pl.BlockSpec(memory_space=pltpu.HBM)] * 9,
        out_specs=(pl.BlockSpec(memory_space=pltpu.VMEM),) * 5,
        scratch_shapes=[
            pltpu.SMEM((1, 2), jnp.int32),
            vmem((MODEL,), F32),
            vmem((ROWS, ATT), BF16),
            vmem((ROWS, ATT), BF16),
            vmem((WINDOW, ATT), BF16),
            vmem((WINDOW, ATT), BF16),
            vmem((WINDOW, ATT), BF16),
            vmem((WINDOW, ATT), BF16),
            vmem((SLOTS * 8, ATT), BF16),
            vmem((ROWS, WINDOW), F32),
            vmem((ROWS, ATT), F32),
            vmem((ROWS, ATT), F32),
            vmem((ROWS, ATT), F32),
            vmem((ROWS, ATT), F32),
            vmem((ROWS, ATT), F32),
            vmem((HEADS, ROWS, WINDOW), BF16),
            vmem((HEADS, ROWS, WINDOW), BF16),
            vmem((3 * ROWS, ATT), BF16),
            vmem((3 * ROWS, MODEL), BF16),
            vmem((3 * ROWS, ATT), BF16),
            vmem((ATT, MODEL), BF16),
            vmem((MODEL, 3 * ATT), BF16),
            vmem((TILE, TILE), BF16),
            vmem((MODEL, ATT), BF16),
            vmem((2 * ATT, MODEL), BF16),
            vmem((3 * ROWS, MODEL), F32),
            vmem((3 * ROWS, SIZE), F32),
            vmem((3 * ROWS, MODEL), BF16),
            vmem((3 * ROWS, ATT), F32),
            vmem((3 * ROWS, 2 * ATT), BF16),
            vmem((SIZE, 3 * ATT), BF16),
            vmem((ATT, SIZE), BF16),
            vmem((2 * ROWS, SIZE), BF16),
            vmem((2 * ROWS, SIZE), BF16),
            vmem((ROWS, ATT), BF16),
            vmem((ROWS, ATT), F32),
            vmem((ROWS, ATT), F32),
            vmem((ROWS, ATT), F32),
            vmem((ROWS, 2 * ATT), BF16),
            vmem((ROWS, MODEL), F32),
            dma((9,)),
            dma((2, CHUNKS, 3)),
            dma((2, CHUNKS, SLOTS)),
            dma((2, CHUNKS)),
            dma((3,)),
            dma((SLOTS,)),
            dma((1,)),
            dma((2,)),
            dma((2,)),
            dma((2,)),
            dma((2,)),
            dma((CHUNKS, 2)),
            dma((CHUNKS, 2)),
            dma((2,)),
            dma((2,)),
            dma((2, CHUNKS, 3)),
            dma((2, CHUNKS, SLOTS)),
            dma((2, CHUNKS)),
        ],
        compiler_params=pltpu.CompilerParams(
            collective_id=0, has_side_effects=True, vmem_limit_bytes=48 * 1024 * 1024
        ),
    )(
        *(
            pltpu.with_memory_space_constraint(x, pltpu.HBM)
            for x in (nbr_blocks, norm_gain, q_time, k_time, v_time, resid, w_out_time, w_qkv_site, grad_site)
        ),
    )
    return pl.pallas_call(
        hand_over,
        out_shape=(narrow, narrow, narrow, narrow, wide),
        in_specs=[anywhere] * 5,
        out_specs=(anywhere,) * 5,
        scratch_shapes=[dma((5,))],
        compiler_params=pltpu.CompilerParams(vmem_limit_bytes=1024 * 1024),
    )(*results)


def solution(mesh):
    rows = P("site", "tm", None)
    return jax.shard_map(
        functools.partial(shards, mesh.shape["tm"], mesh.shape["site"]),
        mesh=mesh,
        in_specs=(rows, rows, rows, rows, P(), P(), P(), rows, P("site", None)),
        out_specs=(rows,) * 5,
        check_vma=False,
    )
```

```python
import functools

import jax
import jax.numpy as jnp
from jax import lax
from jax.experimental import pallas as pl
from jax.experimental.pallas import tpu as pltpu
from jax.sharding import PartitionSpec as P

HEADS = 6
SIZE = 128
ROWS = 128
ATT = HEADS * SIZE
MODEL = 1536
EPSILON = 1e-05
SCALE = SIZE ** (-0.5)
LOG2E = 1.4426950408889634
LN2 = 0.6931471805599453
SLOTS = 5
WINDOW = SLOTS * ROWS
CHUNKS = 3
WIDTH = ATT // CHUNKS
PER = HEADS // CHUNKS
TILE = 256
BLOCK = 32
F32 = jnp.float32
BF16 = jnp.bfloat16
MESH = pl.DeviceIdType.MESH
OWN = slice(2 * ROWS, 3 * ROWS)


def dot(a, b):
    return jnp.dot(a, b, preferred_element_type=F32)


def dot_nt(a, b):
    return lax.dot_general(a, b, (((1,), (1,)), ((), ())), preferred_element_type=F32)


def lane_mean(x):
    return jnp.sum(x, axis=-1, keepdims=True) * (1.0 / x.shape[-1])


def head_cols(h, base=0):
    return slice(h * SIZE + base, (h + 1) * SIZE + base)


def tile_cols(n, base=0):
    return slice(n * TILE + base, (n + 1) * TILE + base)


def loop(count, body):
    for i in range(count):
        body(i)


def kernel(
    tm_count,
    site_count,
    nbr_hbm,
    gain_hbm,
    q_hbm,
    k_hbm,
    v_hbm,
    resid_hbm,
    wo_hbm,
    wqkv_hbm,
    grad_hbm,
    so_out,
    gq_out,
    gk_out,
    gv_out,
    gr_out,
    nbr_ref,
    gain_ref,
    qraw,
    kraw,
    qw,
    kw,
    vw,
    dw,
    dl,
    mask,
    rq_b,
    rk_b,
    itot,
    out_f,
    dcol,
    e_w,
    et_w,
    ow,
    rw,
    gw,
    wo,
    wqkv,
    eye,
    wo_t,
    wkv_t,
    rsum,
    inv_b,
    nb,
    qf,
    kvb,
    pick,
    pool,
    pkb,
    prb,
    dqb,
    dkbase,
    dvbase,
    rko,
    dkv,
    dn,
    load_sem,
    kv_send,
    kv_recv,
    kv_relay,
    q_send,
    q_recv,
    q_relay,
    r_send,
    r_recv,
    g_send,
    g_recv,
    o_send,
    o_recv,
    p_send,
    p_recv,
    d_send,
    d_recv,
    d_relay,
):
    so_v, gq_v, gk_v, gv_v, gr_v = (ref.at[0] for ref in (so_out, gq_out, gk_out, gv_out, gr_out))
    tm = lax.axis_index("tm")
    st = lax.axis_index("site")
    core = lax.rem(tm, 2)
    sib = tm + 1 - 2 * core
    right_chip = lax.rem(tm + 2 - core, tm_count)
    left_chip = lax.rem(tm - 1 - core + tm_count, tm_count)
    up = lax.rem(st + 1, site_count)
    down = lax.rem(st + site_count - 1, site_count)
    time_dests = ((right_chip, core), (left_chip, 3 + core), (sib, 1 + 2 * core))
    relay_from = 1 + 2 * core
    relay_to = 4 * core
    rest = (4 * core, 3 - 2 * core, 4 - 4 * core)

    loads = [
        pltpu.make_async_copy(src, dst, load_sem.at[n])
        for n, (src, dst) in enumerate(
            (
                (k_hbm.at[0], kraw),
                (q_hbm.at[0], qraw),
                (v_hbm.at[0], vw.at[OWN]),
                (resid_hbm.at[0], rw.at[OWN]),
                (grad_hbm.at[0], gw.at[OWN]),
                (wo_hbm, wo),
                (wqkv_hbm, wqkv),
                (gain_hbm, gain_ref),
                (nbr_hbm, nbr_ref),
            )
        )
    ]
    for copy in loads:
        copy.start()

    barrier = pltpu.get_barrier_semaphore()
    for offset in (1, 2, tm_count - 1, tm_count - 2):
        pl.semaphore_signal(
            barrier, inc=1, device_id={"tm": lax.rem(tm + offset, tm_count)}, device_id_type=MESH
        )
    for peer in (up, down):
        pl.semaphore_signal(barrier, inc=1, device_id={"site": peer}, device_id_type=MESH)

    row = lax.broadcasted_iota(jnp.int32, (ROWS, ROWS), 0)
    lane = lax.broadcasted_iota(jnp.int32, (ROWS, ROWS), 1)
    for slot in range(SLOTS):
        shard = tm + slot - 2
        valid = jnp.where((shard >= 0) & (shard < tm_count), 1.0, 0.0).astype(F32)
        if slot == 0:
            band = jnp.where(lane >= row, valid, 0.0)
        elif slot == SLOTS - 1:
            band = jnp.where(lane <= row, valid, 0.0)
        else:
            band = jnp.full((ROWS, ROWS), valid, F32)
        mask[:, slot * ROWS : (slot + 1) * ROWS] = band

    for h in range(HEADS):
        for n in range(3):
            pick[:, head_cols(3 * h + n)] = jnp.where(row == 8 * n + h, 1.0, 0.0).astype(BF16)

    for h in range(HEADS):
        pool[head_cols(h), :] = jnp.where(lane == h, 1.0, 0.0).astype(BF16)

    def normalise(raw, store, inverse, factor):
        def body(h):
            cols = head_cols(h)
            x = raw[:, cols].astype(F32)
            r = lax.rsqrt(lane_mean(x * x) + EPSILON)
            inverse[:, cols] = jnp.broadcast_to(r, (ROWS, SIZE))
            store[OWN, cols] = (x * (r * factor)).astype(BF16)

        loop(HEADS, body)

    wide_row = lax.broadcasted_iota(jnp.int32, (TILE, TILE), 0)
    wide_lane = lax.broadcasted_iota(jnp.int32, (TILE, TILE), 1)
    eye[...] = jnp.where(wide_row == wide_lane, 1.0, 0.0).astype(BF16)

    def transpose(source, base, target, first, last):
        def body(n, carry):
            rows = pl.ds(pl.multiple_of(n * TILE, TILE), TILE)
            cols = pl.ds(pl.multiple_of(n * TILE + base, TILE), TILE)
            target[rows, :] = dot_nt(eye[...], source[:, cols]).astype(BF16)
            return carry

        lax.fori_loop(first, last, body, 0)

    def remote(src, dst, send, recv, device):
        return pltpu.make_async_remote_copy(
            src_ref=src,
            dst_ref=dst,
            send_sem=send,
            recv_sem=recv,
            device_id=device,
            device_id_type=MESH,
        )

    def slot_rows(slot, size=ROWS):
        return pl.ds(pl.multiple_of(slot * size, size), size)

    def kv_copy(kind, ch, n):
        device, slot = time_dests[n]
        cols = tile_cols(ch)
        src = kw.at[OWN, cols] if kind == 0 else v_hbm.at[0, :, cols]
        dst = (kw if kind == 0 else vw).at[slot_rows(slot), cols]
        return remote(
            src, dst, kv_send.at[kind, ch, n], kv_recv.at[kind, ch, slot], {"tm": device}
        )

    def kv_pass(kind, ch):
        cols = tile_cols(ch)
        buffer = kw if kind == 0 else vw
        return remote(
            buffer.at[slot_rows(relay_from), cols],
            buffer.at[slot_rows(relay_to), cols],
            kv_relay.at[kind, ch],
            kv_recv.at[kind, ch, relay_to],
            {"tm": sib},
        )

    def kv_arrive(kind, ch, slot):
        cols = tile_cols(ch)
        here = (kw if kind == 0 else vw).at[slot_rows(slot), cols]
        remote(here, here, kv_relay.at[kind, ch], kv_recv.at[kind, ch, slot], {"tm": sib}).wait_recv()

    def q_copy(n):
        device, slot = time_dests[n]
        return remote(
            qw.at[OWN], qw.at[slot_rows(slot)], q_send.at[n], q_recv.at[slot], {"tm": device}
        )

    def q_pass():
        return remote(
            qw.at[slot_rows(relay_from)],
            qw.at[slot_rows(relay_to)],
            q_relay.at[0],
            q_recv.at[relay_to],
            {"tm": sib},
        )

    def q_arrive(slot):
        here = qw.at[slot_rows(slot)]
        remote(here, here, q_relay.at[0], q_recv.at[slot], {"tm": sib}).wait_recv()

    def site_copy(n, src, dst, send, recv):
        return remote(
            src, dst.at[n * ROWS : (n + 1) * ROWS], send, recv, {"site": (up, down)[n]}
        )

    def out_copy(ch, n):
        cols = tile_cols(ch)
        return remote(
            ow.at[OWN, cols],
            ow.at[n * ROWS : (n + 1) * ROWS, cols],
            o_send.at[ch, n],
            o_recv.at[ch, n],
            {"site": (up, down)[n]},
        )

    def resid_copy(n):
        return site_copy(n, resid_hbm.at[0], rw, r_send.at[n], r_recv.at[n])

    def grad_copy(n):
        return site_copy(n, grad_hbm.at[0], gw, g_send.at[n], g_recv.at[n])

    def pack_copy(n):
        return site_copy(n, pkb.at[n * ROWS : (n + 1) * ROWS], prb, p_send.at[n], p_recv.at[n])

    def d_copy(kind, ch, n):
        device, slot = time_dests[n]
        cols = tile_cols(ch)
        buffer, size = ((dw, ROWS), (dl, 8))[kind]
        return remote(
            buffer.at[2 * size : 3 * size, cols],
            buffer.at[slot_rows(slot, size), cols],
            d_send.at[kind, ch, n],
            d_recv.at[kind, ch, slot],
            {"tm": device},
        )

    def d_pass(kind, ch):
        cols = tile_cols(ch)
        buffer, size = ((dw, ROWS), (dl, 8))[kind]
        return remote(
            buffer.at[slot_rows(relay_from, size), cols],
            buffer.at[slot_rows(relay_to, size), cols],
            d_relay.at[kind, ch],
            d_recv.at[kind, ch, relay_to],
            {"tm": sib},
        )

    def d_arrive(kind, ch, slot):
        cols = tile_cols(ch)
        buffer, size = ((dw, ROWS), (dl, 8))[kind]
        here = buffer.at[slot_rows(slot, size), cols]
        remote(here, here, d_relay.at[kind, ch], d_recv.at[kind, ch, slot], {"tm": sib}).wait_recv()

    pl.semaphore_wait(barrier, 6)
    for n in range(3):
        kv_copy(1, 0, n).start()
    for n in range(2):
        resid_copy(n).start()
    loads[0].wait()
    normalise(kraw, kw, rk_b, 1.0)
    for ch in range(CHUNKS):
        for kind in range(2) if ch == 0 else (1, 0):
            if (kind, ch) != (1, 0):
                for n in range(3):
                    kv_copy(kind, ch, n).start()
    for n in range(3):
        if n == 0:
            loads[1].wait()
            normalise(qraw, qw, rq_b, SCALE * LOG2E)
        q_copy(n).start()
    loads[2].wait()
    loads[3].wait()
    loads[5].wait()
    loads[7].wait()
    loads[8].wait()
    transpose(wo, 0, wo_t, 0, MODEL // TILE)
    loads[6].wait()

    def project_out(ch, first, count):
        rows = slice(first, first + count)
        squares = 0.0
        for n in range(MODEL // TILE):
            cols = tile_cols(n)
            before = rw[rows, cols].astype(F32) if ch == 0 else rsum[rows, cols]
            x = before + dot(ow[rows, tile_cols(ch)], wo[tile_cols(ch), cols])
            rsum[rows, cols] = x
            if ch == CHUNKS - 1:
                nb[rows, cols] = (x * gain_ref[cols][None, :]).astype(BF16)
                squares = squares + x[:, :SIZE] * x[:, :SIZE] + x[:, SIZE:] * x[:, SIZE:]
        if ch == CHUNKS - 1:
            mean = jnp.sum(squares, axis=-1, keepdims=True) * (1.0 / MODEL)
            inv_b[rows, :] = jnp.broadcast_to(lax.rsqrt(mean + EPSILON), (count, SIZE))

    def forward(ch):
        for kind in (1, 0):
            kv_arrive(kind, ch, relay_from)
            kv_pass(kind, ch).start()
        for slot in rest:
            for kind in range(2):
                kv_arrive(kind, ch, slot)
        for part in range(PER):
            h = ch * PER + part
            cols = head_cols(h)
            weights = (
                jnp.exp2(dot_nt(qw[OWN, cols], kw[:, cols])) * mask[...]
            ).astype(BF16)
            e_w[h] = weights
            inverse = 1.0 / jnp.sum(weights.astype(F32), axis=-1, keepdims=True)
            heads_out = dot(weights, vw[:, cols]) * inverse
            itot[:, cols] = jnp.broadcast_to(inverse, (ROWS, SIZE))
            out_f[:, cols] = heads_out
            ow[OWN, cols] = heads_out.astype(BF16)
        for n in range(2):
            out_copy(ch, n).start()
        project_out(ch, 2 * ROWS, ROWS)
        if ch < CHUNKS - 1:
            transpose(wqkv, ATT, wkv_t, 3 * ch, 3 * ch + 3)

    loop(CHUNKS, forward)
    for n in range(2):
        grad_copy(n).start()

    def project_q(first, count):
        rows = slice(first, first + count)

        def body(n):
            inverse = jnp.concatenate([inv_b[rows, :]] * 2, axis=1)
            qf[rows, tile_cols(n)] = dot(nb[rows, :], wqkv[:, tile_cols(n)]) * inverse

        loop(ATT // TILE, body)

    def project_kv(first, count):
        rows = slice(first, first + count)

        def body(n):
            inverse = jnp.concatenate([inv_b[rows, :]] * 2, axis=1)
            product = dot(nb[rows, :], wqkv[:, tile_cols(n, ATT)])
            kvb[rows, tile_cols(n)] = (product * inverse).astype(BF16)

        loop(2 * ATT // TILE, body)

    project_q(2 * ROWS, ROWS)
    project_kv(2 * ROWS, ROWS)
    loads[4].wait()

    first_named, second_named = nbr_ref[0, 0], nbr_ref[0, 1]
    seen = [
        jnp.where((first_named == peer) | (second_named == peer), 1.0, 0.0).astype(F32)
        for peer in (st - 1, st + 1)
    ]

    def site_key(h, x):
        return kvb[x * ROWS : (x + 1) * ROWS, head_cols(h)].astype(F32)

    def site_value(h, x):
        return kvb[x * ROWS : (x + 1) * ROWS, head_cols(h, ATT)].astype(F32)

    def head_sums(x):
        high = x.astype(BF16)
        low = (x - high.astype(F32)).astype(BF16)
        return dot(high, pool[...]) + dot(low, pool[...])

    def site_sums(rows, copies):
        keys = kvb[rows, :ATT].astype(F32)
        values = kvb[rows, ATT:].astype(F32)
        queries = jnp.concatenate([qf[OWN, :]] * copies, axis=0)
        grads = jnp.concatenate([gw[OWN, :].astype(F32)] * copies, axis=0)
        k_inv = lax.rsqrt(head_sums(keys * keys) * (1.0 / SIZE) + EPSILON)
        return k_inv, head_sums(queries * keys), head_sums(grads * values)

    q_inv = lax.rsqrt(head_sums(qf[OWN, :] * qf[OWN, :]) * (1.0 / SIZE) + EPSILON)
    own_sums = site_sums(OWN, 1)

    for n in range(2):
        resid_copy(n).wait_recv()
    for ch in range(CHUNKS):
        for n in range(2):
            out_copy(ch, n).wait_recv()
        project_out(ch, 0, 2 * ROWS)
    project_kv(0, 2 * ROWS)

    near_sums = site_sums(slice(0, 2 * ROWS), 2)
    k_inv, scores, dprobs = (
        [near[:ROWS], near[ROWS:], own] for near, own in zip(near_sums, own_sums)
    )
    scores = [s * (q_inv * r * SCALE) for s, r in zip(scores, k_inv)]
    exps = [jnp.exp(s) for s in scores]
    exps = [exps[0] * seen[0], exps[1] * seen[1], exps[2]]
    inverse = 1.0 / (exps[0] + exps[1] + exps[2])
    probs = [e * inverse for e in exps]
    rounded = [p.astype(BF16).astype(F32) for p in probs]
    delta = probs[0] * dprobs[0] + probs[1] * dprobs[1] + probs[2] * dprobs[2]
    dscores = [p * (d - delta) for p, d in zip(probs, dprobs)]
    along = [d * s for d, s in zip(dscores, scores)]
    scaled = [d * (q_inv * SCALE) for d in dscores]
    for n in range(2):
        x = 1 - n
        pack = 0.0
        for place, value in enumerate((scaled[x], along[x], rounded[x])):
            value = jnp.where(lane < HEADS, value, 0.0)
            pack = pack + (pltpu.roll(value, 8 * place, 1) if place else value)
        pkb[n * ROWS : (n + 1) * ROWS, :] = pack.astype(BF16)
        pack_copy(n).start()
    by_key = [d * r for d, r in zip(scaled, k_inv)]
    by_query = q_inv * q_inv * (along[0] + along[1] + along[2]) * (1.0 / SIZE)
    by_own_key = k_inv[2] * k_inv[2] * along[2] * (1.0 / SIZE)

    q_arrive(relay_from)
    q_pass().start()

    def site_head(h):
        cols = head_cols(h)
        q = qf[OWN, cols]
        keys = [site_key(h, x) for x in range(3)]
        values = [site_value(h, x) for x in range(3)]

        def of_head(compact):
            return compact[:, h : h + 1]

        weights = [of_head(w) for w in rounded]
        factors = [of_head(f) for f in by_key]
        dq = (
            factors[0] * keys[0]
            + factors[1] * keys[1]
            + factors[2] * keys[2]
            - of_head(by_query) * q
        )
        dqb[:, cols] = dq.astype(BF16)
        so_v[:, cols] = (
            weights[0] * values[0] + weights[1] * values[1] + weights[2] * values[2]
        ).astype(BF16)
        dkbase[:, cols] = factors[2] * q - of_head(by_own_key) * keys[2]
        dvbase[:, cols] = weights[2] * gw[OWN, cols].astype(F32)
        rko[:, cols] = jnp.broadcast_to(of_head(k_inv[2]), (ROWS, SIZE))

    loop(HEADS, site_head)

    def back_q(n):
        dn[:, tile_cols(n)] = dot_nt(dqb[...], wqkv[tile_cols(n), :ATT])

    loop(MODEL // TILE, back_q)
    project_q(0, 2 * ROWS)

    for slot in rest:
        q_arrive(slot)

    def key_side(h):
        cols = head_cols(h)
        et_w[h] = (jnp.exp2(dot_nt(kw[OWN, cols], qw[:, cols])) * mask[...]).astype(BF16)

    loop(HEADS, key_side)

    for n in range(2):
        grad_copy(n).wait_recv()
        pack_copy(n).wait_recv()

    def site_keys(h):
        cols = head_cols(h)
        spread = dot(prb[...], pick[:, 3 * h * SIZE : 3 * (h + 1) * SIZE])
        inverse = rko[:, cols]
        dkey, dvalue, along = dkbase[:, cols], dvbase[:, cols], 0.0
        gathered = 0.0
        for x in range(2):
            rows = slice(x * ROWS, (x + 1) * ROWS)
            gathered = gathered + spread[rows, :SIZE] * qf[rows, cols]
            along = along + spread[rows, SIZE : 2 * SIZE]
            dvalue = dvalue + spread[rows, 2 * SIZE :] * gw[rows, cols].astype(F32)
        own_key = kvb[OWN, cols].astype(F32)
        dkey = dkey + inverse * gathered - inverse * inverse * (1.0 / SIZE) * along * own_key
        dkv[:, cols] = dkey.astype(BF16)
        dkv[:, head_cols(h, ATT)] = dvalue.astype(BF16)

    loop(HEADS, site_keys)

    product = 0.0
    for n in range(MODEL // TILE):
        cols = tile_cols(n)
        gained = gain_ref[cols][None, :] * (dn[:, cols] + dot(dkv[...], wkv_t[:, cols]))
        dn[:, cols] = gained
        both = rsum[OWN, cols] * gained
        product = product + both[:, :SIZE] + both[:, SIZE:]
    average = jnp.sum(product, axis=-1, keepdims=True) * (1.0 / MODEL)
    inverse = inv_b[OWN, :]
    factor = inverse * inverse * inverse * average
    inverse = jnp.concatenate([inverse] * 2, axis=1)
    factor = jnp.concatenate([factor] * 2, axis=1)
    for n in range(MODEL // TILE):
        cols = tile_cols(n)
        gr_v[:, cols] = (inverse * dn[:, cols] - rsum[OWN, cols] * factor).astype(BF16)

    def back_out(ch):
        cols = tile_cols(ch)
        d_rows = (dot(gr_v[...], wo_t[:, cols]) * itot[:, cols]).astype(BF16)
        dw[OWN, cols] = d_rows
        for n in range(3):
            d_copy(0, ch, n).start()
        product = out_f[:, cols] * d_rows.astype(F32)
        high = product.astype(BF16)
        low = (product - high.astype(F32)).astype(BF16)
        ones = jnp.ones((8, SIZE), BF16)
        kept = lax.broadcasted_iota(jnp.int32, (8, SIZE), 0)
        for part in range(PER):
            cut = slice(part * SIZE, (part + 1) * SIZE)
            here = head_cols(ch * PER + part)
            total = jnp.sum(product[:, cut], axis=-1, keepdims=True)
            dcol[:, here] = jnp.broadcast_to(total, (ROWS, SIZE))
            line = dot_nt(ones, high[:, cut]) + dot_nt(ones, low[:, cut])
            top = line.astype(BF16).astype(F32)
            dl[16:24, here] = jnp.where(
                kept == 0, top, jnp.where(kept == 1, line - top, 0.0)
            ).astype(BF16)
        for n in range(3):
            d_copy(1, ch, n).start()

    loop(CHUNKS, back_out)

    def query_side(ch):
        for part in range(PER):
            h = ch * PER + part
            cols = head_cols(h)
            dprobs = dot_nt(dw[OWN, cols], vw[:, cols])
            dscores = e_w[h].astype(F32) * (dprobs - dcol[:, cols][:, :1])
            grads = dot(dscores.astype(BF16), kw[:, cols]) * SCALE
            inverse = rq_b[:, cols]
            normed = qraw[:, cols].astype(F32) * inverse
            gq_v[:, cols] = (inverse * (grads - normed * lane_mean(normed * grads))).astype(BF16)

    loop(CHUNKS, query_side)

    def relay_grads(ch):
        for kind in range(2):
            d_arrive(kind, ch, relay_from)
            d_pass(kind, ch).start()


    def key_grads(ch):
        for slot in rest:
            for kind in range(2):
                d_arrive(kind, ch, slot)
        for part in range(PER):
            h = ch * PER + part
            cols = head_cols(h)
            d_rows = dw[:, cols]
            lines = []
            for slot in range(SLOTS):
                line = dl[slot * 8 : (slot + 1) * 8, cols].astype(F32)
                lines.append(line[0:1] + line[1:2])
            weights = et_w[h]
            dprobs = dot_nt(vw[OWN, cols], d_rows)
            dscores = weights.astype(F32) * (dprobs - jnp.concatenate(lines, axis=1))
            grads = dot(dscores.astype(BF16), qw[:, cols]) * LN2
            inverse = rk_b[:, cols]
            normed = kraw[:, cols].astype(F32) * inverse
            gk_v[:, cols] = (inverse * (grads - normed * lane_mean(normed * grads))).astype(BF16)
            gv_v[:, cols] = dot(weights, d_rows).astype(BF16)

    relay_grads(0)
    for ch in range(1, CHUNKS):
        relay_grads(ch)
        if ch < CHUNKS - 1:
            key_grads(ch - 1)
            key_grads(ch)
    key_grads(CHUNKS - 1)

    for ch in range(CHUNKS):
        for kind in range(2):
            for n in range(3):
                kv_copy(kind, ch, n).wait_send()
                d_copy(kind, ch, n).wait_send()
            kv_pass(kind, ch).wait_send()
            d_pass(kind, ch).wait_send()
        for n in range(2):
            out_copy(ch, n).wait_send()
    for n in range(3):
        q_copy(n).wait_send()
    q_pass().wait_send()
    for n in range(2):
        resid_copy(n).wait_send()
        grad_copy(n).wait_send()
        pack_copy(n).wait_send()


def hand_over(*refs):
    sems = refs[-1]
    count = len(refs) // 2
    copies = [
        pltpu.make_async_copy(refs[n], refs[count + n], sems.at[n]) for n in range(count)
    ]
    for copy in copies:
        copy.start()
    for copy in copies:
        copy.wait()


def shards(tm_count, site_count, q_time, k_time, v_time, resid, w_out_time, norm_gain, w_qkv_site, grad_site, nbr_blocks):
    assert q_time.shape == (1, ROWS, ATT) and resid.shape == (1, ROWS, MODEL)
    anywhere = pl.BlockSpec(memory_space=pl.ANY)
    narrow = jax.ShapeDtypeStruct((1, ROWS, ATT), BF16)
    wide = jax.ShapeDtypeStruct((1, ROWS, MODEL), BF16)
    vmem = pltpu.VMEM
    dma = pltpu.SemaphoreType.DMA
    results = pl.pallas_call(
        functools.partial(kernel, tm_count, site_count),
        out_shape=(narrow, narrow, narrow, narrow, wide),
        in_specs=[pl.BlockSpec(memory_space=pltpu.HBM)] * 9,
        out_specs=(pl.BlockSpec(memory_space=pltpu.VMEM),) * 5,
        scratch_shapes=[
            pltpu.SMEM((1, 2), jnp.int32),
            vmem((MODEL,), F32),
            vmem((ROWS, ATT), BF16),
            vmem((ROWS, ATT), BF16),
            vmem((WINDOW, ATT), BF16),
            vmem((WINDOW, ATT), BF16),
            vmem((WINDOW, ATT), BF16),
            vmem((WINDOW, ATT), BF16),
            vmem((SLOTS * 8, ATT), BF16),
            vmem((ROWS, WINDOW), F32),
            vmem((ROWS, ATT), F32),
            vmem((ROWS, ATT), F32),
            vmem((ROWS, ATT), F32),
            vmem((ROWS, ATT), F32),
            vmem((ROWS, ATT), F32),
            vmem((HEADS, ROWS, WINDOW), BF16),
            vmem((HEADS, ROWS, WINDOW), BF16),
            vmem((3 * ROWS, ATT), BF16),
            vmem((3 * ROWS, MODEL), BF16),
            vmem((3 * ROWS, ATT), BF16),
            vmem((ATT, MODEL), BF16),
            vmem((MODEL, 3 * ATT), BF16),
            vmem((TILE, TILE), BF16),
            vmem((MODEL, ATT), BF16),
            vmem((2 * ATT, MODEL), BF16),
            vmem((3 * ROWS, MODEL), F32),
            vmem((3 * ROWS, SIZE), F32),
            vmem((3 * ROWS, MODEL), BF16),
            vmem((3 * ROWS, ATT), F32),
            vmem((3 * ROWS, 2 * ATT), BF16),
            vmem((SIZE, 3 * ATT), BF16),
            vmem((ATT, SIZE), BF16),
            vmem((2 * ROWS, SIZE), BF16),
            vmem((2 * ROWS, SIZE), BF16),
            vmem((ROWS, ATT), BF16),
            vmem((ROWS, ATT), F32),
            vmem((ROWS, ATT), F32),
            vmem((ROWS, ATT), F32),
            vmem((ROWS, 2 * ATT), BF16),
            vmem((ROWS, MODEL), F32),
            dma((9,)),
            dma((2, CHUNKS, 3)),
            dma((2, CHUNKS, SLOTS)),
            dma((2, CHUNKS)),
            dma((3,)),
            dma((SLOTS,)),
            dma((1,)),
            dma((2,)),
            dma((2,)),
            dma((2,)),
            dma((2,)),
            dma((CHUNKS, 2)),
            dma((CHUNKS, 2)),
            dma((2,)),
            dma((2,)),
            dma((2, CHUNKS, 3)),
            dma((2, CHUNKS, SLOTS)),
            dma((2, CHUNKS)),
        ],
        compiler_params=pltpu.CompilerParams(
            collective_id=0, has_side_effects=True, vmem_limit_bytes=48 * 1024 * 1024
        ),
    )(
        *(
            pltpu.with_memory_space_constraint(x, pltpu.HBM)
            for x in (nbr_blocks, norm_gain, q_time, k_time, v_time, resid, w_out_time, w_qkv_site, grad_site)
        ),
    )
    return pl.pallas_call(
        hand_over,
        out_shape=(narrow, narrow, narrow, narrow, wide),
        in_specs=[anywhere] * 5,
        out_specs=(anywhere,) * 5,
        scratch_shapes=[dma((5,))],
        compiler_params=pltpu.CompilerParams(vmem_limit_bytes=1024 * 1024),
    )(*results)


def solution(mesh):
    rows = P("site", "tm", None)
    return jax.shard_map(
        functools.partial(shards, mesh.shape["tm"], mesh.shape["site"]),
        mesh=mesh,
        in_specs=(rows, rows, rows, rows, P(), P(), P(), rows, P("site", None)),
        out_specs=(rows,) * 5,
        check_vma=False,
    )
```
